32 devices in a mesh: dp: 8 (over z, y), seq: 4 (over x, core).
Axes of the slice: x: 2, y: 2, z: 4, core: 2. Of those that a mesh axis runs over, the one named last changes fastest.
Arguments:
- inputs: bfloat16 [2, 4096, 1152], P(None, ('dp', 'seq')), may hold values from -6 to 6
- cotangent: bfloat16 [2, 4096, 1152], P(None, ('dp', 'seq')), may hold values from -6 to 6
- lengths: int32 [2, 4], replicated, may hold values from 1 to 2048, 3840 in all within a row
- deal: int32 [2, 16], replicated, may hold values from 0 to 15, as said below
- w_query: bfloat16 [1152, 1024], P(('dp', 'seq')), may hold values from -0.1875 to 0.1875
- w_key: bfloat16 [1152, 256], P(('dp', 'seq')), may hold values from -0.1875 to 0.1875
- w_value: bfloat16 [1152, 256], P(('dp', 'seq')), may hold values from -0.1875 to 0.1875
- w_out: bfloat16 [1024, 1152], P(('dp', 'seq')), may hold values from -0.375 to 0.375
- w_gate: bfloat16 [1152, 6912], P(('dp', 'seq')), may hold values from -0.1875 to 0.1875
- w_up: bfloat16 [1152, 6912], P(('dp', 'seq')), may hold values from -0.1875 to 0.1875
- w_down: bfloat16 [6912, 1152], P(('dp', 'seq')), may hold values from -0.078125 to 0.078125
- gain_attn_pre: bfloat16 [1152], P(('dp', 'seq')), may hold values from 0.5 to 1.5
- gain_attn_post: bfloat16 [1152], P(('dp', 'seq')), may hold values from 0.5 to 1.5
- gain_ffw_pre: bfloat16 [1152], P(('dp', 'seq')), may hold values from 0.5 to 1.5
- gain_ffw_post: bfloat16 [1152], P(('dp', 'seq')), may hold values from 0.5 to 1.5
- gain_query: bfloat16 [256], P(('dp', 'seq')), may hold values from 0.099609375 to 1.8984375
- gain_key: bfloat16 [256], P(('dp', 'seq')), may hold values from 0.099609375 to 1.8984375
Outputs:
- output: bfloat16 [2, 4096, 1152], P(None, ('dp', 'seq'))
- input_grad: bfloat16 [2, 4096, 1152], P(None, ('dp', 'seq'))
- grad_w_query: float32 [1152, 1024], P(('dp', 'seq'))
- grad_w_key: float32 [1152, 256], P(('dp', 'seq'))
- grad_w_value: float32 [1152, 256], P(('dp', 'seq'))
- grad_w_out: float32 [1024, 1152], P(('dp', 'seq'))
- grad_w_gate: float32 [1152, 6912], P(('dp', 'seq'))
- grad_w_up: float32 [1152, 6912], P(('dp', 'seq'))
- grad_w_down: float32 [6912, 1152], P(('dp', 'seq'))
- grad_gain_attn_pre: float32 [1152], P(('dp', 'seq'))
- grad_gain_attn_post: float32 [1152], P(('dp', 'seq'))
- grad_gain_ffw_pre: float32 [1152], P(('dp', 'seq'))
- grad_gain_ffw_post: float32 [1152], P(('dp', 'seq'))
- grad_gain_query: float32 [256], P(('dp', 'seq'))
- grad_gain_key: float32 [256], P(('dp', 'seq'))
The draws below stay inside these ranges and needn't reach their ends.
Inputs may be any that keep to these rules, and one draw needn't show every extreme that they name: Each row of deal is a permutation of the 16 stretches in which slots 2 g and 2 g + 1 hold stretches i and 15 - i for some i.
All inputs are finite; a program needn't handle non-finite values.
Results may differ from the reference program's by a relative error of at most 0.035.
Values may be sent and summed in bfloat16 or wider, within the bound.
No kernel may reach another device: no remote copies, remote signals or barrier semaphores. Data moves between devices by JAX's collectives and lax.ppermute only.
A program may use at most 320 MiB of HBM per device.

```python
import math
import jax
import jax.numpy as jnp
import numpy as np
from jax import lax

D = 1152
HEADS = 4
HEAD = 256
FF = 6912
MB = 2
STRETCH = 256
TOKENS = 4096
LONGEST = 2048
KW = 9
NCHUNK = 16
SEQS = 4


def draw_deal(key, part):
    pair_count = NCHUNK // 2
    rows_out = []
    for micro_index in range(MB):
        micro_key = jax.random.fold_in(key, 17 + micro_index)
        order = jax.random.permutation(jax.random.fold_in(micro_key, 1), pair_count).astype(jnp.int32)
        flips = jax.random.randint(jax.random.fold_in(micro_key, 2), (pair_count,), 0, 2, dtype=jnp.int32)
        first = jnp.where(flips == 1, NCHUNK - 1 - order, order)
        second = NCHUNK - 1 - first
        rows_out.append(jnp.stack([first, second], axis=1).reshape(NCHUNK))
    return jnp.stack(rows_out, axis=0).astype(jnp.int32)


def steps_of(key, shape, pieces, least, top_value):
    def one(dim, parts):
        steps = jax.random.uniform(jax.random.fold_in(jax.random.fold_in(key, 6), dim), (parts,), jnp.float32, least / len(pieces), top_value / len(pieces))
        return jnp.repeat(jnp.exp(steps), shape[dim] // parts).reshape((-1,) + (1,) * (len(shape) - dim - 1))

    level = one(*pieces[0])
    for cut in pieces[1:]:
        level = level * one(*cut)
    return level


def profile(count, total, reach, lean):
    loads = [(1 << 20) // math.isqrt(rank ** lean) + 1 for rank in range(2, count + 1)]
    spare, holding = total - reach - (count - 1), [1] * (count - 1)
    while spare > 0:
        movable = [i for i in range(count - 1) if holding[i] < reach]
        pool, left = sum([loads[i] for i in movable]), spare
        for i in movable:
            addition = min(reach - holding[i], max(1, left * loads[i] // pool), spare)
            holding[i] = holding[i] + addition
            spare = spare - addition
    return np.array([reach] + holding)


def ragged_sizes(key, number_of, total, most, slope):
    if number_of == 2:
        one = jax.random.randint(key, (), max(1, total - most), min(most, total - 1) + 1)
        return jnp.stack([one, total - one])
    sizes = jnp.asarray(profile(number_of, total, most, slope), jnp.int32)
    pairs = (number_of - 1) // 2
    source_of, taker = sizes[1:1 + 2 * pairs:2], sizes[2:2 + 2 * pairs:2]
    slack = jnp.minimum(source_of - 1, most - taker)
    moved = jax.random.randint(jax.random.fold_in(key, 1), (pairs,), 0, 1 << 20) % (slack + 1)
    sizes = sizes.at[1:1 + 2 * pairs:2].set(source_of - moved).at[2:2 + 2 * pairs:2].set(taker + moved)
    return sizes[jax.random.permutation(jax.random.fold_in(key, 2), number_of)]


def noise(rng, dims, scale, bound, cuts=(), held_as=jnp.bfloat16):
    factor_of = steps_of(rng, dims, cuts, -0.22, 0.18) if cuts else 1.0
    values = jax.random.normal(rng, dims, jnp.float32) * scale * factor_of
    return jnp.minimum(jnp.maximum(values, -bound), bound).astype(held_as)


def setup_inputs(seed: int = 0) -> dict:
    seeds = jax.random.split(jax.random.key(seed), 18)
    inputs = noise(seeds[0], (MB, TOKENS, D), 1.0, 6.0, ((1, 32),))
    cotangent = noise(seeds[1], (MB, TOKENS, D), 1.0, 6.0, ((1, 32),))
    lengths = jax.vmap(lambda own: ragged_sizes(own, SEQS, TOKENS - STRETCH, LONGEST, 2))(jax.random.split(seeds[2], MB)).reshape((MB, SEQS)).astype(jnp.int32)
    deal = draw_deal(jax.random.fold_in(seeds[17], 71), 0)
    w_query = noise(seeds[4], (D, HEADS * HEAD), D ** -0.5, 0.1875, ((0, 32),))
    w_key = noise(seeds[5], (D, HEAD), D ** -0.5, 0.1875, ((0, 32),))
    w_value = noise(seeds[6], (D, HEAD), D ** -0.5, 0.1875, ((0, 32),))
    w_out = noise(seeds[7], (HEADS * HEAD, D), HEAD ** -0.5, 0.375, ((0, 32),))
    w_gate = noise(seeds[8], (D, FF), D ** -0.5, 0.1875, ((0, 32),))
    w_up = noise(seeds[9], (D, FF), D ** -0.5, 0.1875, ((0, 32),))
    w_down = noise(seeds[10], (FF, D), FF ** -0.5, 0.078125, ((0, 32),))
    gain_attn_pre = jnp.clip(1.0 + 0.1 * jax.random.normal(seeds[11], (D,), jnp.float32), 0.5, 1.5).astype(jnp.bfloat16)
    gain_attn_post = jnp.clip(1.0 + 0.1 * jax.random.normal(seeds[12], (D,), jnp.float32), 0.5, 1.5).astype(jnp.bfloat16)
    gain_ffw_pre = jnp.clip(1.0 + 0.1 * jax.random.normal(seeds[13], (D,), jnp.float32), 0.5, 1.5).astype(jnp.bfloat16)
    gain_ffw_post = jnp.clip(1.0 + 0.1 * jax.random.normal(seeds[14], (D,), jnp.float32), 0.5, 1.5).astype(jnp.bfloat16)
    gain_query = jnp.clip(1.0 + 0.18 * jax.random.normal(seeds[15], (HEAD,), jnp.float32), 0.099609375, 1.8984375).astype(jnp.bfloat16)
    gain_key = jnp.clip(1.0 + 0.18 * jax.random.normal(seeds[16], (HEAD,), jnp.float32), 0.099609375, 1.8984375).astype(jnp.bfloat16)
    return dict(inputs=inputs, cotangent=cotangent, lengths=lengths, deal=deal, w_query=w_query, w_key=w_key, w_value=w_value, w_out=w_out, w_gate=w_gate, w_up=w_up, w_down=w_down, gain_attn_pre=gain_attn_pre, gain_attn_post=gain_attn_post, gain_ffw_pre=gain_ffw_pre, gain_ffw_post=gain_ffw_post, gain_query=gain_query, gain_key=gain_key)


@jax.custom_vjp
def low(v):
    return lax.optimization_barrier(v.astype(jnp.bfloat16)).astype(jnp.float32)

@jax.custom_vjp
def low_back(v):
    return v

def low_keep(v):
    return (low(v), None)

def low_pass(kept, grad):
    return (grad,)

def back_keep(v):
    return (v, None)

def back_low(kept, grad):
    return (low(grad),)
low.defvjp(low_keep, low_pass)
low_back.defvjp(back_keep, back_low)
eps = 1e-06
rope_base = 1000000.0
masked_score = -1e+30

def product_hi(left, right):
    return jnp.dot(left, right, precision=lax.Precision.HIGHEST, preferred_element_type=jnp.float32)

def rms_norm(values, gain):
    return values * lax.rsqrt(lax.optimization_barrier(jnp.mean(values * values, axis=-1, keepdims=True)) + eps) * gain

def rotary(values, positions):
    half_width = values.shape[-1] // 2
    freqs = rope_base ** (-2.0 * jnp.arange(half_width, dtype=jnp.float32) / values.shape[-1])
    angle = positions.astype(jnp.float32)[:, None, None] * freqs
    cosine = jnp.cos(angle)
    sine = jnp.sin(angle)
    first = values[..., :half_width]
    second = values[..., half_width:]
    return jnp.concatenate([first * cosine - second * sine, second * cosine + first * sine], axis=-1)

def layout(lengths, row_ids):
    ends = jnp.cumsum(lengths).astype(jnp.int32)
    after = row_ids[:, None] >= ends[None, :]
    segment = lax.optimization_barrier(jnp.sum(after.astype(jnp.int32), axis=1))
    starts = lax.optimization_barrier(jnp.max(jnp.where(after, ends[None, :], 0), axis=1))
    return (segment, row_ids - starts)

def attention(query_rot, key_rot, value_low, lengths):
    span = (KW - 1) * STRETCH
    key_pad = jnp.concatenate([jnp.zeros((span, HEAD), jnp.float32), key_rot], axis=0)
    value_pad = jnp.concatenate([jnp.zeros((span, HEAD), jnp.float32), value_low], axis=0)
    scale = HEAD ** (-0.5)

    def one_stretch(stretch_id):
        first_row = stretch_id * STRETCH
        query_block = lax.dynamic_slice_in_dim(query_rot, first_row, STRETCH, 0)
        key_block = lax.dynamic_slice_in_dim(key_pad, first_row, KW * STRETCH, 0)
        value_block = lax.dynamic_slice_in_dim(value_pad, first_row, KW * STRETCH, 0)
        query_ids = first_row + jnp.arange(STRETCH, dtype=jnp.int32)
        key_ids = first_row - span + jnp.arange(KW * STRETCH, dtype=jnp.int32)
        query_seg, query_pos = layout(lengths, query_ids)
        key_seg, key_pos = layout(lengths, key_ids)
        allowed = (key_ids[None, :] >= 0) & (key_ids[None, :] <= query_ids[:, None]) & (key_seg[None, :] == query_seg[:, None])
        scores = low_back(jnp.einsum('qhd,kd->hqk', query_block, key_block, precision=lax.Precision.HIGHEST) * scale)
        scores = jnp.where(allowed[None], scores, masked_score)
        weights = jax.nn.softmax(scores, axis=-1)
        return jnp.einsum('hqk,kd->qhd', low(weights), value_block, precision=lax.Precision.HIGHEST)
    blocks = lax.map(jax.checkpoint(one_stretch), jnp.arange(NCHUNK, dtype=jnp.int32))
    return blocks.reshape(TOKENS, HEADS, HEAD)

def layer_forward(rows_in, params, lengths):
    query_weight, key_weight, value_weight, out_weight, gate_weight, up_weight, down_weight, pre_attention, post_attention, pre_feed, post_feed, query_gain, key_gain = params
    row_ids = jnp.arange(TOKENS, dtype=jnp.int32)
    segment, positions = layout(lengths, row_ids)
    normed_one = low(rms_norm(rows_in, pre_attention))
    query_raw = low_back(product_hi(normed_one, query_weight)).reshape(TOKENS, HEADS, HEAD)
    key_raw = low_back(product_hi(normed_one, key_weight)).reshape(TOKENS, 1, HEAD)
    value_raw = low_back(product_hi(normed_one, value_weight))
    query_rot = low_back(low(rotary(rms_norm(query_raw, query_gain), positions)))
    key_rot = low(rotary(rms_norm(key_raw, key_gain), positions))[:, 0, :]
    value_low = low(value_raw)
    context = attention(query_rot, key_rot, value_low, lengths)
    context_low = low_back(low(context)).reshape(TOKENS, HEADS * HEAD)
    attended = low_back(product_hi(context_low, out_weight))
    hidden_res = rows_in + rms_norm(attended, post_attention)
    normed_two = low(rms_norm(hidden_res, pre_feed))
    gate_raw = low_back(product_hi(normed_two, gate_weight))
    up_raw = low_back(product_hi(normed_two, up_weight))
    hidden_low = low(jax.nn.gelu(gate_raw, approximate=True) * up_raw)
    mixed = low_back(product_hi(hidden_low, down_weight))
    result = hidden_res + rms_norm(mixed, post_feed)
    valid = row_ids < TOKENS - STRETCH
    return jnp.where(valid[:, None], result, 0.0)

def reference(inputs, cotangent, lengths, deal, w_query, w_key, w_value, w_out, w_gate, w_up, w_down, gain_attn_pre, gain_attn_post, gain_ffw_pre, gain_ffw_post, gain_query, gain_key):
    params = tuple((weight.astype(jnp.float32) for weight in (w_query, w_key, w_value, w_out, w_gate, w_up, w_down, gain_attn_pre, gain_attn_post, gain_ffw_pre, gain_ffw_post, gain_query, gain_key)))
    grad_total = tuple((jnp.zeros(weight.shape, jnp.float32) for weight in params))
    outputs = []
    input_grads = []
    stretch_ids = jnp.arange(NCHUNK, dtype=jnp.int32)
    for micro_index in range(MB):
        dealt_slots = deal[micro_index].astype(jnp.int32)
        match = (dealt_slots[:, None] == stretch_ids[None, :]).astype(jnp.int32)
        inverse = lax.optimization_barrier(jnp.sum(stretch_ids[:, None] * match, axis=0)).astype(jnp.int32)
        seq_lengths = lengths[micro_index]

        def natural(array):
            return array.astype(jnp.float32).reshape(NCHUNK, STRETCH, D)[inverse].reshape(TOKENS, D)

        def dealt(array):
            return array.reshape(NCHUNK, STRETCH, D)[dealt_slots].reshape(TOKENS, D)
        result, pullback = jax.vjp(lambda rows_in, weights: layer_forward(rows_in, weights, seq_lengths), natural(inputs[micro_index]), params)
        row_grad, weight_grads = pullback(natural(cotangent[micro_index]))
        outputs.append(dealt(result).astype(jnp.bfloat16))
        input_grads.append(dealt(row_grad).astype(jnp.bfloat16))
        grad_total = jax.tree.map(jnp.add, grad_total, weight_grads)
    return (jnp.stack(outputs, axis=0), jnp.stack(input_grads, axis=0), grad_total[0], grad_total[1], grad_total[2], grad_total[3], grad_total[4], grad_total[5], grad_total[6], grad_total[7], grad_total[8], grad_total[9], grad_total[10], grad_total[11], grad_total[12])
```

```python
import functools

import jax
import jax.numpy as jnp
from jax import lax
from jax.experimental import pallas as pl
from jax.experimental.pallas import tpu as pltpu
from jax.sharding import PartitionSpec as P

HEADS = 4
HEAD = 256
MB = 2
STRETCH = 256

eps = 1e-06
rope_base = 1000000.0
masked_score = -1e30
bf16 = jnp.bfloat16
f32 = jnp.float32
ALL = ("dp", "seq")


def norm_scale(values):
    return lax.rsqrt(jnp.mean(values * values, axis=-1, keepdims=True) + eps)


def norm_back(values, scale, weighted):
    return scale * weighted - values * (scale * scale * scale) * jnp.mean(
        weighted * values, axis=-1, keepdims=True
    )


def rotate(values, cosine, sine):
    first, second = jnp.split(values, 2, axis=-1)
    return jnp.concatenate([first * cosine - second * sine, second * cosine + first * sine], axis=-1)


def layout_start(ends, row_ids):
    after = row_ids[:, None] >= ends[None, :]
    return jnp.max(jnp.where(after, ends[None, :], 0), axis=1)


def dot(left, right, dims):
    return lax.dot_general(left, right, (dims, ((), ())), preferred_element_type=f32)


def mm(left, right):
    return dot(left, right, ((1,), (0,)))


def mm_tn(left, right):
    return dot(left, right, ((0,), (0,)))


def mm_nt(left, right):
    return dot(left, right, ((1,), (1,)))


def swap(value, axis, bit):
    size = lax.axis_size(axis)
    return lax.ppermute(value, axis, [(i, i ^ bit) for i in range(size)])


def gather_seq(rows):
    far = swap(rows, "seq", 2)
    return jnp.concatenate([rows, swap(rows, "seq", 1), far, swap(far, "seq", 1)], axis=0)


def scatter_seq(parts):
    count = parts.shape[0] // 4
    piece = [parts[i * count : (i + 1) * count] for i in range(4)]
    far = piece[2] + swap(piece[3].astype(bf16), "seq", 1).astype(f32)
    near = piece[0] + swap(piece[1].astype(bf16), "seq", 1).astype(f32)
    return near + swap(far.astype(bf16), "seq", 2).astype(f32)


def gather_dp(shard):
    return lax.all_gather(shard, "dp", axis=0, tiled=True)


def scatter_dp(total):
    return lax.psum_scatter(total.astype(bf16), "dp", scatter_dimension=0, tiled=True)


def query_vectors(meta_ref, ends_ref, micro, rows):
    lanes = lax.broadcasted_iota(jnp.int32, (1, HEADS * rows), 1)
    ids = meta_ref[micro, 0] + lanes % rows
    start = jnp.zeros_like(ids)
    for index in range(ends_ref.shape[1]):
        end = ends_ref[micro, index]
        start = jnp.where(ids >= end, end, start)
    return ids, start


def masked_of(key_stretch, ids, start):
    key = key_stretch * STRETCH + lax.broadcasted_iota(jnp.int32, (STRETCH, 1), 0)
    return (key <= ids) & (key >= start)


def attend_kernel(rows, meta_ref, ends_ref, deal_ref, q_ref, kv_ref, o_ref, lse_ref, top, total, acc):
    micro, slot = pl.program_id(0), pl.program_id(1)

    @pl.when(slot == 0)
    def _():
        top[...] = jnp.full_like(top, masked_score)
        total[...] = jnp.zeros_like(total)
        acc[...] = jnp.zeros_like(acc)

    key_stretch = deal_ref[micro, slot]

    @pl.when((key_stretch <= meta_ref[micro, 1]) & (key_stretch >= meta_ref[micro, 2]))
    def _():
        ids, start = query_vectors(meta_ref, ends_ref, micro, rows)
        block = kv_ref[...].reshape(STRETCH, 2 * HEAD)
        query = q_ref[...].reshape(HEADS * rows, HEAD)
        scores = jnp.where(masked_of(key_stretch, ids, start), mm_nt(block[:, :HEAD], query), masked_score)
        old = top[...]
        new = jnp.maximum(old, jnp.max(scores, axis=0, keepdims=True))
        keep = jnp.exp(old - new)
        terms = jnp.exp(scores - new)
        top[...] = new
        total[...] = total[...] * keep + jnp.sum(terms, axis=0, keepdims=True)
        acc[...] = acc[...] * keep + mm_tn(block[:, HEAD:], terms.astype(bf16))

    @pl.when(slot == pl.num_programs(1) - 1)
    def _():
        out = acc[...] * (1.0 / total[...])
        o_ref[...] = out.T.reshape(o_ref.shape)
        lse_ref[...] = (top[...] + jnp.log(total[...])).reshape(lse_ref.shape)


def attend_back_kernel(
    rows, meta_ref, ends_ref, deal_ref, q_ref, dc_ref, lse_ref, delta_ref, kv_ref, dq_ref, dkv_ref, acc
):
    micro, slot = pl.program_id(0), pl.program_id(1)

    @pl.when(slot == 0)
    def _():
        acc[...] = jnp.zeros_like(acc)

    key_stretch = deal_ref[micro, slot]
    active = (key_stretch <= meta_ref[micro, 1]) & (key_stretch >= meta_ref[micro, 2])

    @pl.when(active)
    def _():
        ids, start = query_vectors(meta_ref, ends_ref, micro, rows)
        block = kv_ref[...].reshape(STRETCH, 2 * HEAD)
        key, value = block[:, :HEAD], block[:, HEAD:]
        query = q_ref[...].reshape(HEADS * rows, HEAD)
        grad = dc_ref[...].reshape(HEADS * rows, HEAD)
        probs = jnp.where(
            masked_of(key_stretch, ids, start),
            jnp.exp(mm_nt(key, query) - lse_ref[...].reshape(1, HEADS * rows)),
            0.0,
        )
        score_grad = probs * (mm_nt(value, grad) - delta_ref[...].reshape(1, HEADS * rows))
        score_grad = score_grad.astype(bf16)
        acc[...] += mm_tn(key, score_grad)
        key_grad = mm(score_grad, query)
        value_grad = mm(probs.astype(bf16), grad)
        both = jnp.concatenate([key_grad, value_grad], axis=1)
        dkv_ref[...] = both.astype(bf16).reshape(dkv_ref.shape)

    @pl.when(jnp.logical_not(active))
    def _():
        dkv_ref[...] = jnp.zeros_like(dkv_ref)

    @pl.when(slot == pl.num_programs(1) - 1)
    def _():
        dq_ref[...] = (acc[...].T * HEAD**-0.5).reshape(dq_ref.shape)


def attend(meta, ends, deal, query, keys):
    rows, slots = query.shape[2], deal.shape[1]
    wide = HEADS * rows
    per_micro = pl.BlockSpec((1, HEADS, rows, HEAD), lambda b, j, *_: (b, 0, 0, 0))
    line = pl.BlockSpec((1, 1, wide), lambda b, j, *_: (b, 0, 0))
    key_spec = pl.BlockSpec((STRETCH // rows, None, rows, 2 * HEAD), lambda b, j, *_: (j, b, 0, 0))
    return pl.pallas_call(
        functools.partial(attend_kernel, rows),
        grid_spec=pltpu.PrefetchScalarGridSpec(
            num_scalar_prefetch=3,
            grid=(MB, slots),
            in_specs=[per_micro, key_spec],
            out_specs=[per_micro, line],
            scratch_shapes=[
                pltpu.VMEM((1, wide), f32),
                pltpu.VMEM((1, wide), f32),
                pltpu.VMEM((HEAD, wide), f32),
            ],
        ),
        out_shape=[
            jax.ShapeDtypeStruct(query.shape, f32),
            jax.ShapeDtypeStruct((MB, 1, wide), f32),
        ],
        name="attend",
        cost_estimate=pl.CostEstimate(
            flops=4 * MB * 9 * STRETCH * wide * HEAD, bytes_accessed=2 * keys.size, transcendentals=MB * 9 * STRETCH * wide
        ),
    )(meta, ends, deal, query, keys)


def attend_back(meta, ends, deal, query, grad, lse, delta, keys):
    rows, slots = query.shape[2], deal.shape[1]
    wide = HEADS * rows
    per_micro = pl.BlockSpec((1, HEADS, rows, HEAD), lambda b, j, *_: (b, 0, 0, 0))
    line = pl.BlockSpec((1, 1, wide), lambda b, j, *_: (b, 0, 0))
    key_spec = pl.BlockSpec((STRETCH // rows, None, rows, 2 * HEAD), lambda b, j, *_: (j, b, 0, 0))
    return pl.pallas_call(
        functools.partial(attend_back_kernel, rows),
        grid_spec=pltpu.PrefetchScalarGridSpec(
            num_scalar_prefetch=3,
            grid=(MB, slots),
            in_specs=[per_micro, per_micro, line, line, key_spec],
            out_specs=[per_micro, key_spec],
            scratch_shapes=[pltpu.VMEM((HEAD, wide), f32)],
        ),
        out_shape=[
            jax.ShapeDtypeStruct(query.shape, f32),
            jax.ShapeDtypeStruct(keys.shape, bf16),
        ],
        name="attend_back",
        cost_estimate=pl.CostEstimate(
            flops=10 * MB * 9 * STRETCH * wide * HEAD, bytes_accessed=4 * keys.size, transcendentals=MB * 9 * STRETCH * wide
        ),
    )(meta, ends, deal, query, grad, lse, delta, keys)


def per_device(
    inputs,
    cotangent,
    lengths,
    deal,
    w_query,
    w_key,
    w_value,
    w_out,
    w_gate,
    w_up,
    w_down,
    gain_attn_pre,
    gain_attn_post,
    gain_ffw_pre,
    gain_ffw_post,
    gain_query,
    gain_key,
):
    rows, width = inputs.shape[1], inputs.shape[2]
    groups, members = lax.axis_size("dp"), lax.axis_size("seq")
    devices = groups * members
    total_rows = rows * devices
    dp_id, seq_id = lax.axis_index("dp"), lax.axis_index("seq")
    device_id = dp_id * members + seq_id
    count = MB * rows
    model_rows = w_query.shape[0]
    ff_rows = w_down.shape[0]
    ff_local = groups * ff_rows
    wide_q = HEADS * HEAD
    wide_qkv = wide_q + 2 * HEAD
    gain_rows, head_rows = gain_attn_pre.shape[0], gain_query.shape[0]
    gain_sizes = [gain_rows] * 4 + [head_rows] * 2
    gain_total = sum(gain_sizes)

    gains = jnp.concatenate([gain_attn_pre, gain_attn_post, gain_ffw_pre, gain_ffw_post, gain_query, gain_key])
    gain_line = jnp.pad(gains[None, :], ((0, 0), (0, wide_qkv - gain_total)))
    attn_shard = jnp.concatenate([jnp.concatenate([w_query, w_key, w_value], axis=1), gain_line], axis=0)
    attn_all = lax.all_gather(attn_shard, ALL, axis=0, tiled=False)
    w_qkv = attn_all[:, :model_rows].reshape(devices * model_rows, wide_qkv)
    gain_all = attn_all[:, model_rows, :gain_total].astype(f32)
    full_gain, at = [], 0
    for size in gain_sizes:
        full_gain.append(gain_all[:, at : at + size].reshape(devices * size))
        at += size
    pre_attention, post_attention, pre_feed, post_feed, query_gain, key_gain = full_gain
    out_weight = lax.all_gather(w_out, ALL, axis=0, tiled=True)

    def columns_to_members(weight):
        split = weight.reshape(model_rows, groups, members, ff_rows)
        split = split.transpose(2, 0, 1, 3).reshape(members, model_rows, ff_local)
        moved = lax.all_to_all(split, "seq", split_axis=0, concat_axis=0, tiled=True)
        return gather_dp(moved.reshape(members * model_rows, ff_local))

    gate_weight = columns_to_members(w_gate)
    up_weight = columns_to_members(w_up)
    down_weight = gather_dp(w_down)

    ends = jnp.cumsum(lengths, axis=1)
    local_ids = jnp.arange(rows, dtype=jnp.int32)
    stretches = lax.dynamic_index_in_dim(deal, device_id * rows // STRETCH, 1, keepdims=False)
    first_rows = stretches * STRETCH + device_id * rows % STRETCH
    my_rows = first_rows[:, None] + local_ids[None, :]
    starts = jnp.stack([layout_start(ends[b], my_rows[b]) for b in range(MB)])
    meta = jnp.stack([first_rows, stretches, starts[:, 0] // STRETCH], axis=1)
    positions = (my_rows - starts).reshape(count)
    valid = (my_rows < total_rows - STRETCH).reshape(count, 1)
    freqs = rope_base ** (-2.0 * jnp.arange(HEAD // 2, dtype=f32) / HEAD)
    angle = positions.astype(f32)[:, None, None] * freqs
    cosine, sine = jnp.cos(angle), jnp.sin(angle)

    rows_in = inputs.reshape(count, width).astype(f32)
    scale_one = norm_scale(rows_in)
    normed_one = (rows_in * scale_one * pre_attention).astype(bf16)
    qkv = mm(normed_one, w_qkv)
    query_raw = qkv[:, :wide_q].reshape(count, HEADS, HEAD)
    key_raw = qkv[:, wide_q : wide_q + HEAD].reshape(count, 1, HEAD)
    value_low = qkv[:, wide_q + HEAD :].astype(bf16)
    query_scale = norm_scale(query_raw)
    query_rot = rotate(query_raw * query_scale * query_gain, cosine, sine).astype(bf16) * HEAD**-0.5
    key_scale = norm_scale(key_raw)
    key_rot = rotate(key_raw * key_scale * key_gain, cosine, sine).astype(bf16)

    def to_heads(values):
        return values.reshape(MB, rows, HEADS, HEAD).transpose(0, 2, 1, 3)

    def from_heads(values):
        return values.transpose(0, 2, 1, 3).reshape(count, HEADS, HEAD)

    query_heads = to_heads(query_rot.astype(bf16))
    keys_mine = jnp.concatenate([key_rot[:, 0], value_low], axis=1).reshape(MB, rows, 2 * HEAD)
    keys_all = lax.all_gather(keys_mine, ALL, axis=0, tiled=False)
    context, lse = attend(meta, ends, deal, query_heads, keys_all)
    context_rows = from_heads(context.astype(bf16)).reshape(count, wide_q)
    attended = mm(context_rows, out_weight)
    scale_two = norm_scale(attended)
    hidden_res = rows_in + attended * scale_two * post_attention
    scale_three = norm_scale(hidden_res)
    normed_two = (hidden_res * scale_three * pre_feed).astype(bf16)

    normed_group = gather_seq(normed_two)
    gate_raw = mm(normed_group, gate_weight)
    up_raw = mm(normed_group, up_weight)
    hidden_low = (jax.nn.gelu(gate_raw, approximate=True) * up_raw).astype(bf16)
    mixed = scatter_seq(mm(hidden_low, down_weight))
    scale_four = norm_scale(mixed)
    result = hidden_res + mixed * scale_four * post_feed
    output = jnp.where(valid, result, 0.0).astype(bf16)

    upstream = jnp.where(valid, cotangent.reshape(count, width).astype(f32), 0.0)
    grad_post_feed = jnp.sum(upstream * mixed * scale_four, axis=0)
    mixed_grad = norm_back(mixed, scale_four, post_feed * upstream).astype(bf16)
    mixed_group = gather_seq(mixed_grad)
    hidden_grad = mm_nt(mixed_group, down_weight)
    _, gelu_pull = jax.vjp(lambda g, u: jax.nn.gelu(g, approximate=True) * u, gate_raw, up_raw)
    gate_grad, up_grad = gelu_pull(hidden_grad)
    gate_grad, up_grad = gate_grad.astype(bf16), up_grad.astype(bf16)
    normed_two_grad = scatter_seq(mm_nt(gate_grad, gate_weight) + mm_nt(up_grad, up_weight))
    grad_down = scatter_dp(mm_tn(hidden_low, mixed_group)).astype(f32)

    def columns_home(total):
        mine = scatter_dp(total).reshape(members, model_rows, ff_local)
        moved = lax.all_to_all(mine, "seq", split_axis=0, concat_axis=0, tiled=True)
        split = moved.reshape(members, model_rows, groups, ff_rows).transpose(1, 2, 0, 3)
        return split.reshape(model_rows, devices * ff_rows).astype(f32)

    grad_gate = columns_home(mm_tn(normed_group, gate_grad))
    grad_up = columns_home(mm_tn(normed_group, up_grad))
    grad_pre_feed = jnp.sum(normed_two_grad * hidden_res * scale_three, axis=0)
    hidden_res_grad = upstream + norm_back(hidden_res, scale_three, pre_feed * normed_two_grad)

    grad_post_attention = jnp.sum(hidden_res_grad * attended * scale_two, axis=0)
    attended_grad = norm_back(attended, scale_two, post_attention * hidden_res_grad).astype(bf16)
    grad_out = lax.psum_scatter(
        mm_tn(context_rows, attended_grad).astype(bf16), ALL, scatter_dimension=0, tiled=True
    ).astype(f32)
    context_grad = to_heads(mm_nt(attended_grad, out_weight).astype(bf16))
    delta = jnp.sum(context_grad.astype(f32) * context, axis=-1).reshape(MB, 1, HEADS * rows)
    query_grads, key_parts = attend_back(
        meta, ends, deal, query_heads, context_grad, lse, delta, keys_all
    )
    key_grads = lax.psum_scatter(key_parts, ALL, scatter_dimension=0, tiled=False)
    key_grads = key_grads.reshape(count, 2 * HEAD)
    value_grad = key_grads[:, HEAD:].astype(bf16)
    key_turned = rotate(key_grads[:, None, :HEAD].astype(f32), cosine, -sine)
    grad_key_gain = jnp.sum(key_turned * key_raw * key_scale, axis=(0, 1))
    key_grad = norm_back(key_raw, key_scale, key_gain * key_turned)[:, 0, :].astype(bf16)
    query_turned = rotate(from_heads(query_grads), cosine, -sine)
    grad_query_gain = jnp.sum(query_turned * query_raw * query_scale, axis=(0, 1))
    query_grad = norm_back(query_raw, query_scale, query_gain * query_turned)
    query_grad = query_grad.reshape(count, wide_q).astype(bf16)
    qkv_grad = jnp.concatenate([query_grad, key_grad, value_grad], axis=1)
    normed_one_grad = mm_nt(qkv_grad, w_qkv)
    grad_pre_attention = jnp.sum(normed_one_grad * rows_in * scale_one, axis=0)
    rows_grad = hidden_res_grad + norm_back(rows_in, scale_one, pre_attention * normed_one_grad)
    input_grad = rows_grad.astype(bf16)
    grad_qkv = mm_tn(normed_one, qkv_grad).reshape(devices, model_rows, wide_qkv)
    gain_grads = [
        grad_pre_attention,
        grad_post_attention,
        grad_pre_feed,
        grad_post_feed,
        grad_query_gain,
        grad_key_gain,
    ]
    gain_grads = jnp.concatenate([g.reshape(devices, -1) for g in gain_grads], axis=1)
    gain_grads = jnp.pad(gain_grads, ((0, 0), (0, wide_qkv - gain_total)))[:, None, :]
    last = jnp.concatenate([grad_qkv, gain_grads], axis=1).astype(bf16)
    last = lax.psum_scatter(last, ALL, scatter_dimension=0, tiled=False).astype(f32)
    gain_out, at = [], 0
    for size in gain_sizes:
        gain_out.append(last[model_rows, at : at + size])
        at += size
    return (
        output.reshape(inputs.shape),
        input_grad.reshape(inputs.shape),
        last[:model_rows, :wide_q],
        last[:model_rows, wide_q : wide_q + HEAD],
        last[:model_rows, wide_q + HEAD :],
        grad_out,
        grad_gate,
        grad_up,
        grad_down,
        *gain_out,
    )


def solution(mesh):
    split = P(None, ALL, None)
    weight, gain = P(ALL, None), P(ALL)
    return jax.shard_map(
        per_device,
        mesh=mesh,
        in_specs=(split, split, P(), P(), *[weight] * 7, *[gain] * 6),
        out_specs=(split, split, *[weight] * 7, *[gain] * 6),
        check_vma=False,
    )
```

```python
import functools
import math

import jax
import jax.numpy as jnp
from jax import lax
from jax.experimental import pallas as pl
from jax.experimental.pallas import tpu as pltpu
from jax.sharding import PartitionSpec as P

HEADS = 4
HEAD = 256
MB = 2
STRETCH = 256

eps = 1e-06
rope_base = 1000000.0
masked_score = -1e30
bf16 = jnp.bfloat16
f32 = jnp.float32
ALL = ("dp", "seq")


def norm_scale(values):
    return lax.rsqrt(jnp.mean(values * values, axis=-1, keepdims=True) + eps)


def norm_back(values, scale, weighted):
    return scale * weighted - values * (scale * scale * scale) * jnp.mean(
        weighted * values, axis=-1, keepdims=True
    )


def rotate(values, cosine, sine):
    first, second = jnp.split(values, 2, axis=-1)
    return jnp.concatenate([first * cosine - second * sine, second * cosine + first * sine], axis=-1)


def layout_start(ends, row_ids):
    after = row_ids[:, None] >= ends[None, :]
    return jnp.max(jnp.where(after, ends[None, :], 0), axis=1)


def dot(left, right, dims):
    return lax.dot_general(left, right, (dims, ((), ())), preferred_element_type=f32)


def mm(left, right):
    return dot(left, right, ((1,), (0,)))


def mm_tn(left, right):
    return dot(left, right, ((0,), (0,)))


def mm_nt(left, right):
    return dot(left, right, ((1,), (1,)))


def xor(value, axis, mask):
    return lax.ppermute(value, axis, [(i, i ^ mask) for i in range(lax.axis_size(axis))])


def xor_both(value, dp_mask, seq_mask):
    members = lax.axis_size("seq")
    mask = dp_mask * members + seq_mask
    return lax.ppermute(value, ALL, [(i, i ^ mask) for i in range(lax.axis_size("dp") * members)])


def flips(value, bits):
    for axis, bit in enumerate(bits):
        halves = [lax.slice_in_dim(value, i, i + 1, axis=axis) for i in (1, 0)]
        value = jnp.where(bit == 1, lax.concatenate(halves, axis), value)
    return value


def add16(left, right):
    return (left.astype(f32) + right.astype(f32)).astype(bf16)


def gather_all(piece):
    count = lax.axis_size("dp") // 2
    first = jnp.stack([piece] + [xor(piece, "dp", 2 * k) for k in range(1, count)])
    side = xor(first, "dp", 1)
    across = xor(first, "seq", 2)
    half = count // 2
    both = jnp.concatenate([xor(side[:half], "seq", 2), xor(across[half:], "dp", 1)])
    near = [first, side, across, both]
    return jnp.concatenate(near + [xor(part, "seq", 1) for part in near]).reshape(-1, piece.shape[1])


def all_labels():
    count = lax.axis_size("dp") // 2
    pairs = [(2 * z + y, 2 * x) for x, y in ((0, 0), (0, 1), (1, 0), (1, 1)) for z in range(count)]
    return pairs + [(d, s + 1) for d, s in pairs]


def scatter_all(total, block):
    count = lax.axis_size("dp") // 2
    parts = total.reshape(-1, block, total.shape[1])
    near, far = parts[: 4 * count], parts[4 * count :]
    near = add16(near, xor(far, "seq", 1))
    first, side, across, both = [near[i * count : (i + 1) * count] for i in range(4)]
    half = count // 2
    low, high = xor(both[:half], "seq", 2), xor(both[half:], "dp", 1)
    side = jnp.concatenate([add16(side[:half], low), side[half:]])
    across = jnp.concatenate([across[:half], add16(across[half:], high)])
    first = first.astype(f32) + xor(side, "dp", 1).astype(f32) + xor(across, "seq", 2).astype(f32)
    result = first[0]
    low_first = first.astype(bf16)
    for k in range(1, count):
        result = result + xor(low_first[k], "dp", 2 * k).astype(f32)
    return result


def gather_group(rows):
    half = rows.shape[0] // 2
    across, along = xor(rows, "seq", 2), xor(rows, "dp", 2)
    corner = [xor(across[:half], "dp", 2), xor(along[half:], "seq", 2)]
    near = [rows, across, along, *corner]
    return jnp.concatenate(near + [xor(part, "seq", 1) for part in near], axis=0)


def scatter_group(total):
    parts = total.reshape(2, -1, total.shape[1])
    near = add16(parts[0], xor(parts[1], "seq", 1))
    mine, across, along, corner = jnp.split(near, 4)
    half = mine.shape[0] // 2
    low, high = xor(corner[:half], "dp", 2), xor(corner[half:], "seq", 2)
    across = jnp.concatenate([add16(across[:half], low), across[half:]])
    along = jnp.concatenate([along[:half], add16(along[half:], high)])
    return mine.astype(f32) + xor(across, "seq", 2).astype(f32) + xor(along, "dp", 2).astype(f32)


def place_kernel(sizes, target_ref, *refs):
    pieces, out = refs[: len(sizes)], refs[len(sizes)]
    buffer, arrived, left = refs[len(sizes) + 1 :]
    ins, outs, block = [], [], 0
    for piece, size in zip(pieces, sizes):
        for index in range(size):
            ins.append(pltpu.make_async_copy(piece.at[index], buffer.at[block], arrived.at[block]))
            outs.append(pltpu.make_async_copy(buffer.at[block], out.at[target_ref[block]], left.at[block]))
            ins[-1].start()
            block += 1
    for copy_in, copy_out in zip(ins, outs):
        copy_in.wait()
        copy_out.start()
    for copy_out in outs:
        copy_out.wait()


def place(pieces, targets):
    sizes = [piece.shape[0] for piece in pieces]
    shape = (sum(sizes), *pieces[0].shape[1:])
    anywhere = pl.BlockSpec(memory_space=pl.ANY)
    return pl.pallas_call(
        functools.partial(place_kernel, sizes),
        grid_spec=pltpu.PrefetchScalarGridSpec(
            num_scalar_prefetch=1,
            grid=(1,),
            in_specs=[anywhere] * len(pieces),
            out_specs=anywhere,
            scratch_shapes=[
                pltpu.VMEM(shape, pieces[0].dtype),
                pltpu.SemaphoreType.DMA((shape[0],)),
                pltpu.SemaphoreType.DMA((shape[0],)),
            ],
        ),
        out_shape=jax.ShapeDtypeStruct(shape, pieces[0].dtype),
        name="place",
        cost_estimate=pl.CostEstimate(flops=0, bytes_accessed=4 * math.prod(shape), transcendentals=0),
    )(targets, *pieces)


def query_vectors(meta_ref, ends_ref, unit, rows):
    lanes = lax.broadcasted_iota(jnp.int32, (1, HEADS * rows), 1)
    ids = meta_ref[3 * unit] + lanes % rows
    start = jnp.zeros_like(ids)
    for index in range(ends_ref.shape[0]):
        end = ends_ref[index]
        start = jnp.where(ids >= end, end, start)
    return ids, start


def mask_of(meta_ref, ends_ref, unit, rows, key_stretch):
    ids, start = query_vectors(meta_ref, ends_ref, unit, rows)
    place_in = lax.broadcasted_iota(jnp.int32, (STRETCH, 1), 0)
    near = meta_ref[6] * rows
    place_in = jnp.where(place_in < rows, place_in + near, place_in - near)
    key = key_stretch * STRETCH + place_in
    return (key <= ids) & (key >= start)


def attend_kernel(
    rows, meta_ref, ends_ref, slots_ref, q_ref, near_ref, far_ref, o_ref, lse_ref, top, total, acc
):
    step = pl.program_id(0)

    @pl.when(step == 0)
    def _():
        top[...] = jnp.full_like(top, masked_score)
        total[...] = jnp.zeros_like(total)
        acc[...] = jnp.zeros_like(acc)

    key_stretch = slots_ref[step]
    for unit in range(2):

        @pl.when((key_stretch <= meta_ref[3 * unit + 1]) & (key_stretch >= meta_ref[3 * unit + 2]))
        def _():
            mask = mask_of(meta_ref, ends_ref, unit, rows, key_stretch)
            block = jnp.concatenate([near_ref[...], far_ref[...]], axis=0)
            query = q_ref[unit].reshape(HEADS * rows, HEAD)
            scores = jnp.where(mask, mm_nt(block[:, :HEAD], query), masked_score)
            old = top[unit]
            new = jnp.maximum(old, jnp.max(scores, axis=0, keepdims=True))
            keep = jnp.exp(old - new)
            terms = jnp.exp(scores - new)
            top[unit] = new
            total[unit] = total[unit] * keep + jnp.sum(terms, axis=0, keepdims=True)
            acc[unit] = acc[unit] * keep + mm_tn(block[:, HEAD:], terms.astype(bf16))

    @pl.when(step == pl.num_programs(0) - 1)
    def _():
        for unit in range(2):
            out = acc[unit] * (1.0 / total[unit])
            o_ref[unit] = out.T.reshape(HEADS, rows, HEAD)
            lse_ref[unit] = top[unit] + jnp.log(total[unit])


def attend_back_kernel(
    rows,
    meta_ref,
    ends_ref,
    slots_ref,
    q_ref,
    dc_ref,
    lse_ref,
    delta_ref,
    near_ref,
    far_ref,
    dq_ref,
    dnear_ref,
    dfar_ref,
    acc,
    both,
):
    step = pl.program_id(0)

    @pl.when(step == 0)
    def _():
        acc[...] = jnp.zeros_like(acc)

    key_stretch = slots_ref[step]
    both[...] = jnp.zeros_like(both)
    for unit in range(2):

        @pl.when((key_stretch <= meta_ref[3 * unit + 1]) & (key_stretch >= meta_ref[3 * unit + 2]))
        def _():
            mask = mask_of(meta_ref, ends_ref, unit, rows, key_stretch)
            block = jnp.concatenate([near_ref[...], far_ref[...]], axis=0)
            key, value = block[:, :HEAD], block[:, HEAD:]
            query = q_ref[unit].reshape(HEADS * rows, HEAD)
            grad = dc_ref[unit].reshape(HEADS * rows, HEAD)
            probs = jnp.where(mask, jnp.exp(mm_nt(key, query) - lse_ref[unit]), 0.0)
            score_grad = (probs * (mm_nt(value, grad) - delta_ref[unit])).astype(bf16)
            acc[unit] += mm_tn(key, score_grad)
            both[:, :HEAD] += mm(score_grad, query)
            both[:, HEAD:] += mm(probs.astype(bf16), grad)

    dnear_ref[...] = both[:rows].astype(bf16)
    dfar_ref[...] = both[rows:].astype(bf16)

    @pl.when(step == pl.num_programs(0) - 1)
    def _():
        for unit in range(2):
            dq_ref[unit] = (acc[unit].T * HEAD**-0.5).reshape(HEADS, rows, HEAD)


def attend_specs(query):
    rows = query.shape[2]
    whole = pl.BlockSpec(query.shape, lambda j, *_: (0, 0, 0, 0))
    line = pl.BlockSpec((2, 1, HEADS * rows), lambda j, *_: (0, 0, 0))
    keys = pl.BlockSpec((None, None, rows, 2 * HEAD), lambda j, *_: (j // 2, j % 2, 0, 0))
    return whole, line, keys


def attend(meta, ends, slots, query, near, far):
    rows = query.shape[2]
    wide = HEADS * rows
    whole, line, keys = attend_specs(query)
    return pl.pallas_call(
        functools.partial(attend_kernel, rows),
        grid_spec=pltpu.PrefetchScalarGridSpec(
            num_scalar_prefetch=3,
            grid=(slots.shape[0],),
            in_specs=[whole, keys, keys],
            out_specs=[whole, line],
            scratch_shapes=[
                pltpu.VMEM((2, 1, wide), f32),
                pltpu.VMEM((2, 1, wide), f32),
                pltpu.VMEM((2, HEAD, wide), f32),
            ],
        ),
        out_shape=[
            jax.ShapeDtypeStruct(query.shape, f32),
            jax.ShapeDtypeStruct((2, 1, wide), f32),
        ],
        name="attend",
        cost_estimate=pl.CostEstimate(
            flops=4 * 2 * 9 * STRETCH * wide * HEAD,
            bytes_accessed=4 * near.size,
            transcendentals=2 * 9 * STRETCH * wide,
        ),
    )(meta, ends, slots, query, near, far)


def attend_back(meta, ends, slots, query, grad, lse, delta, near, far):
    rows = query.shape[2]
    wide = HEADS * rows
    whole, line, keys = attend_specs(query)
    return pl.pallas_call(
        functools.partial(attend_back_kernel, rows),
        grid_spec=pltpu.PrefetchScalarGridSpec(
            num_scalar_prefetch=3,
            grid=(slots.shape[0],),
            in_specs=[whole, whole, line, line, keys, keys],
            out_specs=[whole, keys, keys],
            scratch_shapes=[
                pltpu.VMEM((2, HEAD, wide), f32),
                pltpu.VMEM((STRETCH, 2 * HEAD), f32),
            ],
        ),
        out_shape=[
            jax.ShapeDtypeStruct(query.shape, f32),
            jax.ShapeDtypeStruct(near.shape, bf16),
            jax.ShapeDtypeStruct(near.shape, bf16),
        ],
        name="attend_back",
        cost_estimate=pl.CostEstimate(
            flops=10 * 2 * 9 * STRETCH * wide * HEAD,
            bytes_accessed=8 * near.size,
            transcendentals=2 * 9 * STRETCH * wide,
        ),
    )(meta, ends, slots, query, grad, lse, delta, near, far)


def per_device(
    inputs,
    cotangent,
    lengths,
    deal,
    w_query,
    w_key,
    w_value,
    w_out,
    w_gate,
    w_up,
    w_down,
    gain_attn_pre,
    gain_attn_post,
    gain_ffw_pre,
    gain_ffw_post,
    gain_query,
    gain_key,
):
    rows, width = inputs.shape[1], inputs.shape[2]
    groups, members = lax.axis_size("dp"), lax.axis_size("seq")
    devices = groups * members
    total_rows = rows * devices
    dp_id, seq_id = lax.axis_index("dp"), lax.axis_index("seq")
    half_bit, x_bit, y_bit, z_bit = seq_id % 2, seq_id // 2, dp_id % 2, dp_id // 2 % 2
    tops = groups // 4
    count = 2 * rows
    model_rows, out_rows, ff_rows = w_query.shape[0], w_out.shape[0], w_down.shape[0]
    ff_local = 2 * tops * ff_rows
    wide_q = HEADS * HEAD
    gain_sizes = [gain_attn_pre.shape[0]] * 4 + [gain_query.shape[0]] * 2
    gain_total = sum(gain_sizes)
    block_rows = (model_rows + 8) // 8 * 8

    def regroup(array):
        kept = lax.dynamic_index_in_dim(array, y_bit, 0, keepdims=False)
        sent = lax.dynamic_index_in_dim(array, 1 - y_bit, 0, keepdims=False)
        return jnp.concatenate([kept, xor(sent, "dp", 1)], axis=0)

    def ungroup(array):
        kept, sent = array[:rows], array[rows:]
        return flips(jnp.stack([kept, xor(sent, "dp", 1)]), [y_bit])

    rows_in = regroup(inputs).astype(f32)

    gains = jnp.concatenate([gain_attn_pre, gain_attn_post, gain_ffw_pre, gain_ffw_post, gain_query, gain_key])
    gain_line = jnp.pad(gains[None, :], ((0, 0), (0, 2 * HEAD - gain_total)))
    kv_shard = jnp.concatenate([jnp.concatenate([w_key, w_value], axis=1), gain_line], axis=0)
    kv_weight = gather_all(jnp.pad(kv_shard, ((0, block_rows - model_rows - 1), (0, 0))))
    q_weight = gather_all(jnp.pad(w_query, ((0, block_rows - model_rows), (0, 0))))
    out_weight = gather_all(w_out)
    labels = all_labels()
    natural = jnp.stack([(dp_id ^ d) * members + (seq_id ^ s) for d, s in labels])

    def selection(size, block, padded):
        within = jnp.arange(padded, dtype=jnp.int32)
        source = jnp.where(within < block, natural[:, None] * block + within, -1).reshape(-1)
        return (jnp.arange(size, dtype=jnp.int32)[:, None] == source[None, :]).astype(bf16)

    model_pick = selection(width, model_rows, block_rows)
    head_pick = selection(wide_q, out_rows, out_rows)
    device_pick = selection(devices, 1, 1)
    gain_blocks = kv_weight.reshape(devices, block_rows, 2 * HEAD)[:, model_rows, :gain_total]
    gain_all = mm(device_pick, gain_blocks)
    full_gain, at = [], 0
    for size in gain_sizes:
        full_gain.append(gain_all[:, at : at + size].reshape(devices * size))
        at += size
    pre_attention, post_attention, pre_feed, post_feed, query_gain, key_gain = full_gain

    def by_owner(weight):
        split = weight.reshape(model_rows, tops, 2, 2, members, ff_rows)
        return split.transpose(2, 4, 0, 1, 3, 5).reshape(2, 2, 2, model_rows, ff_local)

    group_bits = [z_bit, x_bit, half_bit]

    def exchange(pieces):
        near = flips(pieces, group_bits)
        got = [near[0, 0, 0]]
        for index in range(1, 8):
            i, j, k = index // 4, index // 2 % 2, index % 2
            got.append(xor_both(near[i, j, k], 2 * i, 2 * j + k))
        return flips(jnp.stack(got).reshape(pieces.shape), group_bits)

    def spread(piece):
        tall = [piece] + [xor(piece, "dp", 4 * k) for k in range(1, tops)]
        return tall + [xor(part, "dp", 1) for part in tall]

    halves = jnp.stack([by_owner(w_gate), by_owner(w_up)], axis=3)
    halves = exchange(halves).transpose(3, 0, 1, 2, 4, 5)
    halves = halves.reshape(2, 2, members * model_rows, ff_local)
    top_id = dp_id // 4
    sources = [((top_id ^ k) * 2 + v) * 2 + (y_bit ^ u) for u in range(2) for k in range(tops) for v in range(2)]
    sources = jnp.stack(sources).astype(jnp.int32)
    gate_weight, up_weight = [place(spread(halves[i]), sources).reshape(width, ff_local) for i in range(2)]
    owners = jnp.stack([(top_id ^ k) * 2 + (y_bit ^ u) for u in range(2) for k in range(tops)]).astype(jnp.int32)
    down_weight = place(spread(w_down[None]), owners).reshape(ff_local, width)

    seq_ends = jnp.cumsum(lax.dynamic_index_in_dim(lengths, y_bit, 0, keepdims=False))
    dealt = lax.dynamic_index_in_dim(deal, y_bit, 0, keepdims=False)
    unit_ids = jnp.stack([(dp_id ^ u) * members + seq_id for u in range(2)])
    stretches = dealt[unit_ids * rows // STRETCH]
    first_rows = stretches * STRETCH + unit_ids * rows % STRETCH
    my_rows = (first_rows[:, None] + jnp.arange(rows, dtype=jnp.int32)).reshape(count)
    starts = layout_start(seq_ends, my_rows)
    lows = starts.reshape(2, rows)[:, 0] // STRETCH
    meta = jnp.concatenate([jnp.stack([first_rows, stretches, lows], axis=1).reshape(-1), half_bit[None]])
    layers = groups // 2
    slot_ids = jnp.stack(
        [
            ((dp_id // 2 ^ z) * 2 + (y_bit ^ u)) * (members // 2) + (x_bit ^ x)
            for x in range(2)
            for z in range(layers)
            for u in range(2)
        ]
    )
    slots = dealt[slot_ids]
    positions = my_rows - starts
    valid = (my_rows < total_rows - STRETCH)[:, None]
    freqs = rope_base ** (-2.0 * jnp.arange(HEAD // 2, dtype=f32) / HEAD)
    angle = positions.astype(f32)[:, None, None] * freqs
    cosine, sine = jnp.cos(angle), jnp.sin(angle)

    scale_one = norm_scale(rows_in)
    normed_one = (rows_in * scale_one * pre_attention).astype(bf16)
    picked_one = mm(normed_one, model_pick).astype(bf16)
    kv_raw = mm(picked_one, kv_weight)
    key_raw = kv_raw[:, :HEAD].reshape(count, 1, HEAD)
    key_scale = norm_scale(key_raw)
    key_rot = rotate(key_raw * key_scale * key_gain, cosine, sine).astype(bf16)
    keys_mine = jnp.concatenate([key_rot[:, 0], kv_raw[:, HEAD:].astype(bf16)], axis=1)
    keys_mine = keys_mine.reshape(2, rows, 2 * HEAD)
    column = [keys_mine] + [xor(keys_mine, "dp", 2 * k) for k in range(1, layers)]
    across = [xor(part, "seq", 2) for part in column]
    column, across = jnp.stack(column), jnp.stack(across)
    near_keys = jnp.concatenate([column, across])
    far_keys = jnp.concatenate([xor(column, "seq", 1), xor(across, "seq", 1)])

    query_raw = mm(picked_one, q_weight).reshape(count, HEADS, HEAD)
    query_scale = norm_scale(query_raw)
    query_rot = rotate(query_raw * query_scale * query_gain, cosine, sine).astype(bf16) * HEAD**-0.5

    def to_heads(values):
        return values.reshape(2, rows, HEADS, HEAD).transpose(0, 2, 1, 3)

    def from_heads(values):
        return values.transpose(0, 2, 1, 3).reshape(count, HEADS, HEAD)

    query_heads = to_heads(query_rot.astype(bf16))
    context, lse = attend(meta, seq_ends, slots, query_heads, near_keys, far_keys)
    context_rows = from_heads(context.astype(bf16)).reshape(count, wide_q)
    context_rows = mm(context_rows, head_pick).astype(bf16)
    attended = mm(context_rows, out_weight)
    scale_two = norm_scale(attended)
    hidden_res = rows_in + attended * scale_two * post_attention
    scale_three = norm_scale(hidden_res)
    normed_two = (hidden_res * scale_three * pre_feed).astype(bf16)

    normed_group = gather_group(normed_two)
    gate_raw = mm(normed_group, gate_weight)
    up_raw = mm(normed_group, up_weight)
    hidden_low = (jax.nn.gelu(gate_raw, approximate=True) * up_raw).astype(bf16)
    mixed = scatter_group(mm(hidden_low, down_weight).astype(bf16))
    scale_four = norm_scale(mixed)
    result = hidden_res + mixed * scale_four * post_feed
    output = ungroup(jnp.where(valid, result, 0.0).astype(bf16))

    upstream = jnp.where(valid, regroup(cotangent).astype(f32), 0.0)
    grad_post_feed = jnp.sum(upstream * mixed * scale_four, axis=0)
    mixed_grad = norm_back(mixed, scale_four, post_feed * upstream).astype(bf16)
    mixed_group = gather_group(mixed_grad)
    hidden_grad = mm_nt(mixed_group, down_weight)
    _, gelu_pull = jax.vjp(lambda g, u: jax.nn.gelu(g, approximate=True) * u, gate_raw, up_raw)
    gate_grad, up_grad = gelu_pull(hidden_grad)
    gate_grad, up_grad = gate_grad.astype(bf16), up_grad.astype(bf16)
    normed_two_grad = scatter_group((mm_nt(gate_grad, gate_weight) + mm_nt(up_grad, up_weight)).astype(bf16))

    def collect(total):
        kept = lax.dynamic_index_in_dim(total, y_bit, 2, keepdims=False)
        sent = lax.dynamic_index_in_dim(total, 1 - y_bit, 2, keepdims=False)
        kept = add16(kept, xor(sent, "dp", 1))
        result = lax.dynamic_index_in_dim(kept, top_id, 0, keepdims=False).astype(f32)
        for k in range(1, tops):
            part = lax.dynamic_index_in_dim(kept, top_id ^ k, 0, keepdims=False)
            result = result + xor(part, "dp", 4 * k).astype(f32)
        return result

    def columns_home(total):
        mine = collect(total.astype(bf16).reshape(tops, 2, 2, members * model_rows, ff_local))
        return mine.astype(bf16).reshape(2, 2, 2, model_rows, ff_local)

    grad_down = mm_tn(hidden_low, mixed_group).astype(bf16).reshape(tops, 1, 2, ff_rows, width)
    grad_down = collect(grad_down)[0]
    both_grads = [columns_home(mm_tn(normed_group, grad)) for grad in (gate_grad, up_grad)]
    both_grads = exchange(jnp.stack(both_grads, axis=3))
    both_grads = both_grads.reshape(2, members, 2, model_rows, tops, 2, ff_rows)
    both_grads = both_grads.transpose(2, 3, 4, 0, 5, 1, 6).reshape(2, model_rows, -1).astype(f32)
    grad_pre_feed = jnp.sum(normed_two_grad * hidden_res * scale_three, axis=0)
    hidden_res_grad = upstream + norm_back(hidden_res, scale_three, pre_feed * normed_two_grad)

    grad_post_attention = jnp.sum(hidden_res_grad * attended * scale_two, axis=0)
    attended_grad = norm_back(attended, scale_two, post_attention * hidden_res_grad).astype(bf16)
    grad_out = scatter_all(mm_tn(context_rows, attended_grad).astype(bf16), out_rows)
    context_grad = mm_nt(attended_grad, out_weight).astype(bf16)
    context_grad = to_heads(mm_nt(context_grad, head_pick).astype(bf16))
    delta = jnp.sum(context_grad.astype(f32) * context, axis=-1).reshape(2, 1, HEADS * rows)
    query_grads, near_part, far_part = attend_back(
        meta, seq_ends, slots, query_heads, context_grad, lse, delta, near_keys, far_keys
    )
    near_part = add16(near_part, xor(far_part, "seq", 1)).reshape(2, layers, count, 2 * HEAD)
    near_part = add16(near_part[0], xor(near_part[1], "seq", 2))
    key_grads = near_part[0].astype(f32)
    for k in range(1, layers):
        key_grads = key_grads + xor(near_part[k], "dp", 2 * k).astype(f32)
    query_turned = rotate(from_heads(query_grads), cosine, -sine)
    grad_query_gain = jnp.sum(query_turned * query_raw * query_scale, axis=(0, 1))
    query_grad = norm_back(query_raw, query_scale, query_gain * query_turned)
    query_grad = query_grad.reshape(count, wide_q).astype(bf16)
    grad_query = scatter_all(mm_tn(picked_one, query_grad).astype(bf16), block_rows)
    value_grad = key_grads[:, HEAD:].astype(bf16)
    key_turned = rotate(key_grads[:, None, :HEAD], cosine, -sine)
    grad_key_gain = jnp.sum(key_turned * key_raw * key_scale, axis=(0, 1))
    key_grad = norm_back(key_raw, key_scale, key_gain * key_turned)[:, 0, :].astype(bf16)
    kv_grad = jnp.concatenate([key_grad, value_grad], axis=1)
    normed_one_grad = mm_nt(query_grad, mm(model_pick, q_weight).astype(bf16))
    normed_one_grad += mm_nt(kv_grad, mm(model_pick, kv_weight).astype(bf16))
    grad_pre_attention = jnp.sum(normed_one_grad * rows_in * scale_one, axis=0)
    rows_grad = hidden_res_grad + norm_back(rows_in, scale_one, pre_attention * normed_one_grad)
    input_grad = ungroup(rows_grad.astype(bf16))
    grad_kv = mm_tn(picked_one, kv_grad).reshape(devices, block_rows, 2 * HEAD)
    gain_grads = [
        grad_pre_attention,
        grad_post_attention,
        grad_pre_feed,
        grad_post_feed,
        grad_query_gain,
        grad_key_gain,
    ]
    gain_grads = jnp.concatenate([g.reshape(devices, -1) for g in gain_grads], axis=1)
    gain_grads = mm_tn(device_pick, gain_grads.astype(bf16))
    gain_grads = jnp.pad(
        gain_grads[:, None, :], ((0, 0), (model_rows, block_rows - model_rows - 1), (0, 2 * HEAD - gain_total))
    )
    last = scatter_all((grad_kv + gain_grads).astype(bf16).reshape(devices * block_rows, 2 * HEAD), block_rows)
    gain_out, at = [], 0
    for size in gain_sizes:
        gain_out.append(last[model_rows, at : at + size])
        at += size
    return (
        output,
        input_grad,
        grad_query[:model_rows],
        last[:model_rows, :HEAD],
        last[:model_rows, HEAD:],
        grad_out,
        both_grads[0],
        both_grads[1],
        grad_down,
        *gain_out,
    )


def solution(mesh):
    split = P(None, ALL, None)
    weight, gain = P(ALL, None), P(ALL)
    return jax.shard_map(
        per_device,
        mesh=mesh,
        in_specs=(split, split, P(), P(), *[weight] * 7, *[gain] * 6),
        out_specs=(split, split, *[weight] * 7, *[gain] * 6),
        check_vma=False,
    )
```

```python
import functools
import math

import jax
import jax.numpy as jnp
from jax import lax
from jax.experimental import pallas as pl
from jax.experimental.pallas import tpu as pltpu
from jax.sharding import PartitionSpec as P

HEADS = 4
HEAD = 256
MB = 2
STRETCH = 256

eps = 1e-06
rope_base = 1000000.0
masked_score = -1e30
bf16 = jnp.bfloat16
f32 = jnp.float32
ALL = ("dp", "seq")


def norm_scale(values):
    return lax.rsqrt(jnp.mean(values * values, axis=-1, keepdims=True) + eps)


def norm_back(values, scale, weighted):
    return scale * weighted - values * (scale * scale * scale) * jnp.mean(
        weighted * values, axis=-1, keepdims=True
    )


def rotate(values, cosine, sine):
    first, second = jnp.split(values, 2, axis=-1)
    return jnp.concatenate([first * cosine - second * sine, second * cosine + first * sine], axis=-1)


def layout_start(ends, row_ids):
    after = row_ids[:, None] >= ends[None, :]
    return jnp.max(jnp.where(after, ends[None, :], 0), axis=1)


def dot(left, right, dims):
    return lax.dot_general(left, right, (dims, ((), ())), preferred_element_type=f32)


def mm(left, right):
    return dot(left, right, ((1,), (0,)))


def mm_tn(left, right):
    return dot(left, right, ((0,), (0,)))


def mm_nt(left, right):
    return dot(left, right, ((1,), (1,)))


def xor(value, axis, mask):
    return lax.ppermute(value, axis, [(i, i ^ mask) for i in range(lax.axis_size(axis))])


def xor_both(value, dp_mask, seq_mask):
    members = lax.axis_size("seq")
    mask = dp_mask * members + seq_mask
    return lax.ppermute(value, ALL, [(i, i ^ mask) for i in range(lax.axis_size("dp") * members)])


def flips(value, bits):
    for axis, bit in enumerate(bits):
        halves = [lax.slice_in_dim(value, i, i + 1, axis=axis) for i in (1, 0)]
        value = jnp.where(bit == 1, lax.concatenate(halves, axis), value)
    return value


def add16(left, right):
    return (left.astype(f32) + right.astype(f32)).astype(bf16)


def after(value, *others):
    return lax.optimization_barrier((value, *others))[0]


def all_masks():
    rows = [(1 << bit, 0) for bit in range(1, 16) if 1 << bit < lax.axis_size("dp")]
    return rows + [(1, 0), (0, 2), (0, 1)]


def gather_all(piece):
    value = piece[None]
    for dp_mask, seq_mask in all_masks():
        value = jnp.concatenate([value, xor_both(value, dp_mask, seq_mask)])
    return value


def all_labels():
    labels = [(0, 0)]
    for dp_mask, seq_mask in all_masks():
        labels = labels + [(d ^ dp_mask, s ^ seq_mask) for d, s in labels]
    return labels


def scatter_all(total):
    for dp_mask, seq_mask in reversed(all_masks()):
        half = total.shape[0] // 2
        got = xor_both(total[half:], dp_mask, seq_mask)
        total = total[:half].astype(f32) + got.astype(f32)
        total = total if half == 1 else total.astype(bf16)
    return total[0]


def gather_group(rows):
    half = rows.shape[0] // 2
    across, along = xor(rows, "seq", 2), xor(rows, "dp", 2)
    corner = [xor(across[:half], "dp", 2), xor(along[half:], "seq", 2)]
    near = [rows, across, along, *corner]
    far = [rows, jnp.concatenate([across, along]), jnp.concatenate(corner)]
    return jnp.concatenate(near + [xor(part, "seq", 1) for part in far], axis=0)


def scatter_group(total):
    parts = total.reshape(2, -1, total.shape[1])
    near = add16(parts[0], xor(parts[1], "seq", 1))
    mine, across, along, corner = jnp.split(near, 4)
    half = mine.shape[0] // 2
    low, high = xor(corner[:half], "dp", 2), xor(corner[half:], "seq", 2)
    across = jnp.concatenate([add16(across[:half], low), across[half:]])
    along = jnp.concatenate([along[:half], add16(along[half:], high)])
    return mine.astype(f32) + xor(across, "seq", 2).astype(f32) + xor(along, "dp", 2).astype(f32)


def place_kernel(sizes, target_ref, *refs):
    pieces, out = refs[: len(sizes)], refs[len(sizes)]
    buffer, arrived, left = refs[len(sizes) + 1 :]
    ins, outs, block = [], [], 0
    for piece, size in zip(pieces, sizes):
        for index in range(size):
            ins.append(pltpu.make_async_copy(piece.at[index], buffer.at[block], arrived.at[block]))
            outs.append(pltpu.make_async_copy(buffer.at[block], out.at[target_ref[block]], left.at[block]))
            ins[-1].start()
            block += 1
    for copy_in, copy_out in zip(ins, outs):
        copy_in.wait()
        copy_out.start()
    for copy_out in outs:
        copy_out.wait()


def place(pieces, targets):
    sizes = [piece.shape[0] for piece in pieces]
    shape = (sum(sizes), *pieces[0].shape[1:])
    anywhere = pl.BlockSpec(memory_space=pl.ANY)
    return pl.pallas_call(
        functools.partial(place_kernel, sizes),
        grid_spec=pltpu.PrefetchScalarGridSpec(
            num_scalar_prefetch=1,
            grid=(1,),
            in_specs=[anywhere] * len(pieces),
            out_specs=anywhere,
            scratch_shapes=[
                pltpu.VMEM(shape, pieces[0].dtype),
                pltpu.SemaphoreType.DMA((shape[0],)),
                pltpu.SemaphoreType.DMA((shape[0],)),
            ],
        ),
        out_shape=jax.ShapeDtypeStruct(shape, pieces[0].dtype),
        name="place",
        cost_estimate=pl.CostEstimate(flops=0, bytes_accessed=4 * math.prod(shape), transcendentals=0),
    )(targets, *pieces)


def project_kernel(scale, picked_ref, weight_ref, gain_ref, cos_ref, sin_ref, raw_ref, out_ref):
    raw = mm(picked_ref[...], weight_ref[...])
    raw_ref[0] = raw
    turned = rotate(raw * norm_scale(raw) * gain_ref[...], cos_ref[...], sin_ref[...]).astype(bf16)
    out_ref[...] = (turned * scale).astype(bf16).reshape(out_ref.shape)


def project(picked, weight, gain, cosine, sine):
    count, deep = picked.shape
    rows = count // 2
    same = lambda h: (0, 0)
    return pl.pallas_call(
        functools.partial(project_kernel, HEAD**-0.5),
        grid=(HEADS,),
        in_specs=[
            pl.BlockSpec((count, deep), same),
            pl.BlockSpec((deep, HEAD), lambda h: (0, h)),
            pl.BlockSpec((1, HEAD), same),
            pl.BlockSpec((count, HEAD // 2), same),
            pl.BlockSpec((count, HEAD // 2), same),
        ],
        out_specs=[
            pl.BlockSpec((1, count, HEAD), lambda h: (h, 0, 0)),
            pl.BlockSpec((2, 1, rows, HEAD), lambda h: (0, h, 0, 0)),
        ],
        out_shape=[
            jax.ShapeDtypeStruct((HEADS, count, HEAD), f32),
            jax.ShapeDtypeStruct((2, HEADS, rows, HEAD), bf16),
        ],
        name="project",
        cost_estimate=pl.CostEstimate(
            flops=2 * count * deep * HEADS * HEAD, bytes_accessed=2 * deep * HEADS * HEAD, transcendentals=0
        ),
    )(picked, weight, gain, cosine, sine)


def project_keys_kernel(picked_ref, weight_ref, gain_ref, cos_ref, sin_ref, raw_ref, out_ref):
    both = mm(picked_ref[...], weight_ref[...])
    raw = both[:, :HEAD]
    raw_ref[...] = raw
    turned = rotate(raw * norm_scale(raw) * gain_ref[...], cos_ref[...], sin_ref[...])
    both = jnp.concatenate([turned, both[:, HEAD:]], axis=1).astype(bf16)
    out_ref[...] = both.reshape(out_ref.shape)


def project_keys(picked, weight, gain, cosine, sine):
    count, deep = picked.shape
    return pl.pallas_call(
        project_keys_kernel,
        out_shape=[
            jax.ShapeDtypeStruct((count, HEAD), f32),
            jax.ShapeDtypeStruct((2, count // 2, 2 * HEAD), bf16),
        ],
        name="project_keys",
        cost_estimate=pl.CostEstimate(
            flops=4 * count * deep * HEAD, bytes_accessed=4 * deep * HEAD, transcendentals=0
        ),
    )(picked, weight, gain, cosine, sine)


def mask_of(meta_ref, ends_ref, unit, rows, key_stretch):
    lanes = lax.broadcasted_iota(jnp.int32, (1, HEADS * rows), 1)
    ids = meta_ref[3 * unit] + lanes % rows
    start = jnp.zeros_like(ids)
    for index in range(ends_ref.shape[0]):
        end = ends_ref[index]
        start = jnp.where(ids >= end, end, start)
    place_in = lax.broadcasted_iota(jnp.int32, (STRETCH, 1), 0)
    near = meta_ref[6] * rows
    place_in = jnp.where(place_in < rows, place_in + near, place_in - near)
    key = key_stretch * STRETCH + place_in
    return (key <= ids) & (key >= start)


def attend_kernel(
    rows, meta_ref, ends_ref, slots_ref, q_ref, near_ref, far_ref, c_ref, turned_ref, lse_ref, top, total, acc
):
    step = pl.program_id(0)

    @pl.when(step == 0)
    def _():
        top[...] = jnp.full_like(top, masked_score)
        total[...] = jnp.zeros_like(total)
        acc[...] = jnp.zeros_like(acc)

    key_stretch = slots_ref[step]
    for unit in range(2):

        @pl.when((key_stretch <= meta_ref[3 * unit + 1]) & (key_stretch >= meta_ref[3 * unit + 2]))
        def _():
            mask = mask_of(meta_ref, ends_ref, unit, rows, key_stretch)
            block = jnp.concatenate([near_ref[...], far_ref[...]], axis=0)
            query = q_ref[unit].reshape(HEADS * rows, HEAD)
            scores = jnp.where(mask, mm_nt(block[:, :HEAD], query), masked_score)
            old = top[unit]
            new = jnp.maximum(old, jnp.max(scores, axis=0, keepdims=True))
            keep = jnp.exp(old - new)
            terms = jnp.exp(scores - new)
            top[unit] = new
            total[unit] = total[unit] * keep + jnp.sum(terms, axis=0, keepdims=True)
            acc[unit] = acc[unit] * keep + mm_tn(block[:, HEAD:], terms.astype(bf16))

    @pl.when(step == pl.num_programs(0) - 1)
    def _():
        for unit in range(2):
            out = acc[unit] * (1.0 / total[unit])
            turned_ref[unit] = out
            lse_ref[unit] = top[unit] + jnp.log(total[unit])
            out = out.T.astype(bf16)
            for head in range(HEADS):
                c_ref[unit * rows : (unit + 1) * rows, head * HEAD : (head + 1) * HEAD] = out[
                    head * rows : (head + 1) * rows
                ]


def attend_back_kernel(
    rows,
    meta_ref,
    ends_ref,
    slots_ref,
    q_ref,
    dc_ref,
    lse_ref,
    turned_ref,
    raw_ref,
    gain_ref,
    cos_ref,
    sin_ref,
    near_ref,
    far_ref,
    dq_ref,
    dgain_ref,
    dnear_ref,
    dfar_ref,
    grads,
    delta,
    acc,
    both,
):
    step = pl.program_id(0)

    @pl.when(step == 0)
    def _():
        acc[...] = jnp.zeros_like(acc)
        for unit in range(2):
            for head in range(HEADS):
                grads[unit, head * rows : (head + 1) * rows] = dc_ref[
                    unit * rows : (unit + 1) * rows, head * HEAD : (head + 1) * HEAD
                ]
            across = grads[unit].astype(f32).T
            delta[unit] = jnp.sum(across * turned_ref[unit], axis=0, keepdims=True)

    key_stretch = slots_ref[step]
    both[...] = jnp.zeros_like(both)
    for unit in range(2):

        @pl.when((key_stretch <= meta_ref[3 * unit + 1]) & (key_stretch >= meta_ref[3 * unit + 2]))
        def _():
            mask = mask_of(meta_ref, ends_ref, unit, rows, key_stretch)
            block = jnp.concatenate([near_ref[...], far_ref[...]], axis=0)
            key, value = block[:, :HEAD], block[:, HEAD:]
            query = q_ref[unit].reshape(HEADS * rows, HEAD)
            grad = grads[unit]
            probs = jnp.where(mask, jnp.exp(mm_nt(key, query) - lse_ref[unit]), 0.0)
            score_grad = (probs * (mm_nt(value, grad) - delta[unit])).astype(bf16)
            acc[unit] += mm_tn(key, score_grad)
            both[:, :HEAD] += mm(score_grad, query)
            both[:, HEAD:] += mm(probs.astype(bf16), grad)

    dnear_ref[...] = both[:rows].astype(bf16)
    dfar_ref[...] = both[rows:].astype(bf16)

    @pl.when(step == pl.num_programs(0) - 1)
    def _():
        gain = gain_ref[...]
        total = jnp.zeros_like(gain)
        for unit in range(2):
            mine = slice(unit * rows, (unit + 1) * rows)
            grad = acc[unit].T * HEAD**-0.5
            for head in range(HEADS):
                back = rotate(grad[head * rows : (head + 1) * rows], cos_ref[mine], -sin_ref[mine])
                raw = raw_ref[head, mine]
                scale = norm_scale(raw)
                total = total + jnp.sum(back * raw * scale, axis=0, keepdims=True)
                back = norm_back(raw, scale, gain * back)
                dq_ref[mine, head * HEAD : (head + 1) * HEAD] = back.astype(bf16)
        dgain_ref[...] = total


def whole_of(array):
    return pl.BlockSpec(array.shape, lambda *_: (0,) * len(array.shape))


def attend(meta, ends, slots, query, near, far):
    rows = query.shape[2]
    wide = HEADS * rows
    keys = pl.BlockSpec((None, None, rows, 2 * HEAD), lambda j, *_: (j // 2, j % 2, 0, 0))
    outs = [
        jax.ShapeDtypeStruct((2 * rows, HEADS * HEAD), bf16),
        jax.ShapeDtypeStruct((2, HEAD, wide), f32),
        jax.ShapeDtypeStruct((2, 1, wide), f32),
    ]
    return pl.pallas_call(
        functools.partial(attend_kernel, rows),
        grid_spec=pltpu.PrefetchScalarGridSpec(
            num_scalar_prefetch=3,
            grid=(slots.shape[0],),
            in_specs=[whole_of(query), keys, keys],
            out_specs=[whole_of(out) for out in outs],
            scratch_shapes=[
                pltpu.VMEM((2, 1, wide), f32),
                pltpu.VMEM((2, 1, wide), f32),
                pltpu.VMEM((2, HEAD, wide), f32),
            ],
        ),
        out_shape=outs,
        name="attend",
        cost_estimate=pl.CostEstimate(
            flops=4 * 2 * 9 * STRETCH * wide * HEAD,
            bytes_accessed=4 * near.size,
            transcendentals=2 * 9 * STRETCH * wide,
        ),
    )(meta, ends, slots, query, near, far)


def attend_back(meta, ends, slots, query, grad, lse, turned, raw, gain, cosine, sine, near, far):
    rows = query.shape[2]
    wide = HEADS * rows
    keys = pl.BlockSpec((None, None, rows, 2 * HEAD), lambda j, *_: (j // 2, j % 2, 0, 0))
    fixed = [query, grad, lse, turned, raw, gain, cosine, sine]
    outs = [jax.ShapeDtypeStruct(grad.shape, bf16), jax.ShapeDtypeStruct(gain.shape, f32)]
    return pl.pallas_call(
        functools.partial(attend_back_kernel, rows),
        grid_spec=pltpu.PrefetchScalarGridSpec(
            num_scalar_prefetch=3,
            grid=(slots.shape[0],),
            in_specs=[*[whole_of(array) for array in fixed], keys, keys],
            out_specs=[*[whole_of(out) for out in outs], keys, keys],
            scratch_shapes=[
                pltpu.VMEM((2, wide, HEAD), bf16),
                pltpu.VMEM((2, 1, wide), f32),
                pltpu.VMEM((2, HEAD, wide), f32),
                pltpu.VMEM((STRETCH, 2 * HEAD), f32),
            ],
        ),
        out_shape=[*outs, jax.ShapeDtypeStruct(near.shape, bf16), jax.ShapeDtypeStruct(near.shape, bf16)],
        name="attend_back",
        cost_estimate=pl.CostEstimate(
            flops=10 * 2 * 9 * STRETCH * wide * HEAD,
            bytes_accessed=8 * near.size,
            transcendentals=2 * 9 * STRETCH * wide,
        ),
    )(meta, ends, slots, *fixed, near, far)


def blocks_of(tops, low, member, members, ff):
    return [(((hi * 2 + low) * 2 + y) * members + member) * ff for hi in range(tops) for y in range(2)]

def pack_kernel(tops, members, ff, gate_ref, up_ref, out_ref):
    for which, ref in enumerate((gate_ref, up_ref)):
        value = ref[...]
        for low in range(2):
            for member in range(members):
                cuts = [value[:, at : at + ff] for at in blocks_of(tops, low, member, members, ff)]
                out_ref[low, member, which] = jnp.concatenate(cuts, axis=1)

def pack(gate, up, tops, members, ff):
    rows = gate.shape[0]
    return pl.pallas_call(functools.partial(pack_kernel, tops, members, ff),
        out_shape=jax.ShapeDtypeStruct((2, members, 2, rows, 2 * tops * ff), bf16), name="pack")(gate, up)

def unpack_kernel(tops, members, ff, low_ref, in_ref, gate_ref, up_ref):
    for which, ref in enumerate((gate_ref, up_ref)):
        pieces = [None] * (2 * tops * 2 * members)
        for low in range(2):
            for member in range(members):
                value = in_ref[member, low_ref[0] ^ low, which].astype(f32)
                for i, at in enumerate(blocks_of(tops, low, member, members, ff)):
                    pieces[at // ff] = value[:, i * ff : (i + 1) * ff]
        ref[...] = jnp.concatenate(pieces, axis=1)

def unpack(moved, low_bit, tops, members, ff):
    rows = moved.shape[3]
    shape = jax.ShapeDtypeStruct((rows, 4 * tops * members * ff), f32)
    return pl.pallas_call(functools.partial(unpack_kernel, tops, members, ff),
        in_specs=[pl.BlockSpec(memory_space=pltpu.SMEM), pl.BlockSpec(memory_space=pltpu.VMEM)],
        out_shape=[shape, shape], name="unpack")(low_bit[None], moved)

def merge_kernel(in_ref, gate_ref, up_ref):
    for which, ref in enumerate((gate_ref, up_ref)):
        for low in range(2):
            ref[low] = jnp.concatenate([in_ref[m, low, which] for m in range(in_ref.shape[0])], axis=0)

def merge(moved):
    members, _, _, rows, wide = moved.shape
    shape = jax.ShapeDtypeStruct((2, members * rows, wide), bf16)
    return pl.pallas_call(merge_kernel, out_shape=[shape, shape], name="merge")(moved)

def split_kernel(gate_ref, up_ref, out_ref):
    members, rows = out_ref.shape[1], out_ref.shape[3]
    for which, ref in enumerate((gate_ref, up_ref)):
        for low in range(2):
            value = ref[low]
            for m in range(members):
                out_ref[low, m, which] = value[m * rows : (m + 1) * rows]

def split(gate, up, members):
    _, tall, wide = gate.shape
    return pl.pallas_call(split_kernel,
        out_shape=jax.ShapeDtypeStruct((2, members, 2, tall // members, wide), bf16), name="split")(gate, up)


def per_device(
    inputs,
    cotangent,
    lengths,
    deal,
    w_query,
    w_key,
    w_value,
    w_out,
    w_gate,
    w_up,
    w_down,
    gain_attn_pre,
    gain_attn_post,
    gain_ffw_pre,
    gain_ffw_post,
    gain_query,
    gain_key,
):
    rows, width = inputs.shape[1], inputs.shape[2]
    groups, members = lax.axis_size("dp"), lax.axis_size("seq")
    devices = groups * members
    total_rows = rows * devices
    dp_id, seq_id = lax.axis_index("dp"), lax.axis_index("seq")
    half_bit, x_bit, y_bit, z_bit = seq_id % 2, seq_id // 2, dp_id % 2, dp_id // 2 % 2
    tops = groups // 4
    count = 2 * rows
    model_rows, out_rows, ff_rows = w_query.shape[0], w_out.shape[0], w_down.shape[0]
    ff_local = 2 * tops * ff_rows
    wide_q = HEADS * HEAD
    gain_sizes = [gain_attn_pre.shape[0]] * 4 + [gain_query.shape[0]] * 2
    gain_total = sum(gain_sizes)
    block_rows = (model_rows + 8) // 8 * 8

    def regroup(array):
        kept = lax.dynamic_index_in_dim(array, y_bit, 0, keepdims=False)
        sent = lax.dynamic_index_in_dim(array, 1 - y_bit, 0, keepdims=False)
        return jnp.concatenate([kept, xor(sent, "dp", 1)], axis=0)

    def ungroup(array):
        kept, sent = array[:rows], array[rows:]
        return flips(jnp.stack([kept, xor(sent, "dp", 1)]), [y_bit])

    rows_in = regroup(inputs).astype(f32)

    gains = jnp.concatenate([gain_attn_pre, gain_attn_post, gain_ffw_pre, gain_ffw_post, gain_query, gain_key])
    gain_line = jnp.pad(gains[None, :], ((0, 0), (0, 2 * HEAD - gain_total)))
    kv_shard = jnp.concatenate([jnp.concatenate([w_key, w_value], axis=1), gain_line], axis=0)
    kv_blocks = gather_all(jnp.pad(kv_shard, ((0, block_rows - model_rows - 1), (0, 0))))
    kv_weight = kv_blocks.reshape(devices * block_rows, 2 * HEAD)
    q_shard = after(jnp.pad(w_query, ((0, block_rows - model_rows), (0, 0))), kv_weight)
    q_weight = gather_all(q_shard).reshape(devices * block_rows, wide_q)
    out_blocks = gather_all(after(w_out, q_weight))
    labels = all_labels()
    natural = jnp.stack([(dp_id ^ d) * members + (seq_id ^ s) for d, s in labels]).astype(jnp.int32)

    def selection(size, block, padded):
        within = jnp.arange(padded, dtype=jnp.int32)
        source = jnp.where(within < block, natural[:, None] * block + within, -1).reshape(-1)
        return (jnp.arange(size, dtype=jnp.int32)[:, None] == source[None, :]).astype(bf16)

    model_pick = selection(width, model_rows, block_rows)
    relative = jnp.arange(devices, dtype=jnp.int32)
    relative = jnp.sum(jnp.where(natural[:, None] == relative[None, :], relative[:, None], 0), axis=0)
    out_weight = place([out_blocks], natural).reshape(wide_q, width)
    device_pick = selection(devices, 1, 1)
    gain_blocks = kv_blocks[:, model_rows, :gain_total]
    gain_all = mm(device_pick, gain_blocks)
    full_gain, at = [], 0
    for size in gain_sizes:
        full_gain.append(gain_all[:, at : at + size].reshape(devices * size))
        at += size
    pre_attention, post_attention, pre_feed, post_feed, query_gain, key_gain = full_gain

    top_id = dp_id // 4

    def spread(piece):
        tall = [piece] + [xor(piece, "dp", 4 * k) for k in range(1, tops)]
        return tall + [xor(part, "dp", 1) for part in tall]

    def swap_columns(packed):
        kept = lax.dynamic_index_in_dim(packed, z_bit, 0, keepdims=False)
        sent = lax.dynamic_index_in_dim(packed, 1 - z_bit, 0, keepdims=False)
        both = jnp.stack([kept, xor(sent, "dp", 2)], axis=1)
        return lax.all_to_all(both, "seq", split_axis=0, concat_axis=0, tiled=True)

    def feed_weights(w_gate, w_up, w_down):
        owners = [(top_id ^ k) * 2 + (y_bit ^ u) for u in range(2) for k in range(tops)]
        down_weight = place(spread(w_down[None]), jnp.stack(owners).astype(jnp.int32)).reshape(ff_local, width)
        halves = merge(swap_columns(pack(w_gate, w_up, tops, members, ff_rows)))
        sources = [((top_id ^ k) * 2 + (z_bit ^ v)) * 2 + (y_bit ^ u) for u in range(2) for k in range(tops) for v in range(2)]
        sources = jnp.stack(sources).astype(jnp.int32)
        gate_weight, up_weight = [place(spread(half), sources).reshape(width, ff_local) for half in halves]
        return gate_weight, up_weight, down_weight

    seq_ends = jnp.cumsum(lax.dynamic_index_in_dim(lengths, y_bit, 0, keepdims=False))
    dealt = lax.dynamic_index_in_dim(deal, y_bit, 0, keepdims=False)
    unit_ids = jnp.stack([(dp_id ^ u) * members + seq_id for u in range(2)])
    stretches = dealt[unit_ids * rows // STRETCH]
    first_rows = stretches * STRETCH + unit_ids * rows % STRETCH
    my_rows = (first_rows[:, None] + jnp.arange(rows, dtype=jnp.int32)).reshape(count)
    starts = layout_start(seq_ends, my_rows)
    lows = starts.reshape(2, rows)[:, 0] // STRETCH
    meta = jnp.concatenate([jnp.stack([first_rows, stretches, lows], axis=1).reshape(-1), half_bit[None]])
    layers = groups // 2
    slot_ids = jnp.stack(
        [
            ((dp_id // 2 ^ z) * 2 + (y_bit ^ u)) * (members // 2) + (x_bit ^ x)
            for x in range(2)
            for z in range(layers)
            for u in range(2)
        ]
    )
    slots = dealt[slot_ids]
    positions = my_rows - starts
    valid = (my_rows < total_rows - STRETCH)[:, None]
    freqs = rope_base ** (-2.0 * jnp.arange(HEAD // 2, dtype=f32) / HEAD)
    angle = positions.astype(f32)[:, None] * freqs
    cosine, sine = jnp.cos(angle), jnp.sin(angle)

    scale_one = norm_scale(rows_in)
    normed_one = (rows_in * scale_one * pre_attention).astype(bf16)
    picked_one = mm(normed_one, model_pick).astype(bf16)
    key_raw, keys_mine = project_keys(picked_one, kv_weight, key_gain[None], cosine, sine)
    column = [keys_mine] + [xor(keys_mine, "dp", 2 * k) for k in range(1, layers)]
    across = [xor(part, "seq", 2) for part in column]
    column, across = jnp.stack(column), jnp.stack(across)
    near_keys = jnp.concatenate([column, across])
    far_keys = jnp.concatenate([xor(column, "seq", 1), xor(across, "seq", 1)])
    gate_weight, up_weight, down_weight = feed_weights(*lax.optimization_barrier((w_gate, w_up, w_down, keys_mine))[:3])
    query_raw, query_heads = project(picked_one, q_weight, query_gain[None], cosine, sine)
    q_natural = mm(model_pick, q_weight).astype(bf16)
    kv_natural = mm(model_pick, kv_weight).astype(bf16)
    query_heads, q_natural, kv_natural = lax.optimization_barrier((query_heads, q_natural, kv_natural))
    context_rows, turned, lse = attend(meta, seq_ends, slots, query_heads, near_keys, far_keys)
    attended = mm(context_rows, out_weight)
    scale_two = norm_scale(attended)
    hidden_res = rows_in + attended * scale_two * post_attention
    scale_three = norm_scale(hidden_res)
    normed_two = (hidden_res * scale_three * pre_feed).astype(bf16)

    normed_group = gather_group(normed_two)
    gate_raw = mm(normed_group, gate_weight)
    up_raw = mm(normed_group, up_weight)
    hidden_low = (jax.nn.gelu(gate_raw, approximate=True) * up_raw).astype(bf16)
    mixed = scatter_group(mm(hidden_low, down_weight).astype(bf16))
    scale_four = norm_scale(mixed)
    result = hidden_res + mixed * scale_four * post_feed
    output = ungroup(jnp.where(valid, result, 0.0).astype(bf16))

    upstream = jnp.where(valid, regroup(cotangent).astype(f32), 0.0)
    grad_post_feed = jnp.sum(upstream * mixed * scale_four, axis=0)
    mixed_grad = norm_back(mixed, scale_four, post_feed * upstream).astype(bf16)
    mixed_group = gather_group(mixed_grad)
    hidden_grad = mm_nt(mixed_group, down_weight)
    _, gelu_pull = jax.vjp(lambda g, u: jax.nn.gelu(g, approximate=True) * u, gate_raw, up_raw)
    gate_grad, up_grad = gelu_pull(hidden_grad)
    gate_grad, up_grad = gate_grad.astype(bf16), up_grad.astype(bf16)
    partial_grad = (mm_nt(gate_grad, gate_weight) + mm_nt(up_grad, up_weight)).astype(bf16)
    normed_two_grad = scatter_group(partial_grad)
    grad_pre_feed = jnp.sum(normed_two_grad * hidden_res * scale_three, axis=0)
    hidden_res_grad = upstream + norm_back(hidden_res, scale_three, pre_feed * normed_two_grad)

    def halve(total):
        kept = lax.dynamic_index_in_dim(total, y_bit, 2, keepdims=False)
        return kept, xor(lax.dynamic_index_in_dim(total, 1 - y_bit, 2, keepdims=False), "dp", 1)

    def finish(kept, got):
        kept = add16(kept, got)
        mine = lax.dynamic_index_in_dim(kept, top_id, 0, keepdims=False)
        rest = [xor(lax.dynamic_index_in_dim(kept, top_id ^ k, 0, keepdims=False), "dp", 4 * k) for k in range(1, tops)]
        return [mine, *rest]

    def total_of(parts):
        return functools.reduce(jnp.add, [part.astype(f32) for part in parts])

    def column_blocks(total):
        return total.astype(bf16).reshape(tops, 2, 2, members * model_rows, ff_local)

    hidden_low, mixed_group, normed_group, gate_grad, up_grad, _ = lax.optimization_barrier(
        (hidden_low, mixed_group, normed_group, gate_grad, up_grad, partial_grad)
    )
    down_halves = halve(mm_tn(hidden_low, mixed_group).astype(bf16).reshape(tops, 1, 2, ff_rows, width))
    gate_halves = halve(column_blocks(mm_tn(normed_group, gate_grad)))
    up_halves = halve(column_blocks(mm_tn(normed_group, up_grad)))

    grad_post_attention = jnp.sum(hidden_res_grad * attended * scale_two, axis=0)
    attended_grad = norm_back(attended, scale_two, post_attention * hidden_res_grad).astype(bf16)
    context_grad = mm_nt(attended_grad, out_weight).astype(bf16)
    query_grad, grad_query_gain, near_part, far_part = attend_back(
        meta, seq_ends, slots, query_heads, context_grad, lse, turned, query_raw, query_gain[None], cosine, sine, near_keys, far_keys
    )
    halves = lax.optimization_barrier((down_halves, gate_halves, up_halves, context_grad))[:3]
    down_parts, gate_parts, up_parts = [finish(*half) for half in halves]
    far_part = xor(far_part, "seq", 1)
    near_part = add16(near_part, far_part).reshape(2, layers, count, 2 * HEAD)
    near_part = add16(near_part[0], xor(near_part[1], "seq", 2))
    key_grads = near_part[0].astype(f32)
    for k in range(1, layers):
        key_grads = key_grads + xor(near_part[k], "dp", 2 * k).astype(f32)
    attended_low, query_low, _ = lax.optimization_barrier((attended_grad, query_grad, far_part))
    grad_out = mm_tn(context_rows, attended_low).astype(bf16).reshape(devices, out_rows, width)
    grad_query = mm_tn(picked_one, query_low).astype(bf16).reshape(devices, block_rows, wide_q)
    grad_query = scatter_all(grad_query)
    grad_out = scatter_all(place([grad_out], relative))
    down_parts, gate_parts, up_parts, _ = lax.optimization_barrier((down_parts, gate_parts, up_parts, near_part))
    grad_down = total_of(down_parts)[0]
    both_grads = split(total_of(gate_parts).astype(bf16), total_of(up_parts).astype(bf16), members)
    grad_gate, grad_up = unpack(swap_columns(both_grads), z_bit, tops, members, ff_rows)
    value_grad = key_grads[:, HEAD:].astype(bf16)
    key_turned = rotate(key_grads[:, :HEAD], cosine, -sine)
    key_scale = norm_scale(key_raw)
    grad_key_gain = jnp.sum(key_turned * key_raw * key_scale, axis=0)
    key_grad = norm_back(key_raw, key_scale, key_gain * key_turned).astype(bf16)
    kv_grad = jnp.concatenate([key_grad, value_grad], axis=1)
    normed_one_grad = mm_nt(query_grad, q_natural) + mm_nt(kv_grad, kv_natural)
    grad_pre_attention = jnp.sum(normed_one_grad * rows_in * scale_one, axis=0)
    rows_grad = hidden_res_grad + norm_back(rows_in, scale_one, pre_attention * normed_one_grad)
    input_grad = ungroup(rows_grad.astype(bf16))
    grad_kv = mm_tn(picked_one, kv_grad).reshape(devices, block_rows, 2 * HEAD)
    gain_grads = [
        grad_pre_attention,
        grad_post_attention,
        grad_pre_feed,
        grad_post_feed,
        grad_query_gain,
        grad_key_gain,
    ]
    gain_grads = jnp.concatenate([g.reshape(devices, -1) for g in gain_grads], axis=1)
    gain_grads = mm_tn(device_pick, gain_grads.astype(bf16))
    gain_grads = jnp.pad(
        gain_grads[:, None, :], ((0, 0), (model_rows, block_rows - model_rows - 1), (0, 2 * HEAD - gain_total))
    )
    last = scatter_all((grad_kv + gain_grads).astype(bf16))
    gain_out, at = [], 0
    for size in gain_sizes:
        gain_out.append(last[model_rows, at : at + size])
        at += size
    return (
        output,
        input_grad,
        grad_query[:model_rows],
        last[:model_rows, :HEAD],
        last[:model_rows, HEAD:],
        grad_out,
        grad_gate,
        grad_up,
        grad_down,
        *gain_out,
    )


def solution(mesh):
    split = P(None, ALL, None)
    weight, gain = P(ALL, None), P(ALL)
    return jax.shard_map(
        per_device,
        mesh=mesh,
        in_specs=(split, split, P(), P(), *[weight] * 7, *[gain] * 6),
        out_specs=(split, split, *[weight] * 7, *[gain] * 6),
        check_vma=False,
    )
```

```python
import functools
import math

import jax
import jax.numpy as jnp
from jax import lax
from jax.experimental import pallas as pl
from jax.experimental.layout import Layout, with_layout_constraint
from jax.experimental.pallas import tpu as pltpu
from jax.sharding import PartitionSpec as P

HEADS = 4
HEAD = 256
MB = 2
STRETCH = 256

eps = 1e-06
rope_base = 1000000.0
masked_score = -1e30
bf16 = jnp.bfloat16
f32 = jnp.float32
ALL = ("dp", "seq")


def norm_scale(values):
    return lax.rsqrt(jnp.mean(values * values, axis=-1, keepdims=True) + eps)


def norm_back(values, scale, weighted):
    return scale * weighted - values * (scale * scale * scale) * jnp.mean(
        weighted * values, axis=-1, keepdims=True
    )


def rotate(values, cosine, sine):
    first, second = jnp.split(values, 2, axis=-1)
    return jnp.concatenate([first * cosine - second * sine, second * cosine + first * sine], axis=-1)


def layout_start(ends, row_ids):
    after = row_ids[:, None] >= ends[None, :]
    return jnp.max(jnp.where(after, ends[None, :], 0), axis=1)


def dot(left, right, dims):
    return lax.dot_general(left, right, (dims, ((), ())), preferred_element_type=f32)


def mm(left, right):
    return dot(left, right, ((1,), (0,)))


def mm_tn(left, right):
    return dot(left, right, ((0,), (0,)))


def mm_nt(left, right):
    return dot(left, right, ((1,), (1,)))


def xor(value, axis, mask):
    return lax.ppermute(value, axis, [(i, i ^ mask) for i in range(lax.axis_size(axis))])


def xor_both(value, dp_mask, seq_mask):
    members = lax.axis_size("seq")
    mask = dp_mask * members + seq_mask
    return lax.ppermute(value, ALL, [(i, i ^ mask) for i in range(lax.axis_size("dp") * members)])


def flips(value, bits):
    for axis, bit in enumerate(bits):
        halves = [lax.slice_in_dim(value, i, i + 1, axis=axis) for i in (1, 0)]
        value = jnp.where(bit == 1, lax.concatenate(halves, axis), value)
    return value


def add16(left, right):
    return (left.astype(f32) + right.astype(f32)).astype(bf16)


def after(value, *others):
    return lax.optimization_barrier((value, *others))[0]


def all_masks():
    rows = [(1 << bit, 0) for bit in range(1, 16) if 1 << bit < lax.axis_size("dp")]
    return rows + [(1, 0), (0, 2), (0, 1)]


def gather_all(piece):
    value = piece[None]
    for dp_mask, seq_mask in all_masks():
        value = jnp.concatenate([value, xor_both(value, dp_mask, seq_mask)])
    return value


def all_labels():
    labels = [(0, 0)]
    for dp_mask, seq_mask in all_masks():
        labels = labels + [(d ^ dp_mask, s ^ seq_mask) for d, s in labels]
    return labels


def scatter_all(total):
    for dp_mask, seq_mask in reversed(all_masks()):
        half = total.shape[0] // 2
        got = xor_both(total[half:], dp_mask, seq_mask)
        total = total[:half].astype(f32) + got.astype(f32)
        total = total if half == 1 else total.astype(bf16)
    return total[0]


def gather_group(rows):
    half = rows.shape[0] // 2
    across, along = xor(rows, "seq", 2), xor(rows, "dp", 2)
    corner = [xor(across[:half], "dp", 2), xor(along[half:], "seq", 2)]
    near = [rows, across, along, *corner]
    far = [rows, jnp.concatenate([across, along]), jnp.concatenate(corner)]
    return jnp.concatenate(near + [xor(part, "seq", 1) for part in far], axis=0)


def scatter_group(total):
    parts = total.reshape(2, -1, total.shape[1])
    near = add16(parts[0], xor(parts[1], "seq", 1))
    mine, across, along, corner = jnp.split(near, 4)
    half = mine.shape[0] // 2
    low, high = xor(corner[:half], "dp", 2), xor(corner[half:], "seq", 2)
    across = jnp.concatenate([add16(across[:half], low), across[half:]])
    along = jnp.concatenate([along[:half], add16(along[half:], high)])
    return mine.astype(f32) + xor(across, "seq", 2).astype(f32) + xor(along, "dp", 2).astype(f32)


def place_kernel(sizes, target_ref, *refs):
    pieces, out = refs[: len(sizes)], refs[len(sizes)]
    buffer, arrived, left = refs[len(sizes) + 1 :]
    ins, outs, block = [], [], 0
    for piece, size in zip(pieces, sizes):
        for index in range(size):
            ins.append(pltpu.make_async_copy(piece.at[index], buffer.at[block], arrived.at[block]))
            outs.append(pltpu.make_async_copy(buffer.at[block], out.at[target_ref[block]], left.at[block]))
            ins[-1].start()
            block += 1
    for copy_in, copy_out in zip(ins, outs):
        copy_in.wait()
        copy_out.start()
    for copy_out in outs:
        copy_out.wait()


def place(pieces, targets):
    sizes = [piece.shape[0] for piece in pieces]
    shape = (sum(sizes), *pieces[0].shape[1:])
    anywhere = pl.BlockSpec(memory_space=pl.ANY)
    return pl.pallas_call(
        functools.partial(place_kernel, sizes),
        grid_spec=pltpu.PrefetchScalarGridSpec(
            num_scalar_prefetch=1,
            grid=(1,),
            in_specs=[anywhere] * len(pieces),
            out_specs=anywhere,
            scratch_shapes=[
                pltpu.VMEM(shape, pieces[0].dtype),
                pltpu.SemaphoreType.DMA((shape[0],)),
                pltpu.SemaphoreType.DMA((shape[0],)),
            ],
        ),
        out_shape=jax.ShapeDtypeStruct(shape, pieces[0].dtype),
        name="place",
        cost_estimate=pl.CostEstimate(flops=0, bytes_accessed=4 * math.prod(shape), transcendentals=0),
    )(targets, *pieces)


def project_kernel(scale, picked_ref, weight_ref, gain_ref, cos_ref, sin_ref, raw_ref, out_ref):
    raw = mm(picked_ref[...], weight_ref[...])
    raw_ref[0] = raw
    turned = rotate(raw * norm_scale(raw) * gain_ref[...], cos_ref[...], sin_ref[...]).astype(bf16)
    out_ref[...] = (turned * scale).astype(bf16).reshape(out_ref.shape)


def project(picked, weight, gain, cosine, sine):
    count, deep = picked.shape
    rows = count // 2
    same = lambda h: (0, 0)
    return pl.pallas_call(
        functools.partial(project_kernel, HEAD**-0.5),
        grid=(HEADS,),
        in_specs=[
            pl.BlockSpec((count, deep), same),
            pl.BlockSpec((deep, HEAD), lambda h: (0, h)),
            pl.BlockSpec((1, HEAD), same),
            pl.BlockSpec((count, HEAD // 2), same),
            pl.BlockSpec((count, HEAD // 2), same),
        ],
        out_specs=[
            pl.BlockSpec((1, count, HEAD), lambda h: (h, 0, 0)),
            pl.BlockSpec((2, 1, rows, HEAD), lambda h: (0, h, 0, 0)),
        ],
        out_shape=[
            jax.ShapeDtypeStruct((HEADS, count, HEAD), f32),
            jax.ShapeDtypeStruct((2, HEADS, rows, HEAD), bf16),
        ],
        name="project",
        cost_estimate=pl.CostEstimate(
            flops=2 * count * deep * HEADS * HEAD, bytes_accessed=2 * deep * HEADS * HEAD, transcendentals=0
        ),
    )(picked, weight, gain, cosine, sine)


def project_keys_kernel(picked_ref, weight_ref, gain_ref, cos_ref, sin_ref, raw_ref, out_ref):
    both = mm(picked_ref[...], weight_ref[...])
    raw = both[:, :HEAD]
    raw_ref[...] = raw
    turned = rotate(raw * norm_scale(raw) * gain_ref[...], cos_ref[...], sin_ref[...])
    both = jnp.concatenate([turned, both[:, HEAD:]], axis=1).astype(bf16)
    out_ref[...] = both.reshape(out_ref.shape)


def project_keys(picked, weight, gain, cosine, sine):
    count, deep = picked.shape
    return pl.pallas_call(
        project_keys_kernel,
        out_shape=[
            jax.ShapeDtypeStruct((count, HEAD), f32),
            jax.ShapeDtypeStruct((2, count // 2, 2 * HEAD), bf16),
        ],
        name="project_keys",
        cost_estimate=pl.CostEstimate(
            flops=4 * count * deep * HEAD, bytes_accessed=4 * deep * HEAD, transcendentals=0
        ),
    )(picked, weight, gain, cosine, sine)


def mask_of(meta_ref, ends_ref, unit, rows, key_stretch):
    lanes = lax.broadcasted_iota(jnp.int32, (1, HEADS * rows), 1)
    ids = meta_ref[3 * unit] + lanes % rows
    start = jnp.zeros_like(ids)
    for index in range(ends_ref.shape[0]):
        end = ends_ref[index]
        start = jnp.where(ids >= end, end, start)
    place_in = lax.broadcasted_iota(jnp.int32, (STRETCH, 1), 0)
    near = meta_ref[6] * rows
    place_in = jnp.where(place_in < rows, place_in + near, place_in - near)
    key = key_stretch * STRETCH + place_in
    return (key <= ids) & (key >= start)


def attend_kernel(
    rows, meta_ref, ends_ref, slots_ref, q_ref, near_ref, far_ref, c_ref, turned_ref, lse_ref, top, total, acc
):
    step = pl.program_id(0)

    @pl.when(step == 0)
    def _():
        top[...] = jnp.full_like(top, masked_score)
        total[...] = jnp.zeros_like(total)
        acc[...] = jnp.zeros_like(acc)

    key_stretch = slots_ref[step]
    for unit in range(2):

        @pl.when((key_stretch <= meta_ref[3 * unit + 1]) & (key_stretch >= meta_ref[3 * unit + 2]))
        def _():
            mask = mask_of(meta_ref, ends_ref, unit, rows, key_stretch)
            block = jnp.concatenate([near_ref[...], far_ref[...]], axis=0)
            query = q_ref[unit].reshape(HEADS * rows, HEAD)
            scores = jnp.where(mask, mm_nt(block[:, :HEAD], query), masked_score)
            old = top[unit]
            new = jnp.maximum(old, jnp.max(scores, axis=0, keepdims=True))
            keep = jnp.exp(old - new)
            terms = jnp.exp(scores - new)
            top[unit] = new
            total[unit] = total[unit] * keep + jnp.sum(terms, axis=0, keepdims=True)
            acc[unit] = acc[unit] * keep + mm_tn(block[:, HEAD:], terms.astype(bf16))

    @pl.when(step == pl.num_programs(0) - 1)
    def _():
        for unit in range(2):
            out = acc[unit] * (1.0 / total[unit])
            turned_ref[unit] = out
            lse_ref[unit] = top[unit] + jnp.log(total[unit])
            out = out.T.astype(bf16)
            for head in range(HEADS):
                c_ref[unit * rows : (unit + 1) * rows, head * HEAD : (head + 1) * HEAD] = out[
                    head * rows : (head + 1) * rows
                ]


def attend_back_kernel(
    rows,
    meta_ref,
    ends_ref,
    slots_ref,
    q_ref,
    dc_ref,
    lse_ref,
    turned_ref,
    raw_ref,
    gain_ref,
    cos_ref,
    sin_ref,
    near_ref,
    far_ref,
    dq_ref,
    dgain_ref,
    dnear_ref,
    dfar_ref,
    grads,
    delta,
    acc,
    both,
):
    step = pl.program_id(0)

    @pl.when(step == 0)
    def _():
        acc[...] = jnp.zeros_like(acc)
        for unit in range(2):
            for head in range(HEADS):
                grads[unit, head * rows : (head + 1) * rows] = dc_ref[
                    unit * rows : (unit + 1) * rows, head * HEAD : (head + 1) * HEAD
                ]
            across = grads[unit].astype(f32).T
            delta[unit] = jnp.sum(across * turned_ref[unit], axis=0, keepdims=True)

    key_stretch = slots_ref[step]
    both[...] = jnp.zeros_like(both)
    for unit in range(2):

        @pl.when((key_stretch <= meta_ref[3 * unit + 1]) & (key_stretch >= meta_ref[3 * unit + 2]))
        def _():
            mask = mask_of(meta_ref, ends_ref, unit, rows, key_stretch)
            block = jnp.concatenate([near_ref[...], far_ref[...]], axis=0)
            key, value = block[:, :HEAD], block[:, HEAD:]
            query = q_ref[unit].reshape(HEADS * rows, HEAD)
            grad = grads[unit]
            probs = jnp.where(mask, jnp.exp(mm_nt(key, query) - lse_ref[unit]), 0.0)
            score_grad = (probs * (mm_nt(value, grad) - delta[unit])).astype(bf16)
            acc[unit] += mm_tn(key, score_grad)
            both[:, :HEAD] += mm(score_grad, query)
            both[:, HEAD:] += mm(probs.astype(bf16), grad)

    dnear_ref[...] = both[:rows].astype(bf16)
    dfar_ref[...] = both[rows:].astype(bf16)

    @pl.when(step == pl.num_programs(0) - 1)
    def _():
        gain = gain_ref[...]
        total = jnp.zeros_like(gain)
        for unit in range(2):
            mine = slice(unit * rows, (unit + 1) * rows)
            grad = acc[unit].T * HEAD**-0.5
            for head in range(HEADS):
                back = rotate(grad[head * rows : (head + 1) * rows], cos_ref[mine], -sin_ref[mine])
                raw = raw_ref[head, mine]
                scale = norm_scale(raw)
                total = total + jnp.sum(back * raw * scale, axis=0, keepdims=True)
                back = norm_back(raw, scale, gain * back)
                dq_ref[mine, head * HEAD : (head + 1) * HEAD] = back.astype(bf16)
        dgain_ref[...] = total


def whole_of(array):
    return pl.BlockSpec(array.shape, lambda *_: (0,) * len(array.shape))


def attend(meta, ends, slots, query, near, far):
    rows = query.shape[2]
    wide = HEADS * rows
    keys = pl.BlockSpec((None, None, rows, 2 * HEAD), lambda j, *_: (j // 2, j % 2, 0, 0))
    outs = [
        jax.ShapeDtypeStruct((2 * rows, HEADS * HEAD), bf16),
        jax.ShapeDtypeStruct((2, HEAD, wide), f32),
        jax.ShapeDtypeStruct((2, 1, wide), f32),
    ]
    return pl.pallas_call(
        functools.partial(attend_kernel, rows),
        grid_spec=pltpu.PrefetchScalarGridSpec(
            num_scalar_prefetch=3,
            grid=(slots.shape[0],),
            in_specs=[whole_of(query), keys, keys],
            out_specs=[whole_of(out) for out in outs],
            scratch_shapes=[
                pltpu.VMEM((2, 1, wide), f32),
                pltpu.VMEM((2, 1, wide), f32),
                pltpu.VMEM((2, HEAD, wide), f32),
            ],
        ),
        out_shape=outs,
        name="attend",
        cost_estimate=pl.CostEstimate(
            flops=4 * 2 * 9 * STRETCH * wide * HEAD,
            bytes_accessed=4 * near.size,
            transcendentals=2 * 9 * STRETCH * wide,
        ),
    )(meta, ends, slots, query, near, far)


def attend_back(meta, ends, slots, query, grad, lse, turned, raw, gain, cosine, sine, near, far):
    rows = query.shape[2]
    wide = HEADS * rows
    keys = pl.BlockSpec((None, None, rows, 2 * HEAD), lambda j, *_: (j // 2, j % 2, 0, 0))
    fixed = [query, grad, lse, turned, raw, gain, cosine, sine]
    outs = [jax.ShapeDtypeStruct(grad.shape, bf16), jax.ShapeDtypeStruct(gain.shape, f32)]
    return pl.pallas_call(
        functools.partial(attend_back_kernel, rows),
        grid_spec=pltpu.PrefetchScalarGridSpec(
            num_scalar_prefetch=3,
            grid=(slots.shape[0],),
            in_specs=[*[whole_of(array) for array in fixed], keys, keys],
            out_specs=[*[whole_of(out) for out in outs], keys, keys],
            scratch_shapes=[
                pltpu.VMEM((2, wide, HEAD), bf16),
                pltpu.VMEM((2, 1, wide), f32),
                pltpu.VMEM((2, HEAD, wide), f32),
                pltpu.VMEM((STRETCH, 2 * HEAD), f32),
            ],
        ),
        out_shape=[*outs, jax.ShapeDtypeStruct(near.shape, bf16), jax.ShapeDtypeStruct(near.shape, bf16)],
        name="attend_back",
        cost_estimate=pl.CostEstimate(
            flops=10 * 2 * 9 * STRETCH * wide * HEAD,
            bytes_accessed=8 * near.size,
            transcendentals=2 * 9 * STRETCH * wide,
        ),
    )(meta, ends, slots, *fixed, near, far)


def blocks_of(tops, low, member, members, ff):
    return [(((hi * 2 + low) * 2 + y) * members + member) * ff for hi in range(tops) for y in range(2)]

def pack_kernel(tops, members, ff, gate_ref, up_ref, out_ref):
    for which, ref in enumerate((gate_ref, up_ref)):
        value = ref[...]
        for low in range(2):
            for member in range(members):
                cuts = [value[:, at : at + ff] for at in blocks_of(tops, low, member, members, ff)]
                out_ref[low, member, which] = jnp.concatenate(cuts, axis=1)

def pack(gate, up, tops, members, ff):
    rows = gate.shape[0]
    return pl.pallas_call(functools.partial(pack_kernel, tops, members, ff),
        out_shape=jax.ShapeDtypeStruct((2, members, 2, rows, 2 * tops * ff), bf16), name="pack")(gate, up)

def unpack_kernel(tops, members, ff, low_ref, in_ref, gate_ref, up_ref):
    for which, ref in enumerate((gate_ref, up_ref)):
        pieces = [None] * (2 * tops * 2 * members)
        for low in range(2):
            for member in range(members):
                value = in_ref[member, low_ref[0] ^ low, which].astype(f32)
                for i, at in enumerate(blocks_of(tops, low, member, members, ff)):
                    pieces[at // ff] = value[:, i * ff : (i + 1) * ff]
        ref[...] = jnp.concatenate(pieces, axis=1)

def unpack(moved, low_bit, tops, members, ff):
    rows = moved.shape[3]
    shape = jax.ShapeDtypeStruct((rows, 4 * tops * members * ff), f32)
    return pl.pallas_call(functools.partial(unpack_kernel, tops, members, ff),
        in_specs=[pl.BlockSpec(memory_space=pltpu.SMEM), pl.BlockSpec(memory_space=pltpu.VMEM)],
        out_shape=[shape, shape], name="unpack")(low_bit[None], moved)

def merge_kernel(in_ref, gate_ref, up_ref):
    for which, ref in enumerate((gate_ref, up_ref)):
        for low in range(2):
            ref[low] = jnp.concatenate([in_ref[m, low, which] for m in range(in_ref.shape[0])], axis=0)

def merge(moved):
    members, _, _, rows, wide = moved.shape
    shape = jax.ShapeDtypeStruct((2, members * rows, wide), bf16)
    return pl.pallas_call(merge_kernel, out_shape=[shape, shape], name="merge")(moved)

def split_kernel(gate_ref, up_ref, out_ref):
    members, rows = out_ref.shape[1], out_ref.shape[3]
    for which, ref in enumerate((gate_ref, up_ref)):
        for low in range(2):
            value = ref[low]
            for m in range(members):
                out_ref[low, m, which] = value[m * rows : (m + 1) * rows]

def split(gate, up, members):
    _, tall, wide = gate.shape
    return pl.pallas_call(split_kernel,
        out_shape=jax.ShapeDtypeStruct((2, members, 2, tall // members, wide), bf16), name="split")(gate, up)


def per_device(
    inputs,
    cotangent,
    lengths,
    deal,
    w_query,
    w_key,
    w_value,
    w_out,
    w_gate,
    w_up,
    w_down,
    gain_attn_pre,
    gain_attn_post,
    gain_ffw_pre,
    gain_ffw_post,
    gain_query,
    gain_key,
):
    rows, width = inputs.shape[1], inputs.shape[2]
    groups, members = lax.axis_size("dp"), lax.axis_size("seq")
    devices = groups * members
    total_rows = rows * devices
    dp_id, seq_id = lax.axis_index("dp"), lax.axis_index("seq")
    half_bit, x_bit, y_bit, z_bit = seq_id % 2, seq_id // 2, dp_id % 2, dp_id // 2 % 2
    tops = groups // 4
    count = 2 * rows
    model_rows, out_rows, ff_rows = w_query.shape[0], w_out.shape[0], w_down.shape[0]
    ff_local = 2 * tops * ff_rows
    wide_q = HEADS * HEAD
    gain_sizes = [gain_attn_pre.shape[0]] * 4 + [gain_query.shape[0]] * 2
    gain_total = sum(gain_sizes)
    block_rows = (model_rows + 8) // 8 * 8

    def regroup(array):
        kept = lax.dynamic_index_in_dim(array, y_bit, 0, keepdims=False)
        sent = lax.dynamic_index_in_dim(array, 1 - y_bit, 0, keepdims=False)
        return jnp.concatenate([kept, xor(sent, "dp", 1)], axis=0)

    def ungroup(array):
        kept, sent = array[:rows], array[rows:]
        return flips(jnp.stack([kept, xor(sent, "dp", 1)]), [y_bit])

    rows_in = regroup(inputs).astype(f32)

    gain_line, at = jnp.zeros((1, 2 * HEAD), f32), 0
    for gain in (gain_attn_pre, gain_attn_post, gain_ffw_pre, gain_ffw_post, gain_query, gain_key):
        gain_line += jnp.pad(gain.astype(f32)[None, :], ((0, 0), (at, 2 * HEAD - at - gain.shape[0])))
        at += gain.shape[0]
    gain_line = gain_line.astype(bf16)
    kv_shard = jnp.concatenate([jnp.concatenate([w_key, w_value], axis=1), gain_line], axis=0)
    kv_blocks = gather_all(jnp.pad(kv_shard, ((0, block_rows - model_rows - 1), (0, 0))))
    kv_weight = kv_blocks.reshape(devices * block_rows, 2 * HEAD)
    q_shard = jnp.pad(w_query, ((0, block_rows - model_rows), (0, 0)))
    q_weight = lax.all_gather(q_shard, ALL, axis=0, tiled=True)
    out_weight = lax.all_gather(w_out, ALL, axis=0, tiled=True)
    labels = all_labels()
    natural = jnp.stack([(dp_id ^ d) * members + (seq_id ^ s) for d, s in labels]).astype(jnp.int32)

    def selection(order, size, block, padded):
        within = jnp.arange(padded, dtype=jnp.int32)
        source = jnp.where(within < block, order[:, None] * block + within, -1).reshape(-1)
        return (jnp.arange(size, dtype=jnp.int32)[:, None] == source[None, :]).astype(bf16)

    model_pick = selection(natural, width, model_rows, block_rows)
    query_pick = selection(jnp.arange(devices, dtype=jnp.int32), width, model_rows, block_rows)
    device_pick = selection(natural, devices, 1, 1)
    gain_blocks = kv_blocks[:, model_rows, :gain_total]
    gain_all = mm(device_pick, gain_blocks)
    full_gain, at = [], 0
    for size in gain_sizes:
        full_gain.append(gain_all[:, at : at + size].reshape(devices * size))
        at += size
    pre_attention, post_attention, pre_feed, post_feed, query_gain, key_gain = full_gain

    top_id = dp_id // 4

    def from_tops(piece):
        return [piece] + [xor(piece, "dp", 4 * k) for k in range(1, tops)]

    def both_sides(tall):
        return tall + [xor(part, "dp", 1) for part in tall]

    def swap_columns(packed):
        kept = lax.dynamic_index_in_dim(packed, z_bit, 0, keepdims=False)
        sent = lax.dynamic_index_in_dim(packed, 1 - z_bit, 0, keepdims=False)
        both = jnp.stack([kept, xor(sent, "dp", 2)], axis=1)
        return lax.all_to_all(both, "seq", split_axis=0, concat_axis=0, tiled=True)

    owners = [(top_id ^ k) * 2 + (y_bit ^ u) for u in range(2) for k in range(tops)]
    owners = jnp.stack(owners).astype(jnp.int32)
    sources = [((top_id ^ k) * 2 + (z_bit ^ v)) * 2 + (y_bit ^ u) for u in range(2) for k in range(tops) for v in range(2)]
    sources = jnp.stack(sources).astype(jnp.int32)
    down_tall = from_tops(w_down[None])
    halves = merge(swap_columns(pack(w_gate, w_up, tops, members, ff_rows)))

    seq_ends = jnp.cumsum(lax.dynamic_index_in_dim(lengths, y_bit, 0, keepdims=False))
    dealt = lax.dynamic_index_in_dim(deal, y_bit, 0, keepdims=False)
    unit_ids = jnp.stack([(dp_id ^ u) * members + seq_id for u in range(2)])
    stretches = dealt[unit_ids * rows // STRETCH]
    first_rows = stretches * STRETCH + unit_ids * rows % STRETCH
    my_rows = (first_rows[:, None] + jnp.arange(rows, dtype=jnp.int32)).reshape(count)
    starts = layout_start(seq_ends, my_rows)
    lows = starts.reshape(2, rows)[:, 0] // STRETCH
    meta = jnp.concatenate([jnp.stack([first_rows, stretches, lows], axis=1).reshape(-1), half_bit[None]])
    layers = groups // 2
    slot_ids = jnp.stack(
        [
            ((dp_id // 2 ^ z) * 2 + (y_bit ^ u)) * (members // 2) + (x_bit ^ x)
            for x in range(2)
            for z in range(layers)
            for u in range(2)
        ]
    )
    slots = dealt[slot_ids]
    positions = my_rows - starts
    valid = (my_rows < total_rows - STRETCH)[:, None]
    freqs = rope_base ** (-2.0 * jnp.arange(HEAD // 2, dtype=f32) / HEAD)
    angle = positions.astype(f32)[:, None] * freqs
    cosine, sine = jnp.cos(angle), jnp.sin(angle)

    scale_one = norm_scale(rows_in)
    normed_one = (rows_in * scale_one * pre_attention).astype(bf16)
    picked_one = mm(normed_one, model_pick).astype(bf16)
    key_raw, keys_mine = project_keys(picked_one, kv_weight, key_gain[None], cosine, sine)
    column = [keys_mine] + [xor(keys_mine, "dp", 2 * k) for k in range(1, layers)]
    halves, column = lax.optimization_barrier((halves, column))
    gate_tall, up_tall = [from_tops(half) for half in halves]
    across = [xor(part, "seq", 2) for part in column]
    across, down_pieces = lax.optimization_barrier((across, both_sides(down_tall)))
    column, across = jnp.stack(column), jnp.stack(across)
    near_keys = jnp.concatenate([column, across])
    far_keys = jnp.concatenate([xor(column, "seq", 1), xor(across, "seq", 1)])
    picked_query = mm(normed_one, query_pick).astype(bf16)
    query_raw, query_heads = project(picked_query, q_weight, query_gain[None], cosine, sine)
    q_natural = mm(query_pick, q_weight).astype(bf16)
    kv_natural = mm(model_pick, kv_weight).astype(bf16)
    query_heads, q_natural, kv_natural, gate_tall = lax.optimization_barrier(
        (query_heads, q_natural, kv_natural, gate_tall)
    )
    down_weight = place(down_pieces, owners).reshape(ff_local, width)
    gate_weight, up_weight = [place(both_sides(tall), sources).reshape(width, ff_local) for tall in (gate_tall, up_tall)]
    context_rows, turned, lse = attend(meta, seq_ends, slots, query_heads, near_keys, far_keys)
    attended = mm(context_rows, out_weight)
    scale_two = norm_scale(attended)
    hidden_res = rows_in + attended * scale_two * post_attention
    scale_three = norm_scale(hidden_res)
    normed_two = (hidden_res * scale_three * pre_feed).astype(bf16)

    normed_group = gather_group(normed_two)
    gate_raw = mm(normed_group, gate_weight)
    up_raw = mm(normed_group, up_weight)
    hidden_low = (jax.nn.gelu(gate_raw, approximate=True) * up_raw).astype(bf16)
    mixed = scatter_group(mm(hidden_low, down_weight).astype(bf16))
    scale_four = norm_scale(mixed)
    result = hidden_res + mixed * scale_four * post_feed
    output = ungroup(jnp.where(valid, result, 0.0).astype(bf16))

    upstream = jnp.where(valid, regroup(cotangent).astype(f32), 0.0)
    grad_post_feed = jnp.sum(upstream * mixed * scale_four, axis=0)
    mixed_grad = norm_back(mixed, scale_four, post_feed * upstream).astype(bf16)
    mixed_group = gather_group(mixed_grad)
    hidden_grad = mm_nt(mixed_group, down_weight)
    _, gelu_pull = jax.vjp(lambda g, u: jax.nn.gelu(g, approximate=True) * u, gate_raw, up_raw)
    gate_grad, up_grad = gelu_pull(hidden_grad)
    gate_grad, up_grad = gate_grad.astype(bf16), up_grad.astype(bf16)
    partial_grad = (mm_nt(gate_grad, gate_weight) + mm_nt(up_grad, up_weight)).astype(bf16)
    normed_two_grad = scatter_group(partial_grad)
    grad_pre_feed = jnp.sum(normed_two_grad * hidden_res * scale_three, axis=0)
    hidden_res_grad = upstream + norm_back(hidden_res, scale_three, pre_feed * normed_two_grad)

    def halve(total):
        kept = lax.dynamic_index_in_dim(total, y_bit, 2, keepdims=False)
        return kept, xor(lax.dynamic_index_in_dim(total, 1 - y_bit, 2, keepdims=False), "dp", 1)

    def by_top(kept, got):
        kept = add16(kept, got)
        return [lax.dynamic_index_in_dim(kept, top_id ^ k, 0, keepdims=False) for k in range(tops)]

    def send_tops(parts):
        return [part if k == 0 else xor(part, "dp", 4 * k) for k, part in enumerate(parts)]

    def total_of(parts):
        return functools.reduce(jnp.add, [part.astype(f32) for part in parts])

    def column_blocks(total):
        total = with_layout_constraint(total.astype(bf16), Layout((0, 1)))
        return total.reshape(tops, 2, 2, members * model_rows, ff_local)

    hidden_low, mixed_group, normed_group, gate_grad, up_grad, _ = lax.optimization_barrier(
        (hidden_low, mixed_group, normed_group, gate_grad, up_grad, partial_grad)
    )
    down_halves = halve(mm_tn(hidden_low, mixed_group).astype(bf16).reshape(tops, 1, 2, ff_rows, width))
    gate_halves = halve(column_blocks(mm_tn(normed_group, gate_grad)))
    up_halves = halve(column_blocks(mm_tn(normed_group, up_grad)))

    grad_post_attention = jnp.sum(hidden_res_grad * attended * scale_two, axis=0)
    attended_grad = norm_back(attended, scale_two, post_attention * hidden_res_grad).astype(bf16)
    out_total = mm_tn(context_rows, attended_grad).astype(bf16)
    attended_grad, out_total, gate_kept, up_kept = lax.optimization_barrier(
        (attended_grad, out_total, gate_halves[0], up_halves[0])
    )
    gate_halves, up_halves = (gate_kept, gate_halves[1]), (up_kept, up_halves[1])
    down_parts = send_tops(by_top(*down_halves))
    grad_out = lax.psum_scatter(out_total, ALL, scatter_dimension=0, tiled=True).astype(f32)
    context_grad = mm_nt(attended_grad, out_weight).astype(bf16)
    context_grad, gate_tops, down_parts = lax.optimization_barrier((context_grad, by_top(*gate_halves), down_parts))
    query_grad, grad_query_gain, near_part, far_part = attend_back(
        meta, seq_ends, slots, query_heads, context_grad, lse, turned, query_raw, query_gain[None], cosine, sine, near_keys, far_keys
    )
    gate_parts = send_tops(gate_tops)
    up_parts = send_tops(by_top(*up_halves))
    far_part = xor(far_part, "seq", 1)
    near_part = add16(near_part, far_part).reshape(2, layers, count, 2 * HEAD)
    near_part = add16(near_part[0], xor(near_part[1], "seq", 2))
    key_parts = [near_part[k] if k == 0 else xor(near_part[k], "dp", 2 * k) for k in range(layers)]
    query_low, _ = lax.optimization_barrier((query_grad, far_part))
    grad_query = mm_tn(picked_one, query_low).astype(bf16).reshape(devices, block_rows, wide_q)
    grad_query = scatter_all(grad_query)
    grad_query, grad_out, key_parts = lax.optimization_barrier((grad_query, grad_out, key_parts))
    key_grads = functools.reduce(jnp.add, [part.astype(f32) for part in key_parts])
    down_parts, gate_parts, up_parts, _ = lax.optimization_barrier((down_parts, gate_parts, up_parts, near_part))
    grad_down = total_of(down_parts)[0]
    both_grads = split(total_of(gate_parts).astype(bf16), total_of(up_parts).astype(bf16), members)
    grad_gate, grad_up = unpack(swap_columns(both_grads), z_bit, tops, members, ff_rows)
    value_grad = key_grads[:, HEAD:].astype(bf16)
    key_turned = rotate(key_grads[:, :HEAD], cosine, -sine)
    key_scale = norm_scale(key_raw)
    grad_key_gain = jnp.sum(key_turned * key_raw * key_scale, axis=0)
    key_grad = norm_back(key_raw, key_scale, key_gain * key_turned).astype(bf16)
    kv_grad = jnp.concatenate([key_grad, value_grad], axis=1)
    normed_one_grad = mm_nt(query_grad, q_natural) + mm_nt(kv_grad, kv_natural)
    grad_pre_attention = jnp.sum(normed_one_grad * rows_in * scale_one, axis=0)
    rows_grad = hidden_res_grad + norm_back(rows_in, scale_one, pre_attention * normed_one_grad)
    input_grad = ungroup(rows_grad.astype(bf16))
    grad_kv = mm_tn(picked_one, kv_grad).reshape(devices, block_rows, 2 * HEAD)
    gain_grads = [
        grad_pre_attention,
        grad_post_attention,
        grad_pre_feed,
        grad_post_feed,
        grad_query_gain,
        grad_key_gain,
    ]
    gain_grads = jnp.concatenate([g.reshape(devices, -1) for g in gain_grads], axis=1)
    gain_grads = mm_tn(device_pick, gain_grads.astype(bf16))
    gain_grads = jnp.pad(
        gain_grads[:, None, :], ((0, 0), (model_rows, block_rows - model_rows - 1), (0, 2 * HEAD - gain_total))
    )
    last = scatter_all((grad_kv + gain_grads).astype(bf16))
    gain_out, at = [], 0
    for size in gain_sizes:
        gain_out.append(last[model_rows, at : at + size])
        at += size
    return (
        output,
        input_grad,
        grad_query[:model_rows],
        last[:model_rows, :HEAD],
        last[:model_rows, HEAD:],
        grad_out,
        grad_gate,
        grad_up,
        grad_down,
        *gain_out,
    )


def solution(mesh):
    split = P(None, ALL, None)
    weight, gain = P(ALL, None), P(ALL)
    return jax.shard_map(
        per_device,
        mesh=mesh,
        in_specs=(split, split, P(), P(), *[weight] * 7, *[gain] * 6),
        out_specs=(split, split, *[weight] * 7, *[gain] * 6),
        check_vma=False,
    )
```

```python
import functools
import math

import jax
import jax.numpy as jnp
from jax import lax
from jax.experimental import pallas as pl
from jax.experimental.layout import Layout, with_layout_constraint
from jax.experimental.pallas import tpu as pltpu
from jax.sharding import PartitionSpec as P

HEADS = 4
HEAD = 256
MB = 2
STRETCH = 256

eps = 1e-06
rope_base = 1000000.0
masked_score = -1e30
bf16 = jnp.bfloat16
f32 = jnp.float32
ALL = ("dp", "seq")


def norm_scale(values):
    return lax.rsqrt(jnp.mean(values * values, axis=-1, keepdims=True) + eps)


def norm_back(values, scale, weighted):
    return scale * weighted - values * (scale * scale * scale) * jnp.mean(
        weighted * values, axis=-1, keepdims=True
    )


def rotate(values, cosine, sine):
    first, second = jnp.split(values, 2, axis=-1)
    return jnp.concatenate([first * cosine - second * sine, second * cosine + first * sine], axis=-1)


def layout_start(ends, row_ids):
    after = row_ids[:, None] >= ends[None, :]
    return jnp.max(jnp.where(after, ends[None, :], 0), axis=1)


def dot(left, right, dims):
    return lax.dot_general(left, right, (dims, ((), ())), preferred_element_type=f32)


def mm(left, right):
    return dot(left, right, ((1,), (0,)))


def mm_tn(left, right):
    return dot(left, right, ((0,), (0,)))


def mm_nt(left, right):
    return dot(left, right, ((1,), (1,)))


def xor(value, axis, mask):
    return lax.ppermute(value, axis, [(i, i ^ mask) for i in range(lax.axis_size(axis))])


def xor_both(value, dp_mask, seq_mask):
    members = lax.axis_size("seq")
    mask = dp_mask * members + seq_mask
    return lax.ppermute(value, ALL, [(i, i ^ mask) for i in range(lax.axis_size("dp") * members)])


def flips(value, bits):
    for axis, bit in enumerate(bits):
        halves = [lax.slice_in_dim(value, i, i + 1, axis=axis) for i in (1, 0)]
        value = jnp.where(bit == 1, lax.concatenate(halves, axis), value)
    return value


def add16(left, right):
    return (left.astype(f32) + right.astype(f32)).astype(bf16)


def together(*values):
    return lax.optimization_barrier(values)


def all_masks():
    rows = [(1 << bit, 0) for bit in range(1, 16) if 1 << bit < lax.axis_size("dp")]
    return rows + [(1, 0), (0, 2), (0, 1)]


def gather_step(value, dp_mask, seq_mask):
    return jnp.concatenate([value, xor_both(value, dp_mask, seq_mask)])


def all_labels():
    labels = [(0, 0)]
    for dp_mask, seq_mask in all_masks():
        labels = labels + [(d ^ dp_mask, s ^ seq_mask) for d, s in labels]
    return labels


def scatter_step(total, dp_mask, seq_mask):
    half = total.shape[0] // 2
    got = xor_both(total[half:], dp_mask, seq_mask)
    total = total[:half].astype(f32) + got.astype(f32)
    return total if half == 1 else total.astype(bf16)


def scatter_rest(total):
    for masks in list(reversed(all_masks()))[1:]:
        total = scatter_step(total, *masks)
    return total[0]


def gather_group(rows):
    half = rows.shape[0] // 2
    across, along = xor(rows, "seq", 2), xor(rows, "dp", 2)
    corner = [xor(across[:half], "dp", 2), xor(along[half:], "seq", 2)]
    near = [rows, across, along, *corner]
    far = [rows, jnp.concatenate([across, along]), jnp.concatenate(corner)]
    return jnp.concatenate(near + [xor(part, "seq", 1) for part in far], axis=0)


def scatter_group(total):
    parts = total.reshape(2, -1, total.shape[1])
    near = add16(parts[0], xor(parts[1], "seq", 1))
    mine, across, along, corner = jnp.split(near, 4)
    half = mine.shape[0] // 2
    low, high = xor(corner[:half], "dp", 2), xor(corner[half:], "seq", 2)
    across = jnp.concatenate([add16(across[:half], low), across[half:]])
    along = jnp.concatenate([along[:half], add16(along[half:], high)])
    return mine.astype(f32) + xor(across, "seq", 2).astype(f32) + xor(along, "dp", 2).astype(f32)


def place_kernel(sizes, target_ref, *refs):
    pieces, out = refs[: len(sizes)], refs[len(sizes)]
    buffer, arrived, left = refs[len(sizes) + 1 :]
    ins, outs, block = [], [], 0
    for piece, size in zip(pieces, sizes):
        for index in range(size):
            ins.append(pltpu.make_async_copy(piece.at[index], buffer.at[block], arrived.at[block]))
            outs.append(pltpu.make_async_copy(buffer.at[block], out.at[target_ref[block]], left.at[block]))
            ins[-1].start()
            block += 1
    for copy_in, copy_out in zip(ins, outs):
        copy_in.wait()
        copy_out.start()
    for copy_out in outs:
        copy_out.wait()


def place(pieces, targets):
    sizes = [piece.shape[0] for piece in pieces]
    shape = (sum(sizes), *pieces[0].shape[1:])
    anywhere = pl.BlockSpec(memory_space=pl.ANY)
    return pl.pallas_call(
        functools.partial(place_kernel, sizes),
        grid_spec=pltpu.PrefetchScalarGridSpec(
            num_scalar_prefetch=1,
            grid=(1,),
            in_specs=[anywhere] * len(pieces),
            out_specs=anywhere,
            scratch_shapes=[
                pltpu.VMEM(shape, pieces[0].dtype),
                pltpu.SemaphoreType.DMA((shape[0],)),
                pltpu.SemaphoreType.DMA((shape[0],)),
            ],
        ),
        out_shape=jax.ShapeDtypeStruct(shape, pieces[0].dtype),
        name="place",
        cost_estimate=pl.CostEstimate(flops=0, bytes_accessed=4 * math.prod(shape), transcendentals=0),
    )(targets, *pieces)


def project_kernel(scale, picked_ref, weight_ref, gain_ref, cos_ref, sin_ref, raw_ref, out_ref):
    raw = mm(picked_ref[...], weight_ref[...])
    raw_ref[0] = raw
    turned = rotate(raw * norm_scale(raw) * gain_ref[...], cos_ref[...], sin_ref[...]).astype(bf16)
    out_ref[...] = (turned * scale).astype(bf16).reshape(out_ref.shape)


def project(picked, weight, gain, cosine, sine):
    count, deep = picked.shape
    rows = count // 2
    same = lambda h: (0, 0)
    return pl.pallas_call(
        functools.partial(project_kernel, HEAD**-0.5),
        grid=(HEADS,),
        in_specs=[
            pl.BlockSpec((count, deep), same),
            pl.BlockSpec((deep, HEAD), lambda h: (0, h)),
            pl.BlockSpec((1, HEAD), same),
            pl.BlockSpec((count, HEAD // 2), same),
            pl.BlockSpec((count, HEAD // 2), same),
        ],
        out_specs=[
            pl.BlockSpec((1, count, HEAD), lambda h: (h, 0, 0)),
            pl.BlockSpec((2, 1, rows, HEAD), lambda h: (0, h, 0, 0)),
        ],
        out_shape=[
            jax.ShapeDtypeStruct((HEADS, count, HEAD), f32),
            jax.ShapeDtypeStruct((2, HEADS, rows, HEAD), bf16),
        ],
        name="project",
        cost_estimate=pl.CostEstimate(
            flops=2 * count * deep * HEADS * HEAD, bytes_accessed=2 * deep * HEADS * HEAD, transcendentals=0
        ),
    )(picked, weight, gain, cosine, sine)


def project_keys_kernel(picked_ref, weight_ref, gain_ref, cos_ref, sin_ref, raw_ref, out_ref):
    both = mm(picked_ref[...], weight_ref[...])
    raw = both[:, :HEAD]
    raw_ref[...] = raw
    turned = rotate(raw * norm_scale(raw) * gain_ref[...], cos_ref[...], sin_ref[...])
    both = jnp.concatenate([turned, both[:, HEAD:]], axis=1).astype(bf16)
    out_ref[...] = both.reshape(out_ref.shape)


def project_keys(picked, weight, gain, cosine, sine):
    count, deep = picked.shape
    return pl.pallas_call(
        project_keys_kernel,
        grid=(1,),
        in_specs=[
            whole_of(picked),
            pl.BlockSpec((deep, 2 * HEAD), lambda i: (0, HEADS // 2)),
            whole_of(gain),
            whole_of(cosine),
            whole_of(sine),
        ],
        out_specs=[
            pl.BlockSpec((count, HEAD), lambda i: (0, 0)),
            pl.BlockSpec((2, count // 2, 2 * HEAD), lambda i: (0, 0, 0)),
        ],
        out_shape=[
            jax.ShapeDtypeStruct((count, HEAD), f32),
            jax.ShapeDtypeStruct((2, count // 2, 2 * HEAD), bf16),
        ],
        name="project_keys",
        cost_estimate=pl.CostEstimate(
            flops=4 * count * deep * HEAD, bytes_accessed=4 * deep * HEAD, transcendentals=0
        ),
    )(picked, weight, gain, cosine, sine)


def mask_of(meta_ref, ends_ref, unit, rows, key_stretch):
    lanes = lax.broadcasted_iota(jnp.int32, (1, HEADS * rows), 1)
    ids = meta_ref[3 * unit] + lanes % rows
    start = jnp.zeros_like(ids)
    for index in range(ends_ref.shape[0]):
        end = ends_ref[index]
        start = jnp.where(ids >= end, end, start)
    place_in = lax.broadcasted_iota(jnp.int32, (STRETCH, 1), 0)
    near = meta_ref[6] * rows
    place_in = jnp.where(place_in < rows, place_in + near, place_in - near)
    key = key_stretch * STRETCH + place_in
    return (key <= ids) & (key >= start)


def attend_kernel(
    rows, meta_ref, ends_ref, slots_ref, q_ref, near_ref, far_ref, c_ref, turned_ref, lse_ref, top, total, acc
):
    step = pl.program_id(0)

    @pl.when(step == 0)
    def _():
        top[...] = jnp.full_like(top, masked_score)
        total[...] = jnp.zeros_like(total)
        acc[...] = jnp.zeros_like(acc)

    key_stretch = slots_ref[step]
    for unit in range(2):

        @pl.when((key_stretch <= meta_ref[3 * unit + 1]) & (key_stretch >= meta_ref[3 * unit + 2]))
        def _():
            mask = mask_of(meta_ref, ends_ref, unit, rows, key_stretch)
            block = jnp.concatenate([near_ref[...], far_ref[...]], axis=0)
            query = q_ref[unit].reshape(HEADS * rows, HEAD)
            scores = jnp.where(mask, mm_nt(block[:, :HEAD], query), masked_score)
            old = top[unit]
            new = jnp.maximum(old, jnp.max(scores, axis=0, keepdims=True))
            keep = jnp.exp(old - new)
            terms = jnp.exp(scores - new)
            top[unit] = new
            total[unit] = total[unit] * keep + jnp.sum(terms, axis=0, keepdims=True)
            acc[unit] = acc[unit] * keep + mm_tn(block[:, HEAD:], terms.astype(bf16))

    @pl.when(step == pl.num_programs(0) - 1)
    def _():
        for unit in range(2):
            out = acc[unit] * (1.0 / total[unit])
            turned_ref[unit] = out
            lse_ref[unit] = top[unit] + jnp.log(total[unit])
            out = out.T.astype(bf16)
            for head in range(HEADS):
                c_ref[unit * rows : (unit + 1) * rows, head * HEAD : (head + 1) * HEAD] = out[
                    head * rows : (head + 1) * rows
                ]


def attend_back_kernel(
    rows,
    meta_ref,
    ends_ref,
    slots_ref,
    q_ref,
    dc_ref,
    lse_ref,
    turned_ref,
    raw_ref,
    gain_ref,
    cos_ref,
    sin_ref,
    near_ref,
    far_ref,
    dq_ref,
    dgain_ref,
    dnear_ref,
    dfar_ref,
    grads,
    delta,
    acc,
    both,
):
    step = pl.program_id(0)

    @pl.when(step == 0)
    def _():
        acc[...] = jnp.zeros_like(acc)
        for unit in range(2):
            for head in range(HEADS):
                grads[unit, head * rows : (head + 1) * rows] = dc_ref[
                    unit * rows : (unit + 1) * rows, head * HEAD : (head + 1) * HEAD
                ]
            across = grads[unit].astype(f32).T
            delta[unit] = jnp.sum(across * turned_ref[unit], axis=0, keepdims=True)

    key_stretch = slots_ref[step]
    both[...] = jnp.zeros_like(both)
    for unit in range(2):

        @pl.when((key_stretch <= meta_ref[3 * unit + 1]) & (key_stretch >= meta_ref[3 * unit + 2]))
        def _():
            mask = mask_of(meta_ref, ends_ref, unit, rows, key_stretch)
            block = jnp.concatenate([near_ref[...], far_ref[...]], axis=0)
            key, value = block[:, :HEAD], block[:, HEAD:]
            query = q_ref[unit].reshape(HEADS * rows, HEAD)
            grad = grads[unit]
            probs = jnp.where(mask, jnp.exp(mm_nt(key, query) - lse_ref[unit]), 0.0)
            score_grad = (probs * (mm_nt(value, grad) - delta[unit])).astype(bf16)
            acc[unit] += mm_tn(key, score_grad)
            both[:, :HEAD] += mm(score_grad, query)
            both[:, HEAD:] += mm(probs.astype(bf16), grad)

    dnear_ref[...] = both[:rows].astype(bf16)
    dfar_ref[...] = both[rows:].astype(bf16)

    @pl.when(step == pl.num_programs(0) - 1)
    def _():
        gain = gain_ref[...]
        total = jnp.zeros_like(gain)
        for unit in range(2):
            mine = slice(unit * rows, (unit + 1) * rows)
            grad = acc[unit].T * HEAD**-0.5
            for head in range(HEADS):
                back = rotate(grad[head * rows : (head + 1) * rows], cos_ref[mine], -sin_ref[mine])
                raw = raw_ref[head, mine]
                scale = norm_scale(raw)
                total = total + jnp.sum(back * raw * scale, axis=0, keepdims=True)
                back = norm_back(raw, scale, gain * back)
                dq_ref[mine, head * HEAD : (head + 1) * HEAD] = back.astype(bf16)
        dgain_ref[...] = total


def whole_of(array):
    return pl.BlockSpec(array.shape, lambda *_: (0,) * len(array.shape))


def attend(meta, ends, slots, query, near, far):
    rows = query.shape[2]
    wide = HEADS * rows
    keys = pl.BlockSpec((None, None, rows, 2 * HEAD), lambda j, *_: (j // 2, j % 2, 0, 0))
    outs = [
        jax.ShapeDtypeStruct((2 * rows, HEADS * HEAD), bf16),
        jax.ShapeDtypeStruct((2, HEAD, wide), f32),
        jax.ShapeDtypeStruct((2, 1, wide), f32),
    ]
    return pl.pallas_call(
        functools.partial(attend_kernel, rows),
        grid_spec=pltpu.PrefetchScalarGridSpec(
            num_scalar_prefetch=3,
            grid=(slots.shape[0],),
            in_specs=[whole_of(query), keys, keys],
            out_specs=[whole_of(out) for out in outs],
            scratch_shapes=[
                pltpu.VMEM((2, 1, wide), f32),
                pltpu.VMEM((2, 1, wide), f32),
                pltpu.VMEM((2, HEAD, wide), f32),
            ],
        ),
        out_shape=outs,
        name="attend",
        cost_estimate=pl.CostEstimate(
            flops=4 * 2 * 9 * STRETCH * wide * HEAD,
            bytes_accessed=4 * near.size,
            transcendentals=2 * 9 * STRETCH * wide,
        ),
    )(meta, ends, slots, query, near, far)


def attend_back(meta, ends, slots, query, grad, lse, turned, raw, gain, cosine, sine, near, far):
    rows = query.shape[2]
    wide = HEADS * rows
    keys = pl.BlockSpec((None, None, rows, 2 * HEAD), lambda j, *_: (j // 2, j % 2, 0, 0))
    fixed = [query, grad, lse, turned, raw, gain, cosine, sine]
    outs = [jax.ShapeDtypeStruct(grad.shape, bf16), jax.ShapeDtypeStruct(gain.shape, f32)]
    return pl.pallas_call(
        functools.partial(attend_back_kernel, rows),
        grid_spec=pltpu.PrefetchScalarGridSpec(
            num_scalar_prefetch=3,
            grid=(slots.shape[0],),
            in_specs=[*[whole_of(array) for array in fixed], keys, keys],
            out_specs=[*[whole_of(out) for out in outs], keys, keys],
            scratch_shapes=[
                pltpu.VMEM((2, wide, HEAD), bf16),
                pltpu.VMEM((2, 1, wide), f32),
                pltpu.VMEM((2, HEAD, wide), f32),
                pltpu.VMEM((STRETCH, 2 * HEAD), f32),
            ],
        ),
        out_shape=[*outs, jax.ShapeDtypeStruct(near.shape, bf16), jax.ShapeDtypeStruct(near.shape, bf16)],
        name="attend_back",
        cost_estimate=pl.CostEstimate(
            flops=10 * 2 * 9 * STRETCH * wide * HEAD,
            bytes_accessed=8 * near.size,
            transcendentals=2 * 9 * STRETCH * wide,
        ),
    )(meta, ends, slots, *fixed, near, far)


def blocks_of(tops, low, member, members, ff):
    return [(((hi * 2 + low) * 2 + y) * members + member) * ff for hi in range(tops) for y in range(2)]

def pack_kernel(tops, members, ff, gate_ref, up_ref, out_ref):
    for which, ref in enumerate((gate_ref, up_ref)):
        value = ref[...]
        for low in range(2):
            for member in range(members):
                cuts = [value[:, at : at + ff] for at in blocks_of(tops, low, member, members, ff)]
                out_ref[low, member, which] = jnp.concatenate(cuts, axis=1)

def pack(gate, up, tops, members, ff):
    rows = gate.shape[0]
    return pl.pallas_call(functools.partial(pack_kernel, tops, members, ff),
        out_shape=jax.ShapeDtypeStruct((2, members, 2, rows, 2 * tops * ff), bf16), name="pack")(gate, up)

def unpack_kernel(tops, members, ff, low_ref, in_ref, gate_ref, up_ref):
    for which, ref in enumerate((gate_ref, up_ref)):
        pieces = [None] * (2 * tops * 2 * members)
        for low in range(2):
            for member in range(members):
                value = in_ref[member, low_ref[0] ^ low, which].astype(f32)
                for i, at in enumerate(blocks_of(tops, low, member, members, ff)):
                    pieces[at // ff] = value[:, i * ff : (i + 1) * ff]
        ref[...] = jnp.concatenate(pieces, axis=1)

def unpack(moved, low_bit, tops, members, ff):
    rows = moved.shape[3]
    shape = jax.ShapeDtypeStruct((rows, 4 * tops * members * ff), f32)
    return pl.pallas_call(functools.partial(unpack_kernel, tops, members, ff),
        in_specs=[pl.BlockSpec(memory_space=pltpu.SMEM), pl.BlockSpec(memory_space=pltpu.VMEM)],
        out_shape=[shape, shape], name="unpack")(low_bit[None], moved)

def merge_kernel(in_ref, gate_ref, up_ref):
    for which, ref in enumerate((gate_ref, up_ref)):
        for low in range(2):
            ref[low] = jnp.concatenate([in_ref[m, low, which] for m in range(in_ref.shape[0])], axis=0)

def merge(moved):
    members, _, _, rows, wide = moved.shape
    shape = jax.ShapeDtypeStruct((2, members * rows, wide), bf16)
    return pl.pallas_call(merge_kernel, out_shape=[shape, shape], name="merge")(moved)

def split_kernel(gate_ref, up_ref, out_ref):
    members, rows = out_ref.shape[1], out_ref.shape[3]
    for which, ref in enumerate((gate_ref, up_ref)):
        for low in range(2):
            value = ref[low]
            for m in range(members):
                out_ref[low, m, which] = value[m * rows : (m + 1) * rows]

def split(gate, up, members):
    _, tall, wide = gate.shape
    return pl.pallas_call(split_kernel,
        out_shape=jax.ShapeDtypeStruct((2, members, 2, tall // members, wide), bf16), name="split")(gate, up)


def per_device(
    inputs,
    cotangent,
    lengths,
    deal,
    w_query,
    w_key,
    w_value,
    w_out,
    w_gate,
    w_up,
    w_down,
    gain_attn_pre,
    gain_attn_post,
    gain_ffw_pre,
    gain_ffw_post,
    gain_query,
    gain_key,
):
    rows, width = inputs.shape[1], inputs.shape[2]
    groups, members = lax.axis_size("dp"), lax.axis_size("seq")
    devices = groups * members
    total_rows = rows * devices
    dp_id, seq_id = lax.axis_index("dp"), lax.axis_index("seq")
    half_bit, x_bit, y_bit, z_bit = seq_id % 2, seq_id // 2, dp_id % 2, dp_id // 2 % 2
    tops = groups // 4
    count = 2 * rows
    model_rows, out_rows, ff_rows = w_query.shape[0], w_out.shape[0], w_down.shape[0]
    ff_local = 2 * tops * ff_rows
    wide_q = HEADS * HEAD
    gain_sizes = [gain_attn_pre.shape[0]] * 4 + [gain_query.shape[0]] * 2
    gain_total = sum(gain_sizes)
    block_rows = (model_rows + 8) // 8 * 8

    def regroup(array):
        kept = lax.dynamic_index_in_dim(array, y_bit, 0, keepdims=False)
        sent = lax.dynamic_index_in_dim(array, 1 - y_bit, 0, keepdims=False)
        return jnp.concatenate([kept, xor(sent, "dp", 1)], axis=0)

    def ungroup(array):
        kept, sent = array[:rows], array[rows:]
        return flips(jnp.stack([kept, xor(sent, "dp", 1)]), [y_bit])

    rows_in = regroup(inputs).astype(f32)

    def column_exchange(packed):
        kept = lax.dynamic_index_in_dim(packed, z_bit, 0, keepdims=False)
        sent = lax.dynamic_index_in_dim(packed, 1 - z_bit, 0, keepdims=False)
        return jnp.stack([kept, xor(sent, "dp", 2)], axis=1)

    def swap_members(parts):
        return lax.all_to_all(parts, "seq", split_axis=0, concat_axis=0, tiled=True)

    gain_line, at = jnp.zeros((1, wide_q + 2 * HEAD), f32), 0
    for gain in (gain_attn_pre, gain_attn_post, gain_ffw_pre, gain_ffw_post, gain_query, gain_key):
        gain_line += jnp.pad(gain.astype(f32)[None, :], ((0, 0), (at, gain_line.shape[1] - at - gain.shape[0])))
        at += gain.shape[0]
    shard = jnp.concatenate([w_query, w_key, w_value], axis=1)
    shard = jnp.concatenate([shard, gain_line.astype(bf16)], axis=0)
    blocks = jnp.pad(shard, ((0, block_rows - model_rows - 1), (0, 0)))[None]
    packed = pack(w_gate, w_up, tops, members, ff_rows)
    *row_masks, y_mask, x_mask, core_mask = all_masks()
    for masks in row_masks:
        blocks = gather_step(blocks, *masks)
    blocks, packed, down_piece = together(blocks, packed, w_down[None])
    column_parts = column_exchange(packed)
    blocks = gather_step(gather_step(blocks, *y_mask), *x_mask)
    blocks, column_parts = together(blocks, column_parts)
    blocks = gather_step(blocks, *core_mask)
    blocks, late_out = together(blocks, w_out)
    qkv_weight = blocks.reshape(devices * block_rows, wide_q + 2 * HEAD)
    out_weight = lax.all_gather(late_out, ALL, axis=0, tiled=True)
    labels = all_labels()
    natural = jnp.stack([(dp_id ^ d) * members + (seq_id ^ s) for d, s in labels]).astype(jnp.int32)

    def selection(order, size, block, padded):
        within = jnp.arange(padded, dtype=jnp.int32)
        source = jnp.where(within < block, order[:, None] * block + within, -1).reshape(-1)
        return (jnp.arange(size, dtype=jnp.int32)[:, None] == source[None, :]).astype(bf16)

    model_pick = selection(natural, width, model_rows, block_rows)
    device_pick = selection(natural, devices, 1, 1)
    gain_blocks = blocks[:, model_rows, :gain_total]
    gain_all = mm(device_pick, gain_blocks)
    full_gain, at = [], 0
    for size in gain_sizes:
        full_gain.append(gain_all[:, at : at + size].reshape(devices * size))
        at += size
    pre_attention, post_attention, pre_feed, post_feed, query_gain, key_gain = full_gain

    top_id = dp_id // 4

    def from_tops(piece):
        return [piece] + [xor(piece, "dp", 4 * k) for k in range(1, tops)]

    def both_sides(tall):
        return tall + [xor(part, "dp", 1) for part in tall]

    owners = [(top_id ^ k) * 2 + (y_bit ^ u) for u in range(2) for k in range(tops)]
    owners = jnp.stack(owners).astype(jnp.int32)
    sources = [((top_id ^ k) * 2 + (z_bit ^ v)) * 2 + (y_bit ^ u) for u in range(2) for k in range(tops) for v in range(2)]
    sources = jnp.stack(sources).astype(jnp.int32)
    down_tall = from_tops(down_piece)
    halves = swap_members(column_parts)

    seq_ends = jnp.cumsum(lax.dynamic_index_in_dim(lengths, y_bit, 0, keepdims=False))
    dealt = lax.dynamic_index_in_dim(deal, y_bit, 0, keepdims=False)
    unit_ids = jnp.stack([(dp_id ^ u) * members + seq_id for u in range(2)])
    stretches = dealt[unit_ids * rows // STRETCH]
    first_rows = stretches * STRETCH + unit_ids * rows % STRETCH
    my_rows = (first_rows[:, None] + jnp.arange(rows, dtype=jnp.int32)).reshape(count)
    starts = layout_start(seq_ends, my_rows)
    lows = starts.reshape(2, rows)[:, 0] // STRETCH
    meta = jnp.concatenate([jnp.stack([first_rows, stretches, lows], axis=1).reshape(-1), half_bit[None]])
    layers = groups // 2
    slot_ids = jnp.stack(
        [
            ((dp_id // 2 ^ z) * 2 + (y_bit ^ u)) * (members // 2) + (x_bit ^ x)
            for x in range(2)
            for z in range(layers)
            for u in range(2)
        ]
    )
    slots = dealt[slot_ids]
    positions = my_rows - starts
    valid = (my_rows < total_rows - STRETCH)[:, None]
    freqs = rope_base ** (-2.0 * jnp.arange(HEAD // 2, dtype=f32) / HEAD)
    angle = positions.astype(f32)[:, None] * freqs
    cosine, sine = jnp.cos(angle), jnp.sin(angle)

    scale_one = norm_scale(rows_in)
    normed_one = (rows_in * scale_one * pre_attention).astype(bf16)
    picked_one = mm(normed_one, model_pick).astype(bf16)
    key_raw, keys_mine = project_keys(picked_one, qkv_weight, key_gain[None], cosine, sine)
    key_raw, down_tall, halves = together(key_raw, down_tall, halves)
    halves = merge(halves)
    column = [keys_mine] + [xor(keys_mine, "dp", 2 * k) for k in range(1, layers)]
    halves, others = together(halves, column[1:])
    column = [column[0], *others]
    gate_tall, up_tall = [from_tops(half) for half in halves]
    across = [xor(part, "seq", 2) for part in column]
    across, down_pieces = lax.optimization_barrier((across, both_sides(down_tall)))
    column, across = jnp.stack(column), jnp.stack(across)
    near_keys = jnp.concatenate([column, across])
    far_keys = jnp.concatenate([xor(column, "seq", 1), xor(across, "seq", 1)])
    query_raw, query_heads = project(picked_one, qkv_weight, query_gain[None], cosine, sine)
    natural_weight = mm(model_pick, qkv_weight).astype(bf16)
    query_heads, natural_weight, gate_tall = lax.optimization_barrier((query_heads, natural_weight, gate_tall))
    gate_pieces = both_sides(gate_tall)
    context_rows, turned, lse = attend(meta, seq_ends, slots, query_heads, near_keys, far_keys)
    context_rows, gate_pieces, up_tall = together(context_rows, gate_pieces, up_tall)
    up_pieces = both_sides(up_tall)
    down_weight = place(down_pieces, owners).reshape(ff_local, width)
    gate_weight, up_weight = [place(pieces, sources).reshape(width, ff_local) for pieces in (gate_pieces, up_pieces)]
    attended = mm(context_rows, out_weight)
    scale_two = norm_scale(attended)
    hidden_res = rows_in + attended * scale_two * post_attention
    scale_three = norm_scale(hidden_res)
    normed_two = (hidden_res * scale_three * pre_feed).astype(bf16)

    normed_group = gather_group(normed_two)
    gate_raw = mm(normed_group, gate_weight)
    up_raw = mm(normed_group, up_weight)
    hidden_low = (jax.nn.gelu(gate_raw, approximate=True) * up_raw).astype(bf16)
    mixed = scatter_group(mm(hidden_low, down_weight).astype(bf16))
    scale_four = norm_scale(mixed)
    result = hidden_res + mixed * scale_four * post_feed
    output = ungroup(jnp.where(valid, result, 0.0).astype(bf16))

    upstream = jnp.where(valid, regroup(cotangent).astype(f32), 0.0)
    grad_post_feed = jnp.sum(upstream * mixed * scale_four, axis=0)
    mixed_grad = norm_back(mixed, scale_four, post_feed * upstream).astype(bf16)
    mixed_group = gather_group(mixed_grad)
    hidden_grad = mm_nt(mixed_group, down_weight)
    _, gelu_pull = jax.vjp(lambda g, u: jax.nn.gelu(g, approximate=True) * u, gate_raw, up_raw)
    gate_grad, up_grad = gelu_pull(hidden_grad)
    gate_grad, up_grad = gate_grad.astype(bf16), up_grad.astype(bf16)
    partial_grad = (mm_nt(gate_grad, gate_weight) + mm_nt(up_grad, up_weight)).astype(bf16)
    hidden_low, mixed_group, normed_group, gate_grad, up_grad, partial_grad = together(
        hidden_low, mixed_group, normed_group, gate_grad, up_grad, partial_grad
    )
    normed_two_grad = scatter_group(partial_grad)
    grad_pre_feed = jnp.sum(normed_two_grad * hidden_res * scale_three, axis=0)
    hidden_res_grad = upstream + norm_back(hidden_res, scale_three, pre_feed * normed_two_grad)

    def halve(total):
        kept = lax.dynamic_index_in_dim(total, y_bit, 2, keepdims=False)
        return kept, xor(lax.dynamic_index_in_dim(total, 1 - y_bit, 2, keepdims=False), "dp", 1)

    def by_top(kept, got):
        kept = add16(kept, got)
        return [lax.dynamic_index_in_dim(kept, top_id ^ k, 0, keepdims=False) for k in range(tops)]

    def send_tops(parts):
        return [part if k == 0 else xor(part, "dp", 4 * k) for k, part in enumerate(parts)]

    def total_of(parts):
        return functools.reduce(jnp.add, [part.astype(f32) for part in parts])

    def column_blocks(total):
        total = with_layout_constraint(total.astype(bf16), Layout((0, 1)))
        return total.reshape(tops, 2, 2, members * model_rows, ff_local)

    down_halves = halve(mm_tn(hidden_low, mixed_group).astype(bf16).reshape(tops, 1, 2, ff_rows, width))
    down_kept, gate_grad = together(down_halves[0], gate_grad)
    gate_halves = halve(column_blocks(mm_tn(normed_group, gate_grad)))
    gate_kept, down_got, up_grad = together(gate_halves[0], down_halves[1], up_grad)
    up_halves = halve(column_blocks(mm_tn(normed_group, up_grad)))
    down_halves, gate_halves = (down_kept, down_got), (gate_kept, gate_halves[1])

    grad_post_attention = jnp.sum(hidden_res_grad * attended * scale_two, axis=0)
    attended_grad = norm_back(attended, scale_two, post_attention * hidden_res_grad).astype(bf16)
    out_total = mm_tn(context_rows, attended_grad).astype(bf16)
    attended_grad, out_total, gate_kept, up_kept = lax.optimization_barrier(
        (attended_grad, out_total, gate_halves[0], up_halves[0])
    )
    gate_halves, up_halves = (gate_kept, gate_halves[1]), (up_kept, up_halves[1])
    down_parts = send_tops(by_top(*down_halves))
    grad_out = lax.psum_scatter(out_total, ALL, scatter_dimension=0, tiled=True).astype(f32)
    context_grad = mm_nt(attended_grad, out_weight).astype(bf16)
    query_grad, grad_query_gain, near_part, far_part = attend_back(
        meta, seq_ends, slots, query_heads, context_grad, lse, turned, query_raw, query_gain[None], cosine, sine, near_keys, far_keys
    )
    far_part, near_part, gate_halves, up_halves, down_parts = lax.optimization_barrier(
        (far_part, near_part, gate_halves, up_halves, down_parts)
    )
    gate_parts, up_parts = [send_tops(by_top(*half)) for half in (gate_halves, up_halves)]
    far_part = xor(far_part, "seq", 1)
    query_low, far_part = together(query_grad, far_part)
    near_part = add16(near_part, far_part).reshape(2, layers, count, 2 * HEAD)
    near_part = add16(near_part[0], xor(near_part[1], "seq", 2))
    grad_query = mm_tn(picked_one, query_low).astype(bf16).reshape(devices, block_rows, wide_q)
    grad_query, near_part = together(scatter_step(grad_query, *core_mask), near_part)
    grad_query = scatter_rest(grad_query)
    key_parts = [near_part[k] if k == 0 else xor(near_part[k], "dp", 2 * k) for k in range(layers)]
    key_grads = functools.reduce(jnp.add, [part.astype(f32) for part in key_parts])
    value_grad = key_grads[:, HEAD:].astype(bf16)
    key_turned = rotate(key_grads[:, :HEAD], cosine, -sine)
    key_scale = norm_scale(key_raw)
    grad_key_gain = jnp.sum(key_turned * key_raw * key_scale, axis=0)
    key_grad = norm_back(key_raw, key_scale, key_gain * key_turned).astype(bf16)
    kv_grad = jnp.concatenate([key_grad, value_grad], axis=1)
    down_parts, gate_parts, up_parts, kv_grad = together(down_parts, gate_parts, up_parts, kv_grad)
    grad_down = total_of(down_parts)[0]
    both_grads = split(total_of(gate_parts).astype(bf16), total_of(up_parts).astype(bf16), members)
    grad_gate, grad_up = unpack(swap_members(column_exchange(both_grads)), z_bit, tops, members, ff_rows)
    normed_one_grad = mm_nt(query_grad, natural_weight[:, :wide_q]) + mm_nt(kv_grad, natural_weight[:, wide_q:])
    grad_pre_attention = jnp.sum(normed_one_grad * rows_in * scale_one, axis=0)
    rows_grad = hidden_res_grad + norm_back(rows_in, scale_one, pre_attention * normed_one_grad)
    input_grad = ungroup(rows_grad.astype(bf16))
    grad_kv = mm_tn(picked_one, kv_grad).reshape(devices, block_rows, 2 * HEAD)
    gain_grads = [
        grad_pre_attention,
        grad_post_attention,
        grad_pre_feed,
        grad_post_feed,
        grad_query_gain,
        grad_key_gain,
    ]
    gain_grads = jnp.concatenate([g.reshape(devices, -1) for g in gain_grads], axis=1)
    gain_grads = mm_tn(device_pick, gain_grads.astype(bf16))
    gain_grads = jnp.pad(
        gain_grads[:, None, :], ((0, 0), (model_rows, block_rows - model_rows - 1), (0, 2 * HEAD - gain_total))
    )
    last = scatter_rest(scatter_step((grad_kv + gain_grads).astype(bf16), *core_mask))
    gain_out, at = [], 0
    for size in gain_sizes:
        gain_out.append(last[model_rows, at : at + size])
        at += size
    return (
        output,
        input_grad,
        grad_query[:model_rows],
        last[:model_rows, :HEAD],
        last[:model_rows, HEAD:],
        grad_out,
        grad_gate,
        grad_up,
        grad_down,
        *gain_out,
    )


def solution(mesh):
    split = P(None, ALL, None)
    weight, gain = P(ALL, None), P(ALL)
    return jax.shard_map(
        per_device,
        mesh=mesh,
        in_specs=(split, split, P(), P(), *[weight] * 7, *[gain] * 6),
        out_specs=(split, split, *[weight] * 7, *[gain] * 6),
        check_vma=False,
    )
```

```python
import functools
import math

import jax
import jax.numpy as jnp
from jax import lax
from jax.experimental import pallas as pl
from jax.experimental.layout import Layout, with_layout_constraint
from jax.experimental.pallas import tpu as pltpu
from jax.sharding import PartitionSpec as P

HEADS = 4
HEAD = 256
MB = 2
STRETCH = 256

eps = 1e-06
rope_base = 1000000.0
masked_score = -1e30
bf16 = jnp.bfloat16
f32 = jnp.float32
ALL = ("dp", "seq")


def norm_scale(values):
    return lax.rsqrt(jnp.mean(values * values, axis=-1, keepdims=True) + eps)


def norm_back(values, scale, weighted):
    return scale * weighted - values * (scale * scale * scale) * jnp.mean(
        weighted * values, axis=-1, keepdims=True
    )


def rotate(values, cosine, sine):
    first, second = jnp.split(values, 2, axis=-1)
    return jnp.concatenate([first * cosine - second * sine, second * cosine + first * sine], axis=-1)


def layout_start(ends, row_ids):
    after = row_ids[:, None] >= ends[None, :]
    return jnp.max(jnp.where(after, ends[None, :], 0), axis=1)


def dot(left, right, dims):
    return lax.dot_general(left, right, (dims, ((), ())), preferred_element_type=f32)


def mm(left, right):
    return dot(left, right, ((1,), (0,)))


def mm_tn(left, right):
    return dot(left, right, ((0,), (0,)))


def mm_nt(left, right):
    return dot(left, right, ((1,), (1,)))


def xor(value, axis, mask):
    return lax.ppermute(value, axis, [(i, i ^ mask) for i in range(lax.axis_size(axis))])


def xor_both(value, dp_mask, seq_mask):
    members = lax.axis_size("seq")
    mask = dp_mask * members + seq_mask
    return lax.ppermute(value, ALL, [(i, i ^ mask) for i in range(lax.axis_size("dp") * members)])


def flips(value, bits):
    for axis, bit in enumerate(bits):
        halves = [lax.slice_in_dim(value, i, i + 1, axis=axis) for i in (1, 0)]
        value = jnp.where(bit == 1, lax.concatenate(halves, axis), value)
    return value


def add16(left, right):
    return (left.astype(f32) + right.astype(f32)).astype(bf16)


def together(*values):
    return lax.optimization_barrier(values)


def all_masks():
    rows = [(1 << bit, 0) for bit in range(1, 16) if 1 << bit < lax.axis_size("dp")]
    return rows + [(1, 0), (0, 2), (0, 1)]


def gather_step(value, dp_mask, seq_mask):
    return jnp.concatenate([value, xor_both(value, dp_mask, seq_mask)])


def all_labels():
    labels = [(0, 0)]
    for dp_mask, seq_mask in all_masks():
        labels = labels + [(d ^ dp_mask, s ^ seq_mask) for d, s in labels]
    return labels


def scatter_step(total, dp_mask, seq_mask):
    half = total.shape[0] // 2
    got = xor_both(total[half:], dp_mask, seq_mask)
    total = total[:half].astype(f32) + got.astype(f32)
    return total if half == 1 else total.astype(bf16)


def scatter_rest(total):
    for masks in list(reversed(all_masks()))[1:]:
        total = scatter_step(total, *masks)
    return total[0]


def gather_group(rows):
    half = rows.shape[0] // 2
    across, along = xor(rows, "seq", 2), xor(rows, "dp", 2)
    corner = [xor(across[:half], "dp", 2), xor(along[half:], "seq", 2)]
    near = [rows, across, along, *corner]
    far = [rows, jnp.concatenate([across, along]), jnp.concatenate(corner)]
    return jnp.concatenate(near + [xor(part, "seq", 1) for part in far], axis=0)


def scatter_group(total):
    parts = total.reshape(2, -1, total.shape[1])
    near = add16(parts[0], xor(parts[1], "seq", 1))
    mine, across, along, corner = jnp.split(near, 4)
    half = mine.shape[0] // 2
    low, high = xor(corner[:half], "dp", 2), xor(corner[half:], "seq", 2)
    across = jnp.concatenate([add16(across[:half], low), across[half:]])
    along = jnp.concatenate([along[:half], add16(along[half:], high)])
    return mine.astype(f32) + xor(across, "seq", 2).astype(f32) + xor(along, "dp", 2).astype(f32)


def place_kernel(sizes, target_ref, *refs):
    pieces, out = refs[: len(sizes)], refs[len(sizes)]
    buffer, arrived, left = refs[len(sizes) + 1 :]
    ins, outs, block = [], [], 0
    for piece, size in zip(pieces, sizes):
        for index in range(size):
            ins.append(pltpu.make_async_copy(piece.at[index], buffer.at[block], arrived.at[block]))
            outs.append(pltpu.make_async_copy(buffer.at[block], out.at[target_ref[block]], left.at[block]))
            ins[-1].start()
            block += 1
    for copy_in, copy_out in zip(ins, outs):
        copy_in.wait()
        copy_out.start()
    for copy_out in outs:
        copy_out.wait()


def place(pieces, targets):
    sizes = [piece.shape[0] for piece in pieces]
    shape = (sum(sizes), *pieces[0].shape[1:])
    anywhere = pl.BlockSpec(memory_space=pl.ANY)
    return pl.pallas_call(
        functools.partial(place_kernel, sizes),
        grid_spec=pltpu.PrefetchScalarGridSpec(
            num_scalar_prefetch=1,
            grid=(1,),
            in_specs=[anywhere] * len(pieces),
            out_specs=anywhere,
            scratch_shapes=[
                pltpu.VMEM(shape, pieces[0].dtype),
                pltpu.SemaphoreType.DMA((shape[0],)),
                pltpu.SemaphoreType.DMA((shape[0],)),
            ],
        ),
        out_shape=jax.ShapeDtypeStruct(shape, pieces[0].dtype),
        name="place",
        cost_estimate=pl.CostEstimate(flops=0, bytes_accessed=4 * math.prod(shape), transcendentals=0),
    )(targets, *pieces)


def project_kernel(scale, picked_ref, weight_ref, gain_ref, cos_ref, sin_ref, raw_ref, out_ref):
    raw = mm(picked_ref[...], weight_ref[...])
    raw_ref[0] = raw
    turned = rotate(raw * norm_scale(raw) * gain_ref[...], cos_ref[...], sin_ref[...]).astype(bf16)
    out_ref[...] = (turned * scale).astype(bf16).reshape(out_ref.shape)


def project(picked, weight, gain, cosine, sine):
    count, deep = picked.shape
    rows = count // 2
    same = lambda h: (0, 0)
    return pl.pallas_call(
        functools.partial(project_kernel, HEAD**-0.5),
        grid=(HEADS,),
        in_specs=[
            pl.BlockSpec((count, deep), same),
            pl.BlockSpec((deep, HEAD), lambda h: (0, h)),
            pl.BlockSpec((1, HEAD), same),
            pl.BlockSpec((count, HEAD // 2), same),
            pl.BlockSpec((count, HEAD // 2), same),
        ],
        out_specs=[
            pl.BlockSpec((1, count, HEAD), lambda h: (h, 0, 0)),
            pl.BlockSpec((2, 1, rows, HEAD), lambda h: (0, h, 0, 0)),
        ],
        out_shape=[
            jax.ShapeDtypeStruct((HEADS, count, HEAD), f32),
            jax.ShapeDtypeStruct((2, HEADS, rows, HEAD), bf16),
        ],
        name="project",
        cost_estimate=pl.CostEstimate(
            flops=2 * count * deep * HEADS * HEAD, bytes_accessed=2 * deep * HEADS * HEAD, transcendentals=0
        ),
    )(picked, weight, gain, cosine, sine)


def project_keys_kernel(picked_ref, weight_ref, gain_ref, cos_ref, sin_ref, raw_ref, out_ref):
    both = mm(picked_ref[...], weight_ref[...])
    raw = both[:, :HEAD]
    raw_ref[...] = raw
    turned = rotate(raw * norm_scale(raw) * gain_ref[...], cos_ref[...], sin_ref[...])
    both = jnp.concatenate([turned, both[:, HEAD:]], axis=1).astype(bf16)
    out_ref[...] = both.reshape(out_ref.shape)


def project_keys(picked, weight, gain, cosine, sine):
    count, deep = picked.shape
    return pl.pallas_call(
        project_keys_kernel,
        grid=(1,),
        in_specs=[
            whole_of(picked),
            pl.BlockSpec((deep, 2 * HEAD), lambda i: (0, HEADS // 2)),
            whole_of(gain),
            whole_of(cosine),
            whole_of(sine),
        ],
        out_specs=[
            pl.BlockSpec((count, HEAD), lambda i: (0, 0)),
            pl.BlockSpec((2, count // 2, 2 * HEAD), lambda i: (0, 0, 0)),
        ],
        out_shape=[
            jax.ShapeDtypeStruct((count, HEAD), f32),
            jax.ShapeDtypeStruct((2, count // 2, 2 * HEAD), bf16),
        ],
        name="project_keys",
        cost_estimate=pl.CostEstimate(
            flops=4 * count * deep * HEAD, bytes_accessed=4 * deep * HEAD, transcendentals=0
        ),
    )(picked, weight, gain, cosine, sine)


def mask_of(meta_ref, ends_ref, unit, rows, key_stretch):
    lanes = lax.broadcasted_iota(jnp.int32, (1, HEADS * rows), 1)
    ids = meta_ref[3 * unit] + lanes % rows
    start = jnp.zeros_like(ids)
    for index in range(ends_ref.shape[0]):
        end = ends_ref[index]
        start = jnp.where(ids >= end, end, start)
    place_in = lax.broadcasted_iota(jnp.int32, (STRETCH, 1), 0)
    near = meta_ref[6] * rows
    place_in = jnp.where(place_in < rows, place_in + near, place_in - near)
    key = key_stretch * STRETCH + place_in
    return (key <= ids) & (key >= start)


def attend_kernel(
    rows, meta_ref, ends_ref, slots_ref, q_ref, near_ref, far_ref, c_ref, turned_ref, lse_ref, top, total, acc
):
    step = pl.program_id(0)

    @pl.when(step == 0)
    def _():
        top[...] = jnp.full_like(top, masked_score)
        total[...] = jnp.zeros_like(total)
        acc[...] = jnp.zeros_like(acc)

    key_stretch = slots_ref[step]
    for unit in range(2):

        @pl.when((key_stretch <= meta_ref[3 * unit + 1]) & (key_stretch >= meta_ref[3 * unit + 2]))
        def _():
            mask = mask_of(meta_ref, ends_ref, unit, rows, key_stretch)
            block = jnp.concatenate([near_ref[...], far_ref[...]], axis=0)
            query = q_ref[unit].reshape(HEADS * rows, HEAD)
            scores = jnp.where(mask, mm_nt(block[:, :HEAD], query), masked_score)
            old = top[unit]
            new = jnp.maximum(old, jnp.max(scores, axis=0, keepdims=True))
            keep = jnp.exp(old - new)
            terms = jnp.exp(scores - new)
            top[unit] = new
            total[unit] = total[unit] * keep + jnp.sum(terms, axis=0, keepdims=True)
            acc[unit] = acc[unit] * keep + mm_tn(block[:, HEAD:], terms.astype(bf16))

    @pl.when(step == pl.num_programs(0) - 1)
    def _():
        for unit in range(2):
            out = acc[unit] * (1.0 / total[unit])
            turned_ref[unit] = out
            lse_ref[unit] = top[unit] + jnp.log(total[unit])
            out = out.T.astype(bf16)
            for head in range(HEADS):
                c_ref[unit * rows : (unit + 1) * rows, head * HEAD : (head + 1) * HEAD] = out[
                    head * rows : (head + 1) * rows
                ]


def attend_back_kernel(
    rows,
    meta_ref,
    ends_ref,
    slots_ref,
    q_ref,
    dc_ref,
    lse_ref,
    turned_ref,
    raw_ref,
    gain_ref,
    cos_ref,
    sin_ref,
    near_ref,
    far_ref,
    dq_ref,
    dgain_ref,
    dnear_ref,
    dfar_ref,
    grads,
    delta,
    acc,
    both,
):
    step = pl.program_id(0)

    @pl.when(step == 0)
    def _():
        acc[...] = jnp.zeros_like(acc)
        for unit in range(2):
            for head in range(HEADS):
                grads[unit, head * rows : (head + 1) * rows] = dc_ref[
                    unit * rows : (unit + 1) * rows, head * HEAD : (head + 1) * HEAD
                ]
            across = grads[unit].astype(f32).T
            delta[unit] = jnp.sum(across * turned_ref[unit], axis=0, keepdims=True)

    key_stretch = slots_ref[step]
    both[...] = jnp.zeros_like(both)
    for unit in range(2):

        @pl.when((key_stretch <= meta_ref[3 * unit + 1]) & (key_stretch >= meta_ref[3 * unit + 2]))
        def _():
            mask = mask_of(meta_ref, ends_ref, unit, rows, key_stretch)
            block = jnp.concatenate([near_ref[...], far_ref[...]], axis=0)
            key, value = block[:, :HEAD], block[:, HEAD:]
            query = q_ref[unit].reshape(HEADS * rows, HEAD)
            grad = grads[unit]
            probs = jnp.where(mask, jnp.exp(mm_nt(key, query) - lse_ref[unit]), 0.0)
            score_grad = (probs * (mm_nt(value, grad) - delta[unit])).astype(bf16)
            acc[unit] += mm_tn(key, score_grad)
            both[:, :HEAD] += mm(score_grad, query)
            both[:, HEAD:] += mm(probs.astype(bf16), grad)

    dnear_ref[...] = both[:rows].astype(bf16)
    dfar_ref[...] = both[rows:].astype(bf16)

    @pl.when(step == pl.num_programs(0) - 1)
    def _():
        gain = gain_ref[...]
        total = jnp.zeros_like(gain)
        for unit in range(2):
            mine = slice(unit * rows, (unit + 1) * rows)
            grad = acc[unit].T * HEAD**-0.5
            for head in range(HEADS):
                back = rotate(grad[head * rows : (head + 1) * rows], cos_ref[mine], -sin_ref[mine])
                raw = raw_ref[head, mine]
                scale = norm_scale(raw)
                total = total + jnp.sum(back * raw * scale, axis=0, keepdims=True)
                back = norm_back(raw, scale, gain * back)
                dq_ref[mine, head * HEAD : (head + 1) * HEAD] = back.astype(bf16)
        dgain_ref[...] = total


def whole_of(array):
    return pl.BlockSpec(array.shape, lambda *_: (0,) * len(array.shape))


def attend(meta, ends, slots, query, near, far):
    rows = query.shape[2]
    wide = HEADS * rows
    keys = pl.BlockSpec((None, None, rows, 2 * HEAD), lambda j, *_: (j // 2, j % 2, 0, 0))
    outs = [
        jax.ShapeDtypeStruct((2 * rows, HEADS * HEAD), bf16),
        jax.ShapeDtypeStruct((2, HEAD, wide), f32),
        jax.ShapeDtypeStruct((2, 1, wide), f32),
    ]
    return pl.pallas_call(
        functools.partial(attend_kernel, rows),
        grid_spec=pltpu.PrefetchScalarGridSpec(
            num_scalar_prefetch=3,
            grid=(slots.shape[0],),
            in_specs=[whole_of(query), keys, keys],
            out_specs=[whole_of(out) for out in outs],
            scratch_shapes=[
                pltpu.VMEM((2, 1, wide), f32),
                pltpu.VMEM((2, 1, wide), f32),
                pltpu.VMEM((2, HEAD, wide), f32),
            ],
        ),
        out_shape=outs,
        name="attend",
        cost_estimate=pl.CostEstimate(
            flops=4 * 2 * 9 * STRETCH * wide * HEAD,
            bytes_accessed=4 * near.size,
            transcendentals=2 * 9 * STRETCH * wide,
        ),
    )(meta, ends, slots, query, near, far)


def attend_back(meta, ends, slots, query, grad, lse, turned, raw, gain, cosine, sine, near, far):
    rows = query.shape[2]
    wide = HEADS * rows
    keys = pl.BlockSpec((None, None, rows, 2 * HEAD), lambda j, *_: (j // 2, j % 2, 0, 0))
    fixed = [query, grad, lse, turned, raw, gain, cosine, sine]
    outs = [jax.ShapeDtypeStruct(grad.shape, bf16), jax.ShapeDtypeStruct(gain.shape, f32)]
    return pl.pallas_call(
        functools.partial(attend_back_kernel, rows),
        grid_spec=pltpu.PrefetchScalarGridSpec(
            num_scalar_prefetch=3,
            grid=(slots.shape[0],),
            in_specs=[*[whole_of(array) for array in fixed], keys, keys],
            out_specs=[*[whole_of(out) for out in outs], keys, keys],
            scratch_shapes=[
                pltpu.VMEM((2, wide, HEAD), bf16),
                pltpu.VMEM((2, 1, wide), f32),
                pltpu.VMEM((2, HEAD, wide), f32),
                pltpu.VMEM((STRETCH, 2 * HEAD), f32),
            ],
        ),
        out_shape=[*outs, jax.ShapeDtypeStruct(near.shape, bf16), jax.ShapeDtypeStruct(near.shape, bf16)],
        name="attend_back",
        cost_estimate=pl.CostEstimate(
            flops=10 * 2 * 9 * STRETCH * wide * HEAD,
            bytes_accessed=8 * near.size,
            transcendentals=2 * 9 * STRETCH * wide,
        ),
    )(meta, ends, slots, *fixed, near, far)


def blocks_of(tops, low, member, members, ff):
    return [(((hi * 2 + low) * 2 + y) * members + member) * ff for hi in range(tops) for y in range(2)]

def pack_kernel(tops, members, ff, gate_ref, up_ref, out_ref):
    for which, ref in enumerate((gate_ref, up_ref)):
        value = ref[...]
        for low in range(2):
            for member in range(members):
                cuts = [value[:, at : at + ff] for at in blocks_of(tops, low, member, members, ff)]
                out_ref[low, member, which] = jnp.concatenate(cuts, axis=1)

def pack(gate, up, tops, members, ff):
    rows = gate.shape[0]
    return pl.pallas_call(functools.partial(pack_kernel, tops, members, ff),
        out_shape=jax.ShapeDtypeStruct((2, members, 2, rows, 2 * tops * ff), bf16), name="pack")(gate, up)

def unpack_kernel(tops, members, ff, low_ref, in_ref, gate_ref, up_ref):
    for which, ref in enumerate((gate_ref, up_ref)):
        pieces = [None] * (2 * tops * 2 * members)
        for low in range(2):
            for member in range(members):
                value = in_ref[member, low_ref[0] ^ low, which].astype(f32)
                for i, at in enumerate(blocks_of(tops, low, member, members, ff)):
                    pieces[at // ff] = value[:, i * ff : (i + 1) * ff]
        ref[...] = jnp.concatenate(pieces, axis=1)

def unpack(moved, low_bit, tops, members, ff):
    rows = moved.shape[3]
    shape = jax.ShapeDtypeStruct((rows, 4 * tops * members * ff), f32)
    return pl.pallas_call(functools.partial(unpack_kernel, tops, members, ff),
        in_specs=[pl.BlockSpec(memory_space=pltpu.SMEM), pl.BlockSpec(memory_space=pltpu.VMEM)],
        out_shape=[shape, shape], name="unpack")(low_bit[None], moved)

def merge_kernel(in_ref, gate_ref, up_ref):
    for which, ref in enumerate((gate_ref, up_ref)):
        for low in range(2):
            ref[low] = jnp.concatenate([in_ref[m, low, which] for m in range(in_ref.shape[0])], axis=0)

def merge(moved):
    members, _, _, rows, wide = moved.shape
    shape = jax.ShapeDtypeStruct((2, members * rows, wide), bf16)
    return pl.pallas_call(merge_kernel, out_shape=[shape, shape], name="merge")(moved)

def split_kernel(gate_ref, up_ref, out_ref):
    members, rows = out_ref.shape[1], out_ref.shape[3]
    for which, ref in enumerate((gate_ref, up_ref)):
        for low in range(2):
            value = ref[low]
            for m in range(members):
                out_ref[low, m, which] = value[m * rows : (m + 1) * rows]

def split(gate, up, members):
    _, tall, wide = gate.shape
    return pl.pallas_call(split_kernel,
        out_shape=jax.ShapeDtypeStruct((2, members, 2, tall // members, wide), bf16), name="split")(gate, up)


def per_device(
    inputs,
    cotangent,
    lengths,
    deal,
    w_query,
    w_key,
    w_value,
    w_out,
    w_gate,
    w_up,
    w_down,
    gain_attn_pre,
    gain_attn_post,
    gain_ffw_pre,
    gain_ffw_post,
    gain_query,
    gain_key,
):
    rows, width = inputs.shape[1], inputs.shape[2]
    groups, members = lax.axis_size("dp"), lax.axis_size("seq")
    devices = groups * members
    total_rows = rows * devices
    dp_id, seq_id = lax.axis_index("dp"), lax.axis_index("seq")
    half_bit, x_bit, y_bit, z_bit = seq_id % 2, seq_id // 2, dp_id % 2, dp_id // 2 % 2
    tops = groups // 4
    count = 2 * rows
    model_rows, out_rows, ff_rows = w_query.shape[0], w_out.shape[0], w_down.shape[0]
    ff_local = 2 * tops * ff_rows
    wide_q = HEADS * HEAD
    gain_sizes = [gain_attn_pre.shape[0]] * 4 + [gain_query.shape[0]] * 2
    gain_total = sum(gain_sizes)
    block_rows = (model_rows + 8) // 8 * 8

    def regroup(array):
        kept = lax.dynamic_index_in_dim(array, y_bit, 0, keepdims=False)
        sent = lax.dynamic_index_in_dim(array, 1 - y_bit, 0, keepdims=False)
        return jnp.concatenate([kept, xor(sent, "dp", 1)], axis=0)

    def ungroup(array):
        kept, sent = array[:rows], array[rows:]
        return flips(jnp.stack([kept, xor(sent, "dp", 1)]), [y_bit])


    def column_exchange(packed):
        kept = lax.dynamic_index_in_dim(packed, z_bit, 0, keepdims=False)
        sent = lax.dynamic_index_in_dim(packed, 1 - z_bit, 0, keepdims=False)
        return jnp.stack([kept, xor(sent, "dp", 2)], axis=1)

    def swap_members(parts):
        return lax.all_to_all(parts, "seq", split_axis=0, concat_axis=0, tiled=True)

    gain_line, at = jnp.zeros((1, wide_q + 2 * HEAD), f32), 0
    for gain in (gain_attn_pre, gain_attn_post, gain_ffw_pre, gain_ffw_post, gain_query, gain_key):
        gain_line += jnp.pad(gain.astype(f32)[None, :], ((0, 0), (at, gain_line.shape[1] - at - gain.shape[0])))
        at += gain.shape[0]
    shard = jnp.concatenate([w_query, w_key, w_value], axis=1)
    shard = jnp.concatenate([shard, gain_line.astype(bf16)], axis=0)
    blocks = jnp.pad(shard, ((0, block_rows - model_rows - 1), (0, 0)))[None]
    packed = pack(w_gate, w_up, tops, members, ff_rows)
    *row_masks, y_mask, x_mask, core_mask = all_masks()
    for masks in row_masks:
        blocks = gather_step(blocks, *masks)
    blocks, packed, down_piece, rows_low = together(blocks, packed, w_down[None], regroup(inputs))
    rows_in = rows_low.astype(f32)
    column_parts = column_exchange(packed)
    blocks = gather_step(gather_step(blocks, *y_mask), *x_mask)
    blocks, column_parts = together(blocks, column_parts)
    blocks = gather_step(blocks, *core_mask)
    blocks, late_out = together(blocks, w_out)
    qkv_weight = blocks.reshape(devices * block_rows, wide_q + 2 * HEAD)
    out_weight = lax.all_gather(late_out, ALL, axis=0, tiled=True)
    labels = all_labels()
    natural = jnp.stack([(dp_id ^ d) * members + (seq_id ^ s) for d, s in labels]).astype(jnp.int32)

    def selection(order, size, block, padded):
        within = jnp.arange(padded, dtype=jnp.int32)
        source = jnp.where(within < block, order[:, None] * block + within, -1).reshape(-1)
        return (jnp.arange(size, dtype=jnp.int32)[:, None] == source[None, :]).astype(bf16)

    model_pick = selection(natural, width, model_rows, block_rows)
    device_pick = selection(natural, devices, 1, 1)
    gain_blocks = blocks[:, model_rows, :gain_total]
    gain_all = mm(device_pick, gain_blocks)
    full_gain, at = [], 0
    for size in gain_sizes:
        full_gain.append(gain_all[:, at : at + size].reshape(devices * size))
        at += size
    pre_attention, post_attention, pre_feed, post_feed, query_gain, key_gain = full_gain

    top_id = dp_id // 4

    def from_tops(piece):
        return [piece] + [xor(piece, "dp", 4 * k) for k in range(1, tops)]

    def both_sides(tall):
        return tall + [xor(part, "dp", 1) for part in tall]

    owners = [(top_id ^ k) * 2 + (y_bit ^ u) for u in range(2) for k in range(tops)]
    owners = jnp.stack(owners).astype(jnp.int32)
    sources = [((top_id ^ k) * 2 + (z_bit ^ v)) * 2 + (y_bit ^ u) for u in range(2) for k in range(tops) for v in range(2)]
    sources = jnp.stack(sources).astype(jnp.int32)
    down_tall = from_tops(down_piece)
    halves = swap_members(column_parts)

    seq_ends = jnp.cumsum(lax.dynamic_index_in_dim(lengths, y_bit, 0, keepdims=False))
    dealt = lax.dynamic_index_in_dim(deal, y_bit, 0, keepdims=False)
    unit_ids = jnp.stack([(dp_id ^ u) * members + seq_id for u in range(2)])
    stretches = dealt[unit_ids * rows // STRETCH]
    first_rows = stretches * STRETCH + unit_ids * rows % STRETCH
    my_rows = (first_rows[:, None] + jnp.arange(rows, dtype=jnp.int32)).reshape(count)
    starts = layout_start(seq_ends, my_rows)
    lows = starts.reshape(2, rows)[:, 0] // STRETCH
    meta = jnp.concatenate([jnp.stack([first_rows, stretches, lows], axis=1).reshape(-1), half_bit[None]])
    layers = groups // 2
    slot_ids = jnp.stack(
        [
            ((dp_id // 2 ^ z) * 2 + (y_bit ^ u)) * (members // 2) + (x_bit ^ x)
            for x in range(2)
            for z in range(layers)
            for u in range(2)
        ]
    )
    slots = dealt[slot_ids]
    positions = my_rows - starts
    valid = (my_rows < total_rows - STRETCH)[:, None]
    freqs = rope_base ** (-2.0 * jnp.arange(HEAD // 2, dtype=f32) / HEAD)
    angle = positions.astype(f32)[:, None] * freqs
    cosine, sine = jnp.cos(angle), jnp.sin(angle)

    scale_one = norm_scale(rows_in)
    normed_one = (rows_in * scale_one * pre_attention).astype(bf16)
    picked_one = mm(normed_one, model_pick).astype(bf16)
    key_raw, keys_mine = project_keys(picked_one, qkv_weight, key_gain[None], cosine, sine)
    key_raw, down_tall, halves = together(key_raw, down_tall, halves)
    halves = merge(halves)
    column = [keys_mine] + [xor(keys_mine, "dp", 2 * k) for k in range(1, layers)]
    halves, others = together(halves, column[1:])
    column = [column[0], *others]
    gate_tall, up_half = together(from_tops(halves[0]), halves[1])
    up_tall = from_tops(up_half)
    across = [xor(part, "seq", 2) for part in column]
    across, down_pieces = lax.optimization_barrier((across, both_sides(down_tall)))
    column, across = jnp.stack(column), jnp.stack(across)
    near_keys = jnp.concatenate([column, across])
    far_keys = jnp.concatenate([xor(column, "seq", 1), xor(across, "seq", 1)])
    query_raw, query_heads = project(picked_one, qkv_weight, query_gain[None], cosine, sine)
    query_heads, gate_tall = together(query_heads, gate_tall)
    gate_pieces = both_sides(gate_tall)
    context_rows, turned, lse = attend(meta, seq_ends, slots, query_heads, near_keys, far_keys)
    context_rows, gate_pieces, up_tall = together(context_rows, gate_pieces, up_tall)
    up_pieces = both_sides(up_tall)
    down_weight = place(down_pieces, owners).reshape(ff_local, width)
    gate_weight, up_weight = [place(pieces, sources).reshape(width, ff_local) for pieces in (gate_pieces, up_pieces)]
    attended = mm(context_rows, out_weight)
    scale_two = norm_scale(attended)
    hidden_res = rows_in + attended * scale_two * post_attention
    scale_three = norm_scale(hidden_res)
    normed_two = (hidden_res * scale_three * pre_feed).astype(bf16)

    normed_group = gather_group(normed_two)
    gate_raw = mm(normed_group, gate_weight)
    up_raw = mm(normed_group, up_weight)
    hidden_low = (jax.nn.gelu(gate_raw, approximate=True) * up_raw).astype(bf16)
    mixed = scatter_group(mm(hidden_low, down_weight).astype(bf16))
    natural_weight, mixed = together(mm(model_pick, qkv_weight).astype(bf16), mixed)
    scale_four = norm_scale(mixed)
    result = hidden_res + mixed * scale_four * post_feed
    output = ungroup(jnp.where(valid, result, 0.0).astype(bf16))

    upstream = jnp.where(valid, regroup(cotangent).astype(f32), 0.0)
    grad_post_feed = jnp.sum(upstream * mixed * scale_four, axis=0)
    mixed_grad = norm_back(mixed, scale_four, post_feed * upstream).astype(bf16)
    mixed_group = gather_group(mixed_grad)
    hidden_grad = mm_nt(mixed_group, down_weight)
    _, gelu_pull = jax.vjp(lambda g, u: jax.nn.gelu(g, approximate=True) * u, gate_raw, up_raw)
    gate_grad, up_grad = gelu_pull(hidden_grad)
    gate_grad, up_grad = gate_grad.astype(bf16), up_grad.astype(bf16)
    partial_grad = (mm_nt(gate_grad, gate_weight) + mm_nt(up_grad, up_weight)).astype(bf16)
    hidden_low, mixed_group, normed_group, gate_grad, up_grad, partial_grad = together(
        hidden_low, mixed_group, normed_group, gate_grad, up_grad, partial_grad
    )
    normed_two_grad = scatter_group(partial_grad)
    grad_pre_feed = jnp.sum(normed_two_grad * hidden_res * scale_three, axis=0)
    hidden_res_grad = upstream + norm_back(hidden_res, scale_three, pre_feed * normed_two_grad)

    def halve(total):
        kept = lax.dynamic_index_in_dim(total, y_bit, 2, keepdims=False)
        return kept, xor(lax.dynamic_index_in_dim(total, 1 - y_bit, 2, keepdims=False), "dp", 1)

    def by_top(kept, got):
        kept = add16(kept, got)
        return [lax.dynamic_index_in_dim(kept, top_id ^ k, 0, keepdims=False) for k in range(tops)]

    def send_tops(parts):
        return [part if k == 0 else xor(part, "dp", 4 * k) for k, part in enumerate(parts)]

    def total_of(parts):
        return functools.reduce(jnp.add, [part.astype(f32) for part in parts])

    def column_blocks(total):
        total = with_layout_constraint(total.astype(bf16), Layout((0, 1)))
        return total.reshape(tops, 2, 2, members * model_rows, ff_local)

    down_halves = halve(mm_tn(hidden_low, mixed_group).astype(bf16).reshape(tops, 1, 2, ff_rows, width))
    down_kept, gate_grad = together(down_halves[0], gate_grad)
    gate_halves = halve(column_blocks(mm_tn(normed_group, gate_grad)))
    gate_kept, down_got, up_grad = together(gate_halves[0], down_halves[1], up_grad)
    up_halves = halve(column_blocks(mm_tn(normed_group, up_grad)))
    down_halves, gate_halves = (down_kept, down_got), (gate_kept, gate_halves[1])

    grad_post_attention = jnp.sum(hidden_res_grad * attended * scale_two, axis=0)
    attended_grad = norm_back(attended, scale_two, post_attention * hidden_res_grad).astype(bf16)
    out_total = mm_tn(context_rows, attended_grad).astype(bf16)
    attended_grad, out_total, gate_kept, up_kept = lax.optimization_barrier(
        (attended_grad, out_total, gate_halves[0], up_halves[0])
    )
    gate_halves, up_halves = (gate_kept, gate_halves[1]), (up_kept, up_halves[1])
    down_parts = send_tops(by_top(*down_halves))
    grad_out = lax.psum_scatter(out_total, ALL, scatter_dimension=0, tiled=True)
    context_grad = mm_nt(attended_grad, out_weight).astype(bf16)
    query_grad, grad_query_gain, near_part, far_part = attend_back(
        meta, seq_ends, slots, query_heads, context_grad, lse, turned, query_raw, query_gain[None], cosine, sine, near_keys, far_keys
    )
    far_part, near_part, gate_halves, up_halves, down_parts = lax.optimization_barrier(
        (far_part, near_part, gate_halves, up_halves, down_parts)
    )
    gate_parts, up_parts = [send_tops(by_top(*half)) for half in (gate_halves, up_halves)]
    far_part = xor(far_part, "seq", 1)
    query_low, far_part = together(query_grad, far_part)
    near_part = add16(near_part, far_part).reshape(2, layers, count, 2 * HEAD)
    near_part = add16(near_part[0], xor(near_part[1], "seq", 2))
    grad_query = mm_tn(picked_one, query_low).astype(bf16).reshape(devices, block_rows, wide_q)
    grad_query, near_part, gate_parts = together(scatter_step(grad_query, *core_mask), near_part, gate_parts)
    grad_query = scatter_rest(grad_query)
    key_parts = [near_part[k] if k == 0 else xor(near_part[k], "dp", 2 * k) for k in range(layers)]
    key_parts, up_parts = together(key_parts, up_parts)
    key_grads = functools.reduce(jnp.add, [part.astype(f32) for part in key_parts])
    value_grad = key_grads[:, HEAD:].astype(bf16)
    key_turned = rotate(key_grads[:, :HEAD], cosine, -sine)
    key_scale = norm_scale(key_raw)
    grad_key_gain = jnp.sum(key_turned * key_raw * key_scale, axis=0)
    key_grad = norm_back(key_raw, key_scale, key_gain * key_turned).astype(bf16)
    kv_grad = jnp.concatenate([key_grad, value_grad], axis=1)
    normed_one_grad = mm_nt(query_grad, natural_weight[:, :wide_q]) + mm_nt(kv_grad, natural_weight[:, wide_q:])
    grad_pre_attention = jnp.sum(normed_one_grad * rows_in * scale_one, axis=0)
    rows_grad = hidden_res_grad + norm_back(rows_in, scale_one, pre_attention * normed_one_grad)
    rows_low, down_parts, gate_parts, up_parts = together(rows_grad.astype(bf16), down_parts, gate_parts, up_parts)
    grad_down = total_of(down_parts)[0]
    both_grads = split(total_of(gate_parts).astype(bf16), total_of(up_parts).astype(bf16), members)
    grad_gate, grad_up = unpack(swap_members(column_exchange(both_grads)), z_bit, tops, members, ff_rows)
    input_grad = ungroup(rows_low)
    grad_kv = mm_tn(picked_one, kv_grad).reshape(devices, block_rows, 2 * HEAD)
    gain_grads = [
        grad_pre_attention,
        grad_post_attention,
        grad_pre_feed,
        grad_post_feed,
        grad_query_gain,
        grad_key_gain,
    ]
    gain_grads = jnp.concatenate([g.reshape(devices, -1) for g in gain_grads], axis=1)
    gain_grads = mm_tn(device_pick, gain_grads.astype(bf16))
    gain_grads = jnp.pad(
        gain_grads[:, None, :], ((0, 0), (model_rows, block_rows - model_rows - 1), (0, 2 * HEAD - gain_total))
    )
    last = scatter_rest(scatter_step((grad_kv + gain_grads).astype(bf16), *core_mask))
    last, grad_out = together(last, grad_out)
    grad_out = grad_out.astype(f32)
    gain_out, at = [], 0
    for size in gain_sizes:
        gain_out.append(last[model_rows, at : at + size])
        at += size
    return (
        output,
        input_grad,
        grad_query[:model_rows],
        last[:model_rows, :HEAD],
        last[:model_rows, HEAD:],
        grad_out,
        grad_gate,
        grad_up,
        grad_down,
        *gain_out,
    )


def solution(mesh):
    split = P(None, ALL, None)
    weight, gain = P(ALL, None), P(ALL)
    return jax.shard_map(
        per_device,
        mesh=mesh,
        in_specs=(split, split, P(), P(), *[weight] * 7, *[gain] * 6),
        out_specs=(split, split, *[weight] * 7, *[gain] * 6),
        check_vma=False,
    )
```

```python
import functools
import math

import jax
import jax.numpy as jnp
from jax import lax
from jax.experimental import pallas as pl
from jax.experimental.layout import Layout, with_layout_constraint
from jax.experimental.pallas import tpu as pltpu
from jax.sharding import PartitionSpec as P

HEADS = 4
HEAD = 256
MB = 2
STRETCH = 256

eps = 1e-06
rope_base = 1000000.0
masked_score = -1e30
bf16 = jnp.bfloat16
f32 = jnp.float32
ALL = ("dp", "seq")


def norm_scale(values):
    return lax.rsqrt(jnp.mean(values * values, axis=-1, keepdims=True) + eps)


def norm_back(values, scale, weighted):
    return scale * weighted - values * (scale * scale * scale) * jnp.mean(
        weighted * values, axis=-1, keepdims=True
    )


def rotate(values, cosine, sine):
    first, second = jnp.split(values, 2, axis=-1)
    return jnp.concatenate([first * cosine - second * sine, second * cosine + first * sine], axis=-1)


def layout_start(ends, row_ids):
    after = row_ids[:, None] >= ends[None, :]
    return jnp.max(jnp.where(after, ends[None, :], 0), axis=1)


def dot(left, right, dims):
    return lax.dot_general(left, right, (dims, ((), ())), preferred_element_type=f32)


def mm(left, right):
    return dot(left, right, ((1,), (0,)))


def mm_tn(left, right):
    return dot(left, right, ((0,), (0,)))


def mm_nt(left, right):
    return dot(left, right, ((1,), (1,)))


def xor(value, axis, mask):
    return lax.ppermute(value, axis, [(i, i ^ mask) for i in range(lax.axis_size(axis))])


def xor_both(value, dp_mask, seq_mask):
    members = lax.axis_size("seq")
    mask = dp_mask * members + seq_mask
    return lax.ppermute(value, ALL, [(i, i ^ mask) for i in range(lax.axis_size("dp") * members)])


def flips(value, bits):
    for axis, bit in enumerate(bits):
        halves = [lax.slice_in_dim(value, i, i + 1, axis=axis) for i in (1, 0)]
        value = jnp.where(bit == 1, lax.concatenate(halves, axis), value)
    return value


def add16(left, right):
    return (left.astype(f32) + right.astype(f32)).astype(bf16)


def together(*values):
    return lax.optimization_barrier(values)


def all_masks():
    rows = [(1 << bit, 0) for bit in range(1, 16) if 1 << bit < lax.axis_size("dp")]
    return rows + [(1, 0), (0, 2), (0, 1)]


def gather_step(value, dp_mask, seq_mask):
    return jnp.concatenate([value, xor_both(value, dp_mask, seq_mask)])


def all_labels():
    labels = [(0, 0)]
    for dp_mask, seq_mask in all_masks():
        labels = labels + [(d ^ dp_mask, s ^ seq_mask) for d, s in labels]
    return labels


def scatter_step(total, dp_mask, seq_mask):
    half = total.shape[0] // 2
    got = xor_both(total[half:], dp_mask, seq_mask)
    total = total[:half].astype(f32) + got.astype(f32)
    return total if half == 1 else total.astype(bf16)


def gather_group(rows):
    half = rows.shape[0] // 2
    across, along = xor(rows, "seq", 2), xor(rows, "dp", 2)
    corner = [xor(across[:half], "dp", 2), xor(along[half:], "seq", 2)]
    near = [rows, across, along, *corner]
    far = [rows, jnp.concatenate([across, along]), jnp.concatenate(corner)]
    return jnp.concatenate(near + [xor(part, "seq", 1) for part in far], axis=0)


def scatter_group(total):
    parts = total.reshape(2, -1, total.shape[1])
    near = add16(parts[0], xor(parts[1], "seq", 1))
    mine, across, along, corner = jnp.split(near, 4)
    half = mine.shape[0] // 2
    low, high = xor(corner[:half], "dp", 2), xor(corner[half:], "seq", 2)
    across = jnp.concatenate([add16(across[:half], low), across[half:]])
    along = jnp.concatenate([along[:half], add16(along[half:], high)])
    return mine.astype(f32) + xor(across, "seq", 2).astype(f32) + xor(along, "dp", 2).astype(f32)


def place_kernel(sizes, target_ref, *refs):
    pieces, out = refs[: len(sizes)], refs[len(sizes)]
    buffer, arrived, left = refs[len(sizes) + 1 :]
    ins, outs, block = [], [], 0
    for piece, size in zip(pieces, sizes):
        for index in range(size):
            ins.append(pltpu.make_async_copy(piece.at[index], buffer.at[block], arrived.at[block]))
            outs.append(pltpu.make_async_copy(buffer.at[block], out.at[target_ref[block]], left.at[block]))
            ins[-1].start()
            block += 1
    for copy_in, copy_out in zip(ins, outs):
        copy_in.wait()
        copy_out.start()
    for copy_out in outs:
        copy_out.wait()


def place(pieces, targets):
    sizes = [piece.shape[0] for piece in pieces]
    shape = (sum(sizes), *pieces[0].shape[1:])
    anywhere = pl.BlockSpec(memory_space=pl.ANY)
    return pl.pallas_call(
        functools.partial(place_kernel, sizes),
        grid_spec=pltpu.PrefetchScalarGridSpec(
            num_scalar_prefetch=1,
            grid=(1,),
            in_specs=[anywhere] * len(pieces),
            out_specs=anywhere,
            scratch_shapes=[
                pltpu.VMEM(shape, pieces[0].dtype),
                pltpu.SemaphoreType.DMA((shape[0],)),
                pltpu.SemaphoreType.DMA((shape[0],)),
            ],
        ),
        out_shape=jax.ShapeDtypeStruct(shape, pieces[0].dtype),
        name="place",
        cost_estimate=pl.CostEstimate(flops=0, bytes_accessed=4 * math.prod(shape), transcendentals=0),
    )(targets, *pieces)


def project_kernel(scale, picked_ref, weight_ref, gain_ref, cos_ref, sin_ref, raw_ref, out_ref):
    raw = mm(picked_ref[...], weight_ref[...])
    raw_ref[0] = raw
    turned = rotate(raw * norm_scale(raw) * gain_ref[...], cos_ref[...], sin_ref[...]).astype(bf16)
    out_ref[...] = (turned * scale).astype(bf16).reshape(out_ref.shape)


def project(picked, weight, gain, cosine, sine):
    count, deep = picked.shape
    rows = count // 2
    same = lambda h: (0, 0)
    return pl.pallas_call(
        functools.partial(project_kernel, HEAD**-0.5),
        grid=(HEADS,),
        in_specs=[
            pl.BlockSpec((count, deep), same),
            pl.BlockSpec((deep, HEAD), lambda h: (0, h)),
            pl.BlockSpec((1, HEAD), same),
            pl.BlockSpec((count, HEAD // 2), same),
            pl.BlockSpec((count, HEAD // 2), same),
        ],
        out_specs=[
            pl.BlockSpec((1, count, HEAD), lambda h: (h, 0, 0)),
            pl.BlockSpec((2, 1, rows, HEAD), lambda h: (0, h, 0, 0)),
        ],
        out_shape=[
            jax.ShapeDtypeStruct((HEADS, count, HEAD), f32),
            jax.ShapeDtypeStruct((2, HEADS, rows, HEAD), bf16),
        ],
        name="project",
        cost_estimate=pl.CostEstimate(
            flops=2 * count * deep * HEADS * HEAD, bytes_accessed=2 * deep * HEADS * HEAD, transcendentals=0
        ),
    )(picked, weight, gain, cosine, sine)


def project_keys_kernel(picked_ref, weight_ref, gain_ref, cos_ref, sin_ref, raw_ref, out_ref):
    both = mm(picked_ref[...], weight_ref[...])
    raw = both[:, :HEAD]
    raw_ref[...] = raw
    turned = rotate(raw * norm_scale(raw) * gain_ref[...], cos_ref[...], sin_ref[...])
    both = jnp.concatenate([turned, both[:, HEAD:]], axis=1).astype(bf16)
    out_ref[...] = both.reshape(out_ref.shape)


def project_keys(picked, weight, gain, cosine, sine):
    count, deep = picked.shape
    return pl.pallas_call(
        project_keys_kernel,
        grid=(1,),
        in_specs=[
            whole_of(picked),
            whole_of(weight),
            whole_of(gain),
            whole_of(cosine),
            whole_of(sine),
        ],
        out_specs=[
            pl.BlockSpec((count, HEAD), lambda i: (0, 0)),
            pl.BlockSpec((2, count // 2, 2 * HEAD), lambda i: (0, 0, 0)),
        ],
        out_shape=[
            jax.ShapeDtypeStruct((count, HEAD), f32),
            jax.ShapeDtypeStruct((2, count // 2, 2 * HEAD), bf16),
        ],
        name="project_keys",
        cost_estimate=pl.CostEstimate(
            flops=4 * count * deep * HEAD, bytes_accessed=4 * deep * HEAD, transcendentals=0
        ),
    )(picked, weight, gain, cosine, sine)


def mask_of(meta_ref, ends_ref, unit, rows, key_stretch):
    lanes = lax.broadcasted_iota(jnp.int32, (1, HEADS * rows), 1)
    ids = meta_ref[3 * unit] + lanes % rows
    start = jnp.zeros_like(ids)
    for index in range(ends_ref.shape[0]):
        end = ends_ref[index]
        start = jnp.where(ids >= end, end, start)
    place_in = lax.broadcasted_iota(jnp.int32, (STRETCH, 1), 0)
    near = meta_ref[6] * rows
    place_in = jnp.where(place_in < rows, place_in + near, place_in - near)
    key = key_stretch * STRETCH + place_in
    return (key <= ids) & (key >= start)


def attend_kernel(
    rows, meta_ref, ends_ref, slots_ref, q_ref, near_ref, far_ref, c_ref, turned_ref, lse_ref, top, total, acc
):
    step = pl.program_id(0)

    @pl.when(step == 0)
    def _():
        top[...] = jnp.full_like(top, masked_score)
        total[...] = jnp.zeros_like(total)
        acc[...] = jnp.zeros_like(acc)

    key_stretch = slots_ref[step]
    for unit in range(2):

        @pl.when((key_stretch <= meta_ref[3 * unit + 1]) & (key_stretch >= meta_ref[3 * unit + 2]))
        def _():
            mask = mask_of(meta_ref, ends_ref, unit, rows, key_stretch)
            block = jnp.concatenate([near_ref[...], far_ref[...]], axis=0)
            query = q_ref[unit].reshape(HEADS * rows, HEAD)
            scores = jnp.where(mask, mm_nt(block[:, :HEAD], query), masked_score)
            old = top[unit]
            new = jnp.maximum(old, jnp.max(scores, axis=0, keepdims=True))
            keep = jnp.exp(old - new)
            terms = jnp.exp(scores - new)
            top[unit] = new
            total[unit] = total[unit] * keep + jnp.sum(terms, axis=0, keepdims=True)
            acc[unit] = acc[unit] * keep + mm_tn(block[:, HEAD:], terms.astype(bf16))

    @pl.when(step == pl.num_programs(0) - 1)
    def _():
        for unit in range(2):
            out = acc[unit] * (1.0 / total[unit])
            turned_ref[unit] = out
            lse_ref[unit] = top[unit] + jnp.log(total[unit])
            out = out.T.astype(bf16)
            for head in range(HEADS):
                c_ref[unit * rows : (unit + 1) * rows, head * HEAD : (head + 1) * HEAD] = out[
                    head * rows : (head + 1) * rows
                ]


def attend_back_kernel(
    rows,
    meta_ref,
    ends_ref,
    slots_ref,
    q_ref,
    dc_ref,
    lse_ref,
    turned_ref,
    raw_ref,
    gain_ref,
    cos_ref,
    sin_ref,
    near_ref,
    far_ref,
    dq_ref,
    dgain_ref,
    dnear_ref,
    dfar_ref,
    grads,
    delta,
    acc,
    both,
):
    step = pl.program_id(0)

    @pl.when(step == 0)
    def _():
        acc[...] = jnp.zeros_like(acc)
        for unit in range(2):
            for head in range(HEADS):
                grads[unit, head * rows : (head + 1) * rows] = dc_ref[
                    unit * rows : (unit + 1) * rows, head * HEAD : (head + 1) * HEAD
                ]
            across = grads[unit].astype(f32).T
            delta[unit] = jnp.sum(across * turned_ref[unit], axis=0, keepdims=True)

    key_stretch = slots_ref[step]
    both[...] = jnp.zeros_like(both)
    for unit in range(2):

        @pl.when((key_stretch <= meta_ref[3 * unit + 1]) & (key_stretch >= meta_ref[3 * unit + 2]))
        def _():
            mask = mask_of(meta_ref, ends_ref, unit, rows, key_stretch)
            block = jnp.concatenate([near_ref[...], far_ref[...]], axis=0)
            key, value = block[:, :HEAD], block[:, HEAD:]
            query = q_ref[unit].reshape(HEADS * rows, HEAD)
            grad = grads[unit]
            probs = jnp.where(mask, jnp.exp(mm_nt(key, query) - lse_ref[unit]), 0.0)
            score_grad = (probs * (mm_nt(value, grad) - delta[unit])).astype(bf16)
            acc[unit] += mm_tn(key, score_grad)
            both[:, :HEAD] += mm(score_grad, query)
            both[:, HEAD:] += mm(probs.astype(bf16), grad)

    dnear_ref[...] = both[:rows].astype(bf16)
    dfar_ref[...] = both[rows:].astype(bf16)

    @pl.when(step == pl.num_programs(0) - 1)
    def _():
        gain = gain_ref[...]
        total = jnp.zeros_like(gain)
        for unit in range(2):
            mine = slice(unit * rows, (unit + 1) * rows)
            grad = acc[unit].T * HEAD**-0.5
            for head in range(HEADS):
                back = rotate(grad[head * rows : (head + 1) * rows], cos_ref[mine], -sin_ref[mine])
                raw = raw_ref[head, mine]
                scale = norm_scale(raw)
                total = total + jnp.sum(back * raw * scale, axis=0, keepdims=True)
                back = norm_back(raw, scale, gain * back)
                dq_ref[mine, head * HEAD : (head + 1) * HEAD] = back.astype(bf16)
        dgain_ref[...] = total


def whole_of(array):
    return pl.BlockSpec(array.shape, lambda *_: (0,) * len(array.shape))


def attend(meta, ends, slots, query, near, far):
    rows = query.shape[2]
    wide = HEADS * rows
    keys = pl.BlockSpec((None, None, rows, 2 * HEAD), lambda j, *_: (j // 2, j % 2, 0, 0))
    outs = [
        jax.ShapeDtypeStruct((2 * rows, HEADS * HEAD), bf16),
        jax.ShapeDtypeStruct((2, HEAD, wide), f32),
        jax.ShapeDtypeStruct((2, 1, wide), f32),
    ]
    return pl.pallas_call(
        functools.partial(attend_kernel, rows),
        grid_spec=pltpu.PrefetchScalarGridSpec(
            num_scalar_prefetch=3,
            grid=(slots.shape[0],),
            in_specs=[whole_of(query), keys, keys],
            out_specs=[whole_of(out) for out in outs],
            scratch_shapes=[
                pltpu.VMEM((2, 1, wide), f32),
                pltpu.VMEM((2, 1, wide), f32),
                pltpu.VMEM((2, HEAD, wide), f32),
            ],
        ),
        out_shape=outs,
        name="attend",
        cost_estimate=pl.CostEstimate(
            flops=4 * 2 * 9 * STRETCH * wide * HEAD,
            bytes_accessed=4 * near.size,
            transcendentals=2 * 9 * STRETCH * wide,
        ),
    )(meta, ends, slots, query, near, far)


def attend_back(meta, ends, slots, query, grad, lse, turned, raw, gain, cosine, sine, near, far):
    rows = query.shape[2]
    wide = HEADS * rows
    keys = pl.BlockSpec((None, None, rows, 2 * HEAD), lambda j, *_: (j // 2, j % 2, 0, 0))
    fixed = [query, grad, lse, turned, raw, gain, cosine, sine]
    outs = [jax.ShapeDtypeStruct(grad.shape, bf16), jax.ShapeDtypeStruct(gain.shape, f32)]
    return pl.pallas_call(
        functools.partial(attend_back_kernel, rows),
        grid_spec=pltpu.PrefetchScalarGridSpec(
            num_scalar_prefetch=3,
            grid=(slots.shape[0],),
            in_specs=[*[whole_of(array) for array in fixed], keys, keys],
            out_specs=[*[whole_of(out) for out in outs], keys, keys],
            scratch_shapes=[
                pltpu.VMEM((2, wide, HEAD), bf16),
                pltpu.VMEM((2, 1, wide), f32),
                pltpu.VMEM((2, HEAD, wide), f32),
                pltpu.VMEM((STRETCH, 2 * HEAD), f32),
            ],
        ),
        out_shape=[*outs, jax.ShapeDtypeStruct(near.shape, bf16), jax.ShapeDtypeStruct(near.shape, bf16)],
        name="attend_back",
        cost_estimate=pl.CostEstimate(
            flops=10 * 2 * 9 * STRETCH * wide * HEAD,
            bytes_accessed=8 * near.size,
            transcendentals=2 * 9 * STRETCH * wide,
        ),
    )(meta, ends, slots, *fixed, near, far)


def blocks_of(tops, low, member, members, ff):
    return [(((hi * 2 + low) * 2 + y) * members + member) * ff for hi in range(tops) for y in range(2)]

def pack_kernel(tops, members, ff, gate_ref, up_ref, out_ref):
    for which, ref in enumerate((gate_ref, up_ref)):
        value = ref[...]
        for low in range(2):
            for member in range(members):
                cuts = [value[:, at : at + ff] for at in blocks_of(tops, low, member, members, ff)]
                out_ref[low, member, which] = jnp.concatenate(cuts, axis=1)

def pack(gate, up, tops, members, ff):
    rows = gate.shape[0]
    return pl.pallas_call(functools.partial(pack_kernel, tops, members, ff),
        out_shape=jax.ShapeDtypeStruct((2, members, 2, rows, 2 * tops * ff), bf16), name="pack")(gate, up)

def unpack_kernel(tops, members, ff, low_ref, in_ref, gate_ref, up_ref):
    for which, ref in enumerate((gate_ref, up_ref)):
        pieces = [None] * (2 * tops * 2 * members)
        for low in range(2):
            for member in range(members):
                value = in_ref[member, low_ref[0] ^ low, which].astype(f32)
                for i, at in enumerate(blocks_of(tops, low, member, members, ff)):
                    pieces[at // ff] = value[:, i * ff : (i + 1) * ff]
        ref[...] = jnp.concatenate(pieces, axis=1)

def unpack(moved, low_bit, tops, members, ff):
    rows = moved.shape[3]
    shape = jax.ShapeDtypeStruct((rows, 4 * tops * members * ff), f32)
    return pl.pallas_call(functools.partial(unpack_kernel, tops, members, ff),
        in_specs=[pl.BlockSpec(memory_space=pltpu.SMEM), pl.BlockSpec(memory_space=pltpu.VMEM)],
        out_shape=[shape, shape], name="unpack")(low_bit[None], moved)

def merge_kernel(in_ref, gate_ref, up_ref):
    for which, ref in enumerate((gate_ref, up_ref)):
        for low in range(2):
            ref[low] = jnp.concatenate([in_ref[m, low, which] for m in range(in_ref.shape[0])], axis=0)

def merge(moved):
    members, _, _, rows, wide = moved.shape
    shape = jax.ShapeDtypeStruct((2, members * rows, wide), bf16)
    return pl.pallas_call(merge_kernel, out_shape=[shape, shape], name="merge")(moved)

def split_kernel(gate_ref, up_ref, out_ref):
    members, rows = out_ref.shape[1], out_ref.shape[3]
    for which, ref in enumerate((gate_ref, up_ref)):
        for low in range(2):
            value = ref[low]
            for m in range(members):
                out_ref[low, m, which] = value[m * rows : (m + 1) * rows]

def split(gate, up, members):
    _, tall, wide = gate.shape
    return pl.pallas_call(split_kernel,
        out_shape=jax.ShapeDtypeStruct((2, members, 2, tall // members, wide), bf16), name="split")(gate, up)


def per_device(
    inputs,
    cotangent,
    lengths,
    deal,
    w_query,
    w_key,
    w_value,
    w_out,
    w_gate,
    w_up,
    w_down,
    gain_attn_pre,
    gain_attn_post,
    gain_ffw_pre,
    gain_ffw_post,
    gain_query,
    gain_key,
):
    rows, width = inputs.shape[1], inputs.shape[2]
    groups, members = lax.axis_size("dp"), lax.axis_size("seq")
    devices = groups * members
    total_rows = rows * devices
    dp_id, seq_id = lax.axis_index("dp"), lax.axis_index("seq")
    half_bit, x_bit, y_bit, z_bit = seq_id % 2, seq_id // 2, dp_id % 2, dp_id // 2 % 2
    tops = groups // 4
    count = 2 * rows
    model_rows, out_rows, ff_rows = w_query.shape[0], w_out.shape[0], w_down.shape[0]
    ff_local = 2 * tops * ff_rows
    wide_q = HEADS * HEAD
    gain_sizes = [gain_attn_pre.shape[0]] * 4 + [gain_query.shape[0]] * 2
    gain_total = sum(gain_sizes)
    block_rows = (model_rows + 8) // 8 * 8

    def regroup(array):
        kept = lax.dynamic_index_in_dim(array, y_bit, 0, keepdims=False)
        sent = lax.dynamic_index_in_dim(array, 1 - y_bit, 0, keepdims=False)
        return jnp.concatenate([kept, xor(sent, "dp", 1)], axis=0)

    def ungroup(array):
        kept, sent = array[:rows], array[rows:]
        return flips(jnp.stack([kept, xor(sent, "dp", 1)]), [y_bit])


    def column_exchange(packed):
        kept = lax.dynamic_index_in_dim(packed, z_bit, 0, keepdims=False)
        sent = lax.dynamic_index_in_dim(packed, 1 - z_bit, 0, keepdims=False)
        return jnp.stack([kept, xor(sent, "dp", 2)], axis=1)

    def swap_members(parts):
        return lax.all_to_all(parts, "seq", split_axis=0, concat_axis=0, tiled=True)

    gain_line, at = jnp.zeros((1, 2 * HEAD), f32), 0
    for gain in (gain_attn_pre, gain_attn_post, gain_ffw_pre, gain_ffw_post, gain_query, gain_key):
        gain_line += jnp.pad(gain.astype(f32)[None, :], ((0, 0), (at, gain_line.shape[1] - at - gain.shape[0])))
        at += gain.shape[0]
    shard = jnp.concatenate([jnp.concatenate([w_key, w_value], axis=1), gain_line.astype(bf16)], axis=0)
    blocks = jnp.pad(shard, ((0, block_rows - model_rows - 1), (0, 0)))[None]
    q_blocks = jnp.pad(w_query, ((0, block_rows - model_rows), (0, 0)))[None]
    packed = pack(w_gate, w_up, tops, members, ff_rows)
    first_mask, *more_masks, x_mask, core_mask = all_masks()
    blocks = gather_step(blocks, *first_mask)
    last_mask = first_mask
    for masks in [*more_masks, x_mask]:
        blocks, q_blocks = together(gather_step(blocks, *masks), gather_step(q_blocks, *last_mask))
        last_mask = masks
    blocks, packed, down_piece, rows_low = together(blocks, packed, w_down[None], regroup(inputs))
    rows_in = rows_low.astype(f32)
    column_parts = column_exchange(packed)
    q_blocks = gather_step(q_blocks, *x_mask)
    blocks = gather_step(blocks, *core_mask)
    kv_weight = blocks.reshape(devices * block_rows, 2 * HEAD)
    labels = all_labels()
    natural = jnp.stack([(dp_id ^ d) * members + (seq_id ^ s) for d, s in labels]).astype(jnp.int32)

    def selection(order, size, block, padded):
        within = jnp.arange(padded, dtype=jnp.int32)
        source = jnp.where(within < block, order[:, None] * block + within, -1).reshape(-1)
        return (jnp.arange(size, dtype=jnp.int32)[:, None] == source[None, :]).astype(bf16)

    model_pick = selection(natural, width, model_rows, block_rows)
    device_pick = selection(natural, devices, 1, 1)
    out_pick = selection(natural, wide_q, out_rows, out_rows)
    gain_blocks = blocks[:, model_rows, :gain_total]
    gain_all = mm(device_pick, gain_blocks)
    full_gain, at = [], 0
    for size in gain_sizes:
        full_gain.append(gain_all[:, at : at + size].reshape(devices * size))
        at += size
    pre_attention, post_attention, pre_feed, post_feed, query_gain, key_gain = full_gain

    top_id = dp_id // 4

    def from_tops(piece):
        return [piece] + [xor(piece, "dp", 4 * k) for k in range(1, tops)]

    def both_sides(tall):
        return tall + [xor(part, "dp", 1) for part in tall]

    owners = [(top_id ^ k) * 2 + (y_bit ^ u) for u in range(2) for k in range(tops)]
    owners = jnp.stack(owners).astype(jnp.int32)
    sources = [((top_id ^ k) * 2 + (z_bit ^ v)) * 2 + (y_bit ^ u) for u in range(2) for k in range(tops) for v in range(2)]
    sources = jnp.stack(sources).astype(jnp.int32)

    down_tall = from_tops(down_piece)

    seq_ends = jnp.cumsum(lax.dynamic_index_in_dim(lengths, y_bit, 0, keepdims=False))
    dealt = lax.dynamic_index_in_dim(deal, y_bit, 0, keepdims=False)
    unit_ids = jnp.stack([(dp_id ^ u) * members + seq_id for u in range(2)])
    stretches = dealt[unit_ids * rows // STRETCH]
    first_rows = stretches * STRETCH + unit_ids * rows % STRETCH
    my_rows = (first_rows[:, None] + jnp.arange(rows, dtype=jnp.int32)).reshape(count)
    starts = layout_start(seq_ends, my_rows)
    lows = starts.reshape(2, rows)[:, 0] // STRETCH
    meta = jnp.concatenate([jnp.stack([first_rows, stretches, lows], axis=1).reshape(-1), half_bit[None]])
    layers = groups // 2
    slot_ids = jnp.stack(
        [
            ((dp_id // 2 ^ z) * 2 + (y_bit ^ u)) * (members // 2) + (x_bit ^ x)
            for x in range(2)
            for z in range(layers)
            for u in range(2)
        ]
    )
    slots = dealt[slot_ids]
    positions = my_rows - starts
    valid = (my_rows < total_rows - STRETCH)[:, None]
    freqs = rope_base ** (-2.0 * jnp.arange(HEAD // 2, dtype=f32) / HEAD)
    angle = positions.astype(f32)[:, None] * freqs
    cosine, sine = jnp.cos(angle), jnp.sin(angle)

    scale_one = norm_scale(rows_in)
    normed_one = (rows_in * scale_one * pre_attention).astype(bf16)
    picked_one = mm(normed_one, model_pick).astype(bf16)
    key_raw, keys_mine = project_keys(picked_one, kv_weight, key_gain[None], cosine, sine)
    column = [keys_mine] + [xor(keys_mine, "dp", 2 * k) for k in range(1, layers)]
    column[1], down_tall, column_parts, late_out = together(column[1], down_tall, column_parts, w_out)
    out_weight = lax.all_gather(late_out, ALL, axis=0, tiled=True)
    halves = merge(swap_members(column_parts))
    halves, others, q_blocks = together(halves, column[1:], q_blocks)
    q_weight = gather_step(q_blocks, *core_mask).reshape(devices * block_rows, wide_q)
    column = [column[0], *others]
    gate_tall, up_half = together(from_tops(halves[0]), halves[1])
    up_tall = from_tops(up_half)
    across = [xor(part, "seq", 2) for part in column]
    down_pieces = both_sides(down_tall)
    column, across = jnp.stack(column), jnp.stack(across)
    near_keys = jnp.concatenate([column, across])
    far_keys = jnp.concatenate([xor(column, "seq", 1), xor(across, "seq", 1)])
    query_raw, query_heads = project(picked_one, q_weight, query_gain[None], cosine, sine)
    query_heads, gate_tall = together(query_heads, gate_tall)
    gate_pieces = both_sides(gate_tall)
    context_rows, turned, lse = attend(meta, seq_ends, slots, query_heads, near_keys, far_keys)
    context_rows, gate_pieces, up_tall, down_pieces = together(context_rows, gate_pieces, up_tall, down_pieces)
    picked_context = mm(context_rows, out_pick).astype(bf16)
    up_pieces = both_sides(up_tall)
    down_weight = place(down_pieces, owners).reshape(ff_local, width)
    gate_weight, up_weight = [place(pieces, sources).reshape(width, ff_local) for pieces in (gate_pieces, up_pieces)]
    attended = mm(context_rows, out_weight)
    scale_two = norm_scale(attended)
    hidden_res = rows_in + attended * scale_two * post_attention
    scale_three = norm_scale(hidden_res)
    normed_two = (hidden_res * scale_three * pre_feed).astype(bf16)

    normed_group = gather_group(normed_two)
    gate_raw = mm(normed_group, gate_weight)
    up_raw = mm(normed_group, up_weight)
    hidden_low = (jax.nn.gelu(gate_raw, approximate=True) * up_raw).astype(bf16)
    mixed = scatter_group(mm(hidden_low, down_weight).astype(bf16))
    q_natural, kv_natural = mm(model_pick, q_weight).astype(bf16), mm(model_pick, kv_weight).astype(bf16)
    q_natural, kv_natural, picked_context, mixed = together(q_natural, kv_natural, picked_context, mixed)
    scale_four = norm_scale(mixed)
    result = hidden_res + mixed * scale_four * post_feed
    output = ungroup(jnp.where(valid, result, 0.0).astype(bf16))

    upstream = jnp.where(valid, regroup(cotangent).astype(f32), 0.0)
    grad_post_feed = jnp.sum(upstream * mixed * scale_four, axis=0)
    mixed_grad = norm_back(mixed, scale_four, post_feed * upstream).astype(bf16)
    mixed_group = gather_group(mixed_grad)
    hidden_grad = mm_nt(mixed_group, down_weight)
    _, gelu_pull = jax.vjp(lambda g, u: jax.nn.gelu(g, approximate=True) * u, gate_raw, up_raw)
    gate_grad, up_grad = gelu_pull(hidden_grad)
    gate_grad, up_grad = gate_grad.astype(bf16), up_grad.astype(bf16)
    partial_grad = (mm_nt(gate_grad, gate_weight) + mm_nt(up_grad, up_weight)).astype(bf16)
    hidden_low, mixed_group, normed_group, gate_grad, up_grad, partial_grad = together(
        hidden_low, mixed_group, normed_group, gate_grad, up_grad, partial_grad
    )
    normed_two_grad = scatter_group(partial_grad)
    grad_pre_feed = jnp.sum(normed_two_grad * hidden_res * scale_three, axis=0)
    hidden_res_grad = upstream + norm_back(hidden_res, scale_three, pre_feed * normed_two_grad)

    def halve(total):
        kept = lax.dynamic_index_in_dim(total, y_bit, 2, keepdims=False)
        return kept, xor(lax.dynamic_index_in_dim(total, 1 - y_bit, 2, keepdims=False), "dp", 1)

    def by_top(kept, got):
        kept = add16(kept, got)
        return [lax.dynamic_index_in_dim(kept, top_id ^ k, 0, keepdims=False) for k in range(tops)]

    def send_tops(parts):
        return [part if k == 0 else xor(part, "dp", 4 * k) for k, part in enumerate(parts)]

    def total_of(parts):
        return functools.reduce(jnp.add, [part.astype(f32) for part in parts])

    def column_blocks(total):
        total = with_layout_constraint(total.astype(bf16), Layout((0, 1)))
        return total.reshape(tops, 2, 2, members * model_rows, ff_local)

    down_halves = halve(mm_tn(hidden_low, mixed_group).astype(bf16).reshape(tops, 1, 2, ff_rows, width))
    down_kept, gate_grad = together(down_halves[0], gate_grad)
    gate_halves = halve(column_blocks(mm_tn(normed_group, gate_grad)))
    gate_kept, down_got, up_grad = together(gate_halves[0], down_halves[1], up_grad)
    up_halves = halve(column_blocks(mm_tn(normed_group, up_grad)))
    down_halves, gate_halves = (down_kept, down_got), (gate_kept, gate_halves[1])

    grad_post_attention = jnp.sum(hidden_res_grad * attended * scale_two, axis=0)
    attended_grad = norm_back(attended, scale_two, post_attention * hidden_res_grad).astype(bf16)
    out_total = mm_tn(picked_context, attended_grad).astype(bf16).reshape(devices, out_rows, width)
    attended_grad, out_total, gate_kept, up_kept = lax.optimization_barrier(
        (attended_grad, out_total, gate_halves[0], up_halves[0])
    )
    gate_halves, up_halves = (gate_kept, gate_halves[1]), (up_kept, up_halves[1])
    down_parts = send_tops(by_top(*down_halves))
    context_grad = mm_nt(attended_grad, out_weight).astype(bf16)
    out_total, context_grad, gate_halves = together(scatter_step(out_total, *core_mask), context_grad, gate_halves)
    gate_parts = send_tops(by_top(*gate_halves))
    out_total = scatter_step(out_total, *x_mask)
    query_grad, grad_query_gain, near_part, far_part = attend_back(
        meta, seq_ends, slots, query_heads, context_grad, lse, turned, query_raw, query_gain[None], cosine, sine, near_keys, far_keys
    )
    far_part, near_part, up_halves, down_parts, out_total = together(far_part, near_part, up_halves, down_parts, out_total)
    far_part = xor(far_part, "seq", 1)
    query_low, far_part, up_tops = together(query_grad, far_part, by_top(*up_halves))
    up_parts = send_tops(up_tops)
    for masks in reversed([first_mask, *more_masks]):
        out_total = scatter_step(out_total, *masks)
    near_part = add16(near_part, far_part).reshape(2, layers, count, 2 * HEAD)
    near_part = add16(near_part[0], xor(near_part[1], "seq", 2))
    grad_query = mm_tn(picked_one, query_low).astype(bf16).reshape(devices, block_rows, wide_q)
    grad_query, near_part, gate_parts = together(scatter_step(grad_query, *core_mask), near_part, gate_parts)
    for masks in reversed([first_mask, *more_masks, x_mask]):
        grad_query = scatter_step(grad_query, *masks)
    grad_query = grad_query[0]
    key_parts = [near_part[k] if k == 0 else xor(near_part[k], "dp", 2 * k) for k in range(layers)]
    grad_out = out_total[0]
    key_parts, up_parts = together(key_parts, up_parts)
    key_grads = functools.reduce(jnp.add, [part.astype(f32) for part in key_parts])
    value_grad = key_grads[:, HEAD:].astype(bf16)
    key_turned = rotate(key_grads[:, :HEAD], cosine, -sine)
    key_scale = norm_scale(key_raw)
    grad_key_gain = jnp.sum(key_turned * key_raw * key_scale, axis=0)
    key_grad = norm_back(key_raw, key_scale, key_gain * key_turned).astype(bf16)
    kv_grad = jnp.concatenate([key_grad, value_grad], axis=1)
    normed_one_grad = mm_nt(query_grad, q_natural) + mm_nt(kv_grad, kv_natural)
    grad_pre_attention = jnp.sum(normed_one_grad * rows_in * scale_one, axis=0)
    rows_grad = hidden_res_grad + norm_back(rows_in, scale_one, pre_attention * normed_one_grad)
    rows_low, down_parts, gate_parts, up_parts = together(rows_grad.astype(bf16), down_parts, gate_parts, up_parts)
    grad_down = total_of(down_parts)[0]
    both_grads = split(total_of(gate_parts).astype(bf16), total_of(up_parts).astype(bf16), members)
    input_grad = ungroup(rows_low)
    grad_kv = mm_tn(picked_one, kv_grad).reshape(devices, block_rows, 2 * HEAD)
    gain_grads = [
        grad_pre_attention,
        grad_post_attention,
        grad_pre_feed,
        grad_post_feed,
        grad_query_gain,
        grad_key_gain,
    ]
    gain_grads = jnp.concatenate([g.reshape(devices, -1) for g in gain_grads], axis=1)
    gain_grads = mm_tn(device_pick, gain_grads.astype(bf16))
    gain_grads = jnp.pad(
        gain_grads[:, None, :], ((0, 0), (model_rows, block_rows - model_rows - 1), (0, 2 * HEAD - gain_total))
    )
    last = scatter_step((grad_kv + gain_grads).astype(bf16), *core_mask)
    last, column_parts = together(scatter_step(last, *x_mask), column_exchange(both_grads))
    for masks in reversed(more_masks):
        last = scatter_step(last, *masks)
    last, column_parts = together(last, swap_members(column_parts))
    grad_gate, grad_up = unpack(column_parts, z_bit, tops, members, ff_rows)
    last = scatter_step(last, *first_mask)[0]
    gain_out, at = [], 0
    for size in gain_sizes:
        gain_out.append(last[model_rows, at : at + size])
        at += size
    return (
        output,
        input_grad,
        grad_query[:model_rows],
        last[:model_rows, :HEAD],
        last[:model_rows, HEAD:],
        grad_out,
        grad_gate,
        grad_up,
        grad_down,
        *gain_out,
    )


def solution(mesh):
    split = P(None, ALL, None)
    weight, gain = P(ALL, None), P(ALL)
    return jax.shard_map(
        per_device,
        mesh=mesh,
        in_specs=(split, split, P(), P(), *[weight] * 7, *[gain] * 6),
        out_specs=(split, split, *[weight] * 7, *[gain] * 6),
        check_vma=False,
    )
```

```python
import functools
import math

import jax
import jax.numpy as jnp
from jax import lax
from jax.experimental import pallas as pl
from jax.experimental.layout import Layout, with_layout_constraint
from jax.experimental.pallas import tpu as pltpu
from jax.sharding import PartitionSpec as P

HEADS = 4
HEAD = 256
MB = 2
STRETCH = 256

eps = 1e-06
rope_base = 1000000.0
masked_score = -1e30
bf16 = jnp.bfloat16
f32 = jnp.float32
ALL = ("dp", "seq")


def norm_scale(values):
    return lax.rsqrt(jnp.mean(values * values, axis=-1, keepdims=True) + eps)


def norm_back(values, scale, weighted):
    return scale * weighted - values * (scale * scale * scale) * jnp.mean(
        weighted * values, axis=-1, keepdims=True
    )


def rotate(values, cosine, sine):
    first, second = jnp.split(values, 2, axis=-1)
    return jnp.concatenate([first * cosine - second * sine, second * cosine + first * sine], axis=-1)


def layout_start(ends, row_ids):
    after = row_ids[:, None] >= ends[None, :]
    return jnp.max(jnp.where(after, ends[None, :], 0), axis=1)


def dot(left, right, dims):
    return lax.dot_general(left, right, (dims, ((), ())), preferred_element_type=f32)


def mm(left, right):
    return dot(left, right, ((1,), (0,)))


def mm_tn(left, right):
    return dot(left, right, ((0,), (0,)))


def mm_nt(left, right):
    return dot(left, right, ((1,), (1,)))


def xor(value, axis, mask):
    return lax.ppermute(value, axis, [(i, i ^ mask) for i in range(lax.axis_size(axis))])


def xor_both(value, dp_mask, seq_mask):
    members = lax.axis_size("seq")
    mask = dp_mask * members + seq_mask
    return lax.ppermute(value, ALL, [(i, i ^ mask) for i in range(lax.axis_size("dp") * members)])


def flips(value, bits):
    for axis, bit in enumerate(bits):
        halves = [lax.slice_in_dim(value, i, i + 1, axis=axis) for i in (1, 0)]
        value = jnp.where(bit == 1, lax.concatenate(halves, axis), value)
    return value


def add16(left, right):
    return (left.astype(f32) + right.astype(f32)).astype(bf16)


def together(*values):
    return lax.optimization_barrier(values)


def all_masks():
    rows = [(1 << bit, 0) for bit in range(1, 16) if 1 << bit < lax.axis_size("dp")]
    return rows + [(1, 0), (0, 2), (0, 1)]


def gather_step(value, dp_mask, seq_mask):
    return jnp.concatenate([value, xor_both(value, dp_mask, seq_mask)])


def all_labels():
    labels = [(0, 0)]
    for dp_mask, seq_mask in all_masks():
        labels = labels + [(d ^ dp_mask, s ^ seq_mask) for d, s in labels]
    return labels


def scatter_step(total, dp_mask, seq_mask):
    half = total.shape[0] // 2
    got = xor_both(total[half:], dp_mask, seq_mask)
    total = total[:half].astype(f32) + got.astype(f32)
    return total if half == 1 else total.astype(bf16)


def gather_group(rows):
    half = rows.shape[0] // 2
    across, along = xor(rows, "seq", 2), xor(rows, "dp", 2)
    corner = [xor(across[:half], "dp", 2), xor(along[half:], "seq", 2)]
    near = [rows, across, along, *corner]
    far = [rows, jnp.concatenate([across, along]), jnp.concatenate(corner)]
    return jnp.concatenate(near + [xor(part, "seq", 1) for part in far], axis=0)


def scatter_group(total):
    parts = total.reshape(2, -1, total.shape[1])
    near = add16(parts[0], xor(parts[1], "seq", 1))
    mine, across, along, corner = jnp.split(near, 4)
    half = mine.shape[0] // 2
    low, high = xor(corner[:half], "dp", 2), xor(corner[half:], "seq", 2)
    across = jnp.concatenate([add16(across[:half], low), across[half:]])
    along = jnp.concatenate([along[:half], add16(along[half:], high)])
    return mine.astype(f32) + xor(across, "seq", 2).astype(f32) + xor(along, "dp", 2).astype(f32)


def place_kernel(sizes, target_ref, *refs):
    pieces, out = refs[: len(sizes)], refs[len(sizes)]
    buffer, arrived, left = refs[len(sizes) + 1 :]
    ins, outs, block = [], [], 0
    for piece, size in zip(pieces, sizes):
        for index in range(size):
            ins.append(pltpu.make_async_copy(piece.at[index], buffer.at[block], arrived.at[block]))
            outs.append(pltpu.make_async_copy(buffer.at[block], out.at[target_ref[block]], left.at[block]))
            ins[-1].start()
            block += 1
    for copy_in, copy_out in zip(ins, outs):
        copy_in.wait()
        copy_out.start()
    for copy_out in outs:
        copy_out.wait()


def place(pieces, targets):
    sizes = [piece.shape[0] for piece in pieces]
    shape = (sum(sizes), *pieces[0].shape[1:])
    anywhere = pl.BlockSpec(memory_space=pl.ANY)
    return pl.pallas_call(
        functools.partial(place_kernel, sizes),
        grid_spec=pltpu.PrefetchScalarGridSpec(
            num_scalar_prefetch=1,
            grid=(1,),
            in_specs=[anywhere] * len(pieces),
            out_specs=anywhere,
            scratch_shapes=[
                pltpu.VMEM(shape, pieces[0].dtype),
                pltpu.SemaphoreType.DMA((shape[0],)),
                pltpu.SemaphoreType.DMA((shape[0],)),
            ],
        ),
        out_shape=jax.ShapeDtypeStruct(shape, pieces[0].dtype),
        name="place",
        cost_estimate=pl.CostEstimate(flops=0, bytes_accessed=4 * math.prod(shape), transcendentals=0),
    )(targets, *pieces)


def project_kernel(scale, picked_ref, weight_ref, gain_ref, cos_ref, sin_ref, raw_ref, out_ref):
    raw = mm(picked_ref[...], weight_ref[...])
    raw_ref[0] = raw
    turned = rotate(raw * norm_scale(raw) * gain_ref[...], cos_ref[...], sin_ref[...]).astype(bf16)
    out_ref[...] = (turned * scale).astype(bf16).reshape(out_ref.shape)


def project(picked, weight, gain, cosine, sine):
    count, deep = picked.shape
    rows = count // 2
    same = lambda h: (0, 0)
    return pl.pallas_call(
        functools.partial(project_kernel, HEAD**-0.5),
        grid=(HEADS,),
        in_specs=[
            pl.BlockSpec((count, deep), same),
            pl.BlockSpec((deep, HEAD), lambda h: (0, h)),
            pl.BlockSpec((1, HEAD), same),
            pl.BlockSpec((count, HEAD // 2), same),
            pl.BlockSpec((count, HEAD // 2), same),
        ],
        out_specs=[
            pl.BlockSpec((1, count, HEAD), lambda h: (h, 0, 0)),
            pl.BlockSpec((2, 1, rows, HEAD), lambda h: (0, h, 0, 0)),
        ],
        out_shape=[
            jax.ShapeDtypeStruct((HEADS, count, HEAD), f32),
            jax.ShapeDtypeStruct((2, HEADS, rows, HEAD), bf16),
        ],
        name="project",
        cost_estimate=pl.CostEstimate(
            flops=2 * count * deep * HEADS * HEAD, bytes_accessed=2 * deep * HEADS * HEAD, transcendentals=0
        ),
    )(picked, weight, gain, cosine, sine)


def project_keys_kernel(picked_ref, weight_ref, gain_ref, cos_ref, sin_ref, raw_ref, out_ref):
    both = mm(picked_ref[...], weight_ref[...])
    raw = both[:, :HEAD]
    raw_ref[...] = raw
    turned = rotate(raw * norm_scale(raw) * gain_ref[...], cos_ref[...], sin_ref[...])
    both = jnp.concatenate([turned, both[:, HEAD:]], axis=1).astype(bf16)
    out_ref[...] = both.reshape(out_ref.shape)


def project_keys(picked, weight, gain, cosine, sine):
    count, deep = picked.shape
    return pl.pallas_call(
        project_keys_kernel,
        grid=(1,),
        in_specs=[
            whole_of(picked),
            whole_of(weight),
            whole_of(gain),
            whole_of(cosine),
            whole_of(sine),
        ],
        out_specs=[
            pl.BlockSpec((count, HEAD), lambda i: (0, 0)),
            pl.BlockSpec((2, count // 2, 2 * HEAD), lambda i: (0, 0, 0)),
        ],
        out_shape=[
            jax.ShapeDtypeStruct((count, HEAD), f32),
            jax.ShapeDtypeStruct((2, count // 2, 2 * HEAD), bf16),
        ],
        name="project_keys",
        cost_estimate=pl.CostEstimate(
            flops=4 * count * deep * HEAD, bytes_accessed=4 * deep * HEAD, transcendentals=0
        ),
    )(picked, weight, gain, cosine, sine)


def mask_of(meta_ref, ends_ref, unit, rows, key_stretch):
    lanes = lax.broadcasted_iota(jnp.int32, (1, HEADS * rows), 1)
    ids = meta_ref[3 * unit] + lanes % rows
    start = jnp.zeros_like(ids)
    for index in range(ends_ref.shape[0]):
        end = ends_ref[index]
        start = jnp.where(ids >= end, end, start)
    place_in = lax.broadcasted_iota(jnp.int32, (STRETCH, 1), 0)
    near = meta_ref[6] * rows
    place_in = jnp.where(place_in < rows, place_in + near, place_in - near)
    key = key_stretch * STRETCH + place_in
    return (key <= ids) & (key >= start)


def attend_kernel(
    rows, meta_ref, ends_ref, slots_ref, q_ref, near_ref, far_ref, c_ref, turned_ref, lse_ref, top, total, acc
):
    step = pl.program_id(0)

    @pl.when(step == 0)
    def _():
        top[...] = jnp.full_like(top, masked_score)
        total[...] = jnp.zeros_like(total)
        acc[...] = jnp.zeros_like(acc)

    key_stretch = slots_ref[step]
    for unit in range(2):

        @pl.when((key_stretch <= meta_ref[3 * unit + 1]) & (key_stretch >= meta_ref[3 * unit + 2]))
        def _():
            mask = mask_of(meta_ref, ends_ref, unit, rows, key_stretch)
            block = jnp.concatenate([near_ref[...], far_ref[...]], axis=0)
            query = q_ref[unit].reshape(HEADS * rows, HEAD)
            scores = jnp.where(mask, mm_nt(block[:, :HEAD], query), masked_score)
            old = top[unit]
            new = jnp.maximum(old, jnp.max(scores, axis=0, keepdims=True))
            keep = jnp.exp(old - new)
            terms = jnp.exp(scores - new)
            top[unit] = new
            total[unit] = total[unit] * keep + jnp.sum(terms, axis=0, keepdims=True)
            acc[unit] = acc[unit] * keep + mm_tn(block[:, HEAD:], terms.astype(bf16))

    @pl.when(step == pl.num_programs(0) - 1)
    def _():
        for unit in range(2):
            out = acc[unit] * (1.0 / total[unit])
            turned_ref[unit] = out
            lse_ref[unit] = top[unit] + jnp.log(total[unit])
            out = out.T.astype(bf16)
            for head in range(HEADS):
                c_ref[unit * rows : (unit + 1) * rows, head * HEAD : (head + 1) * HEAD] = out[
                    head * rows : (head + 1) * rows
                ]


def attend_back_kernel(
    rows,
    meta_ref,
    ends_ref,
    slots_ref,
    q_ref,
    dc_ref,
    lse_ref,
    turned_ref,
    raw_ref,
    gain_ref,
    cos_ref,
    sin_ref,
    near_ref,
    far_ref,
    dq_ref,
    dgain_ref,
    dnear_ref,
    dfar_ref,
    grads,
    delta,
    acc,
    both,
):
    step = pl.program_id(0)

    @pl.when(step == 0)
    def _():
        acc[...] = jnp.zeros_like(acc)
        for unit in range(2):
            for head in range(HEADS):
                grads[unit, head * rows : (head + 1) * rows] = dc_ref[
                    unit * rows : (unit + 1) * rows, head * HEAD : (head + 1) * HEAD
                ]
            across = grads[unit].astype(f32).T
            delta[unit] = jnp.sum(across * turned_ref[unit], axis=0, keepdims=True)

    key_stretch = slots_ref[step]
    both[...] = jnp.zeros_like(both)
    for unit in range(2):

        @pl.when((key_stretch <= meta_ref[3 * unit + 1]) & (key_stretch >= meta_ref[3 * unit + 2]))
        def _():
            mask = mask_of(meta_ref, ends_ref, unit, rows, key_stretch)
            block = jnp.concatenate([near_ref[...], far_ref[...]], axis=0)
            key, value = block[:, :HEAD], block[:, HEAD:]
            query = q_ref[unit].reshape(HEADS * rows, HEAD)
            grad = grads[unit]
            probs = jnp.where(mask, jnp.exp(mm_nt(key, query) - lse_ref[unit]), 0.0)
            score_grad = (probs * (mm_nt(value, grad) - delta[unit])).astype(bf16)
            acc[unit] += mm_tn(key, score_grad)
            both[:, :HEAD] += mm(score_grad, query)
            both[:, HEAD:] += mm(probs.astype(bf16), grad)

    dnear_ref[...] = both[:rows].astype(bf16)
    dfar_ref[...] = both[rows:].astype(bf16)

    @pl.when(step == pl.num_programs(0) - 1)
    def _():
        gain = gain_ref[...]
        total = jnp.zeros_like(gain)
        for unit in range(2):
            mine = slice(unit * rows, (unit + 1) * rows)
            grad = acc[unit].T * HEAD**-0.5
            for head in range(HEADS):
                back = rotate(grad[head * rows : (head + 1) * rows], cos_ref[mine], -sin_ref[mine])
                raw = raw_ref[head, mine]
                scale = norm_scale(raw)
                total = total + jnp.sum(back * raw * scale, axis=0, keepdims=True)
                back = norm_back(raw, scale, gain * back)
                dq_ref[mine, head * HEAD : (head + 1) * HEAD] = back.astype(bf16)
        dgain_ref[...] = total


def whole_of(array):
    return pl.BlockSpec(array.shape, lambda *_: (0,) * len(array.shape))


def attend(meta, ends, slots, query, near, far):
    rows = query.shape[2]
    wide = HEADS * rows
    keys = pl.BlockSpec((None, None, rows, 2 * HEAD), lambda j, *_: (j // 2, j % 2, 0, 0))
    outs = [
        jax.ShapeDtypeStruct((2 * rows, HEADS * HEAD), bf16),
        jax.ShapeDtypeStruct((2, HEAD, wide), f32),
        jax.ShapeDtypeStruct((2, 1, wide), f32),
    ]
    return pl.pallas_call(
        functools.partial(attend_kernel, rows),
        grid_spec=pltpu.PrefetchScalarGridSpec(
            num_scalar_prefetch=3,
            grid=(slots.shape[0],),
            in_specs=[whole_of(query), keys, keys],
            out_specs=[whole_of(out) for out in outs],
            scratch_shapes=[
                pltpu.VMEM((2, 1, wide), f32),
                pltpu.VMEM((2, 1, wide), f32),
                pltpu.VMEM((2, HEAD, wide), f32),
            ],
        ),
        out_shape=outs,
        name="attend",
        cost_estimate=pl.CostEstimate(
            flops=4 * 2 * 9 * STRETCH * wide * HEAD,
            bytes_accessed=4 * near.size,
            transcendentals=2 * 9 * STRETCH * wide,
        ),
    )(meta, ends, slots, query, near, far)


def attend_back(meta, ends, slots, query, grad, lse, turned, raw, gain, cosine, sine, near, far):
    rows = query.shape[2]
    wide = HEADS * rows
    keys = pl.BlockSpec((None, None, rows, 2 * HEAD), lambda j, *_: (j // 2, j % 2, 0, 0))
    fixed = [query, grad, lse, turned, raw, gain, cosine, sine]
    outs = [jax.ShapeDtypeStruct(grad.shape, bf16), jax.ShapeDtypeStruct(gain.shape, f32)]
    return pl.pallas_call(
        functools.partial(attend_back_kernel, rows),
        grid_spec=pltpu.PrefetchScalarGridSpec(
            num_scalar_prefetch=3,
            grid=(slots.shape[0],),
            in_specs=[*[whole_of(array) for array in fixed], keys, keys],
            out_specs=[*[whole_of(out) for out in outs], keys, keys],
            scratch_shapes=[
                pltpu.VMEM((2, wide, HEAD), bf16),
                pltpu.VMEM((2, 1, wide), f32),
                pltpu.VMEM((2, HEAD, wide), f32),
                pltpu.VMEM((STRETCH, 2 * HEAD), f32),
            ],
        ),
        out_shape=[*outs, jax.ShapeDtypeStruct(near.shape, bf16), jax.ShapeDtypeStruct(near.shape, bf16)],
        name="attend_back",
        cost_estimate=pl.CostEstimate(
            flops=10 * 2 * 9 * STRETCH * wide * HEAD,
            bytes_accessed=8 * near.size,
            transcendentals=2 * 9 * STRETCH * wide,
        ),
    )(meta, ends, slots, *fixed, near, far)


def blocks_of(tops, low, member, members, ff):
    return [(((hi * 2 + low) * 2 + y) * members + member) * ff for hi in range(tops) for y in range(2)]

def pack_kernel(tops, members, ff, gate_ref, up_ref, out_ref):
    for which, ref in enumerate((gate_ref, up_ref)):
        value = ref[...]
        for low in range(2):
            for member in range(members):
                cuts = [value[:, at : at + ff] for at in blocks_of(tops, low, member, members, ff)]
                out_ref[low, member, which] = jnp.concatenate(cuts, axis=1)

def pack(gate, up, tops, members, ff):
    rows = gate.shape[0]
    return pl.pallas_call(functools.partial(pack_kernel, tops, members, ff),
        out_shape=jax.ShapeDtypeStruct((2, members, 2, rows, 2 * tops * ff), bf16), name="pack")(gate, up)

def unpack_kernel(tops, members, ff, low_ref, in_ref, gate_ref, up_ref):
    for which, ref in enumerate((gate_ref, up_ref)):
        pieces = [None] * (2 * tops * 2 * members)
        for low in range(2):
            for member in range(members):
                value = in_ref[member, low_ref[0] ^ low, which].astype(f32)
                for i, at in enumerate(blocks_of(tops, low, member, members, ff)):
                    pieces[at // ff] = value[:, i * ff : (i + 1) * ff]
        ref[...] = jnp.concatenate(pieces, axis=1)

def unpack(moved, low_bit, tops, members, ff):
    rows = moved.shape[3]
    shape = jax.ShapeDtypeStruct((rows, 4 * tops * members * ff), f32)
    return pl.pallas_call(functools.partial(unpack_kernel, tops, members, ff),
        in_specs=[pl.BlockSpec(memory_space=pltpu.SMEM), pl.BlockSpec(memory_space=pltpu.VMEM)],
        out_shape=[shape, shape], name="unpack")(low_bit[None], moved)

def merge_kernel(in_ref, gate_ref, up_ref):
    for which, ref in enumerate((gate_ref, up_ref)):
        for low in range(2):
            ref[low] = jnp.concatenate([in_ref[m, low, which] for m in range(in_ref.shape[0])], axis=0)

def merge(moved):
    members, _, _, rows, wide = moved.shape
    shape = jax.ShapeDtypeStruct((2, members * rows, wide), bf16)
    return pl.pallas_call(merge_kernel, out_shape=[shape, shape], name="merge")(moved)

def split_kernel(gate_ref, up_ref, out_ref):
    members, rows = out_ref.shape[1], out_ref.shape[3]
    for which, ref in enumerate((gate_ref, up_ref)):
        for low in range(2):
            value = ref[low]
            for m in range(members):
                out_ref[low, m, which] = value[m * rows : (m + 1) * rows]

def split(gate, up, members):
    _, tall, wide = gate.shape
    return pl.pallas_call(split_kernel,
        out_shape=jax.ShapeDtypeStruct((2, members, 2, tall // members, wide), bf16), name="split")(gate, up)


def per_device(
    inputs,
    cotangent,
    lengths,
    deal,
    w_query,
    w_key,
    w_value,
    w_out,
    w_gate,
    w_up,
    w_down,
    gain_attn_pre,
    gain_attn_post,
    gain_ffw_pre,
    gain_ffw_post,
    gain_query,
    gain_key,
):
    rows, width = inputs.shape[1], inputs.shape[2]
    groups, members = lax.axis_size("dp"), lax.axis_size("seq")
    devices = groups * members
    total_rows = rows * devices
    dp_id, seq_id = lax.axis_index("dp"), lax.axis_index("seq")
    half_bit, x_bit, y_bit, z_bit = seq_id % 2, seq_id // 2, dp_id % 2, dp_id // 2 % 2
    tops = groups // 4
    count = 2 * rows
    model_rows, out_rows, ff_rows = w_query.shape[0], w_out.shape[0], w_down.shape[0]
    ff_local = 2 * tops * ff_rows
    wide_q = HEADS * HEAD
    gain_sizes = [gain_attn_pre.shape[0]] * 4 + [gain_query.shape[0]] * 2
    gain_total = sum(gain_sizes)
    block_rows = (model_rows + 8) // 8 * 8

    def regroup(array):
        kept = lax.dynamic_index_in_dim(array, y_bit, 0, keepdims=False)
        sent = lax.dynamic_index_in_dim(array, 1 - y_bit, 0, keepdims=False)
        return jnp.concatenate([kept, xor(sent, "dp", 1)], axis=0)

    def ungroup(array):
        kept, sent = array[:rows], array[rows:]
        return flips(jnp.stack([kept, xor(sent, "dp", 1)]), [y_bit])


    def column_exchange(packed):
        kept = lax.dynamic_index_in_dim(packed, z_bit, 0, keepdims=False)
        sent = lax.dynamic_index_in_dim(packed, 1 - z_bit, 0, keepdims=False)
        return jnp.stack([kept, xor(sent, "dp", 2)], axis=1)

    def swap_members(parts):
        return lax.all_to_all(parts, "seq", split_axis=0, concat_axis=0, tiled=True)

    gain_line, at = jnp.zeros((1, 2 * HEAD), f32), 0
    for gain in (gain_attn_pre, gain_attn_post, gain_ffw_pre, gain_ffw_post, gain_query, gain_key):
        gain_line += jnp.pad(gain.astype(f32)[None, :], ((0, 0), (at, gain_line.shape[1] - at - gain.shape[0])))
        at += gain.shape[0]
    shard = jnp.concatenate([jnp.concatenate([w_key, w_value], axis=1), gain_line.astype(bf16)], axis=0)
    blocks = jnp.pad(shard, ((0, block_rows - model_rows - 1), (0, 0)))[None]
    q_blocks = jnp.pad(w_query, ((0, block_rows - model_rows), (0, 0)))[None]
    packed = pack(w_gate, w_up, tops, members, ff_rows)
    first_mask, *more_masks, x_mask, core_mask = all_masks()
    blocks = gather_step(blocks, *first_mask)
    last_mask = first_mask
    for masks in [*more_masks, x_mask]:
        blocks, q_blocks = together(gather_step(blocks, *masks), gather_step(q_blocks, *last_mask))
        last_mask = masks
    blocks, packed, down_piece, rows_low = together(blocks, packed, w_down[None], regroup(inputs))
    rows_in = rows_low.astype(f32)
    q_blocks = gather_step(q_blocks, *x_mask)
    blocks = gather_step(blocks, *core_mask)
    kv_weight = blocks.reshape(devices * block_rows, 2 * HEAD)
    labels = all_labels()
    natural = jnp.stack([(dp_id ^ d) * members + (seq_id ^ s) for d, s in labels]).astype(jnp.int32)

    def selection(order, size, block, padded):
        within = jnp.arange(padded, dtype=jnp.int32)
        source = jnp.where(within < block, order[:, None] * block + within, -1).reshape(-1)
        return (jnp.arange(size, dtype=jnp.int32)[:, None] == source[None, :]).astype(bf16)

    model_pick = selection(natural, width, model_rows, block_rows)
    device_pick = selection(natural, devices, 1, 1)
    out_pick = selection(natural, wide_q, out_rows, block_rows)
    gain_blocks = blocks[:, model_rows, :gain_total]
    gain_all = mm(device_pick, gain_blocks)
    full_gain, at = [], 0
    for size in gain_sizes:
        full_gain.append(gain_all[:, at : at + size].reshape(devices * size))
        at += size
    pre_attention, post_attention, pre_feed, post_feed, query_gain, key_gain = full_gain

    top_id = dp_id // 4

    def from_tops(piece):
        return [piece] + [xor(piece, "dp", 4 * k) for k in range(1, tops)]

    def both_sides(tall):
        return tall + [xor(part, "dp", 1) for part in tall]

    owners = [(top_id ^ k) * 2 + (y_bit ^ u) for u in range(2) for k in range(tops)]
    owners = jnp.stack(owners).astype(jnp.int32)
    sources = [((top_id ^ k) * 2 + (z_bit ^ v)) * 2 + (y_bit ^ u) for u in range(2) for k in range(tops) for v in range(2)]
    sources = jnp.stack(sources).astype(jnp.int32)

    down_tall = from_tops(down_piece)

    seq_ends = jnp.cumsum(lax.dynamic_index_in_dim(lengths, y_bit, 0, keepdims=False))
    dealt = lax.dynamic_index_in_dim(deal, y_bit, 0, keepdims=False)
    unit_ids = jnp.stack([(dp_id ^ u) * members + seq_id for u in range(2)])
    stretches = dealt[unit_ids * rows // STRETCH]
    first_rows = stretches * STRETCH + unit_ids * rows % STRETCH
    my_rows = (first_rows[:, None] + jnp.arange(rows, dtype=jnp.int32)).reshape(count)
    starts = layout_start(seq_ends, my_rows)
    lows = starts.reshape(2, rows)[:, 0] // STRETCH
    meta = jnp.concatenate([jnp.stack([first_rows, stretches, lows], axis=1).reshape(-1), half_bit[None]])
    layers = groups // 2
    slot_ids = jnp.stack(
        [
            ((dp_id // 2 ^ z) * 2 + (y_bit ^ u)) * (members // 2) + (x_bit ^ x)
            for x in range(2)
            for z in range(layers)
            for u in range(2)
        ]
    )
    slots = dealt[slot_ids]
    positions = my_rows - starts
    valid = (my_rows < total_rows - STRETCH)[:, None]
    freqs = rope_base ** (-2.0 * jnp.arange(HEAD // 2, dtype=f32) / HEAD)
    angle = positions.astype(f32)[:, None] * freqs
    cosine, sine = jnp.cos(angle), jnp.sin(angle)

    scale_one = norm_scale(rows_in)
    normed_one = (rows_in * scale_one * pre_attention).astype(bf16)
    picked_one = mm(normed_one, model_pick).astype(bf16)
    key_raw, keys_mine = project_keys(picked_one, kv_weight, key_gain[None], cosine, sine)
    column = [keys_mine] + [xor(keys_mine, "dp", 2 * k) for k in range(1, layers)]
    key_raw, packed = together(key_raw, packed)
    column_parts = column_exchange(packed)
    others, down_tall, column_parts, late_out, q_blocks = together(column[1:], down_tall, column_parts, w_out, q_blocks)
    column = [column[0], *others]
    out_weight = lax.all_gather(late_out, ALL, axis=0, tiled=True)
    halves = merge(swap_members(column_parts))
    q_weight = gather_step(q_blocks, *core_mask).reshape(devices * block_rows, wide_q)
    gate_tall, up_half = together(from_tops(halves[0]), halves[1])
    up_tall = from_tops(up_half)
    across = [xor(part, "seq", 2) for part in column]
    down_pieces = both_sides(down_tall)
    column, across = jnp.stack(column), jnp.stack(across)
    near_keys = jnp.concatenate([column, across])
    far_keys = jnp.concatenate([xor(column, "seq", 1), xor(across, "seq", 1)])
    query_raw, query_heads = project(picked_one, q_weight, query_gain[None], cosine, sine)
    query_heads, gate_tall = together(query_heads, gate_tall)
    gate_pieces = both_sides(gate_tall)
    context_rows, turned, lse = attend(meta, seq_ends, slots, query_heads, near_keys, far_keys)
    context_rows, gate_pieces, up_tall, down_pieces = together(context_rows, gate_pieces, up_tall, down_pieces)
    picked_context = mm(context_rows, out_pick).astype(bf16)
    up_pieces = both_sides(up_tall)
    down_weight = place(down_pieces, owners).reshape(ff_local, width)
    gate_weight, up_weight = [place(pieces, sources).reshape(width, ff_local) for pieces in (gate_pieces, up_pieces)]
    attended = mm(context_rows, out_weight)
    scale_two = norm_scale(attended)
    hidden_res = rows_in + attended * scale_two * post_attention
    scale_three = norm_scale(hidden_res)
    normed_two = (hidden_res * scale_three * pre_feed).astype(bf16)

    normed_group = gather_group(normed_two)
    gate_raw = mm(normed_group, gate_weight)
    up_raw = mm(normed_group, up_weight)
    hidden_low = (jax.nn.gelu(gate_raw, approximate=True) * up_raw).astype(bf16)
    mixed = scatter_group(mm(hidden_low, down_weight).astype(bf16))
    q_natural, kv_natural = mm(model_pick, q_weight).astype(bf16), mm(model_pick, kv_weight).astype(bf16)
    q_natural, kv_natural, picked_context, mixed = together(q_natural, kv_natural, picked_context, mixed)
    scale_four = norm_scale(mixed)
    result = hidden_res + mixed * scale_four * post_feed
    result = jnp.where(valid, result, 0.0).astype(bf16)

    upstream = jnp.where(valid, regroup(cotangent).astype(f32), 0.0)
    grad_post_feed = jnp.sum(upstream * mixed * scale_four, axis=0)
    mixed_grad = norm_back(mixed, scale_four, post_feed * upstream).astype(bf16)
    mixed_group = gather_group(mixed_grad)
    hidden_grad = mm_nt(mixed_group, down_weight)
    _, gelu_pull = jax.vjp(lambda g, u: jax.nn.gelu(g, approximate=True) * u, gate_raw, up_raw)
    gate_grad, up_grad = gelu_pull(hidden_grad)
    gate_grad, up_grad = gate_grad.astype(bf16), up_grad.astype(bf16)
    partial_grad = (mm_nt(gate_grad, gate_weight) + mm_nt(up_grad, up_weight)).astype(bf16)
    hidden_low, mixed_group, normed_group, gate_grad, up_grad, partial_grad = together(
        hidden_low, mixed_group, normed_group, gate_grad, up_grad, partial_grad
    )
    normed_two_grad = scatter_group(partial_grad)
    grad_pre_feed = jnp.sum(normed_two_grad * hidden_res * scale_three, axis=0)
    hidden_res_grad = upstream + norm_back(hidden_res, scale_three, pre_feed * normed_two_grad)

    def halve(total):
        kept = lax.dynamic_index_in_dim(total, y_bit, 2, keepdims=False)
        return kept, xor(lax.dynamic_index_in_dim(total, 1 - y_bit, 2, keepdims=False), "dp", 1)

    def by_top(kept, got):
        kept = add16(kept, got)
        return [lax.dynamic_index_in_dim(kept, top_id ^ k, 0, keepdims=False) for k in range(tops)]

    def send_tops(parts):
        return [part if k == 0 else xor(part, "dp", 4 * k) for k, part in enumerate(parts)]

    def total_of(parts):
        return functools.reduce(jnp.add, [part.astype(f32) for part in parts])

    def column_blocks(total):
        total = with_layout_constraint(total.astype(bf16), Layout((0, 1)))
        return total.reshape(tops, 2, 2, members * model_rows, ff_local)

    down_halves = halve(mm_tn(hidden_low, mixed_group).astype(bf16).reshape(tops, 1, 2, ff_rows, width))
    down_kept, gate_grad = together(down_halves[0], gate_grad)
    gate_halves = halve(column_blocks(mm_tn(normed_group, gate_grad)))
    gate_kept, down_got, up_grad = together(gate_halves[0], down_halves[1], up_grad)
    up_halves = halve(column_blocks(mm_tn(normed_group, up_grad)))
    down_halves, gate_halves = (down_kept, down_got), (gate_kept, gate_halves[1])

    grad_post_attention = jnp.sum(hidden_res_grad * attended * scale_two, axis=0)
    attended_grad = norm_back(attended, scale_two, post_attention * hidden_res_grad).astype(bf16)
    out_total = mm_tn(picked_context, attended_grad).astype(bf16)
    attended_grad, out_total, gate_kept, up_kept = lax.optimization_barrier(
        (attended_grad, out_total, gate_halves[0], up_halves[0])
    )
    gate_halves, up_halves = (gate_kept, gate_halves[1]), (up_kept, up_halves[1])
    down_parts = send_tops(by_top(*down_halves))
    context_grad = mm_nt(attended_grad, out_weight).astype(bf16)
    query_grad, grad_query_gain, near_part, far_part = attend_back(
        meta, seq_ends, slots, query_heads, context_grad, lse, turned, query_raw, query_gain[None], cosine, sine, near_keys, far_keys
    )
    far_part, near_part, gate_halves, up_halves, down_parts = together(
        far_part, near_part, gate_halves, up_halves, down_parts
    )
    far_part = xor(far_part, "seq", 1)
    query_low, far_part, gate_tops, up_tops = together(query_grad, far_part, by_top(*gate_halves), by_top(*up_halves))
    gate_parts, up_parts = send_tops(gate_tops), send_tops(up_tops)
    near_part = add16(near_part, far_part).reshape(2, layers, count, 2 * HEAD)
    near_part = add16(near_part[0], xor(near_part[1], "seq", 2))
    grad_query = jnp.concatenate([mm_tn(picked_one, query_low).astype(bf16), out_total], axis=1)
    grad_query = grad_query.reshape(devices, block_rows, wide_q + width)
    grad_query, near_part, gate_parts = together(scatter_step(grad_query, *core_mask), near_part, gate_parts)
    grad_query = scatter_step(grad_query, *x_mask)
    key_parts = [near_part[k] if k == 0 else xor(near_part[k], "dp", 2 * k) for k in range(layers)]
    key_parts, up_parts = together(key_parts, up_parts)
    key_grads = functools.reduce(jnp.add, [part.astype(f32) for part in key_parts])
    value_grad = key_grads[:, HEAD:].astype(bf16)
    key_turned = rotate(key_grads[:, :HEAD], cosine, -sine)
    key_scale = norm_scale(key_raw)
    grad_key_gain = jnp.sum(key_turned * key_raw * key_scale, axis=0)
    key_grad = norm_back(key_raw, key_scale, key_gain * key_turned).astype(bf16)
    kv_grad = jnp.concatenate([key_grad, value_grad], axis=1)
    normed_one_grad = mm_nt(query_grad, q_natural) + mm_nt(kv_grad, kv_natural)
    grad_pre_attention = jnp.sum(normed_one_grad * rows_in * scale_one, axis=0)
    rows_grad = hidden_res_grad + norm_back(rows_in, scale_one, pre_attention * normed_one_grad)
    rows_low, result, down_parts, gate_parts, up_parts = together(
        rows_grad.astype(bf16), result, down_parts, gate_parts, up_parts
    )
    output = ungroup(result)
    grad_down = total_of(down_parts)[0]
    both_grads = split(total_of(gate_parts).astype(bf16), total_of(up_parts).astype(bf16), members)
    input_grad = ungroup(rows_low)
    grad_kv = mm_tn(picked_one, kv_grad).reshape(devices, block_rows, 2 * HEAD)
    gain_grads = [
        grad_pre_attention,
        grad_post_attention,
        grad_pre_feed,
        grad_post_feed,
        grad_query_gain,
        grad_key_gain,
    ]
    gain_grads = jnp.concatenate([g.reshape(devices, -1) for g in gain_grads], axis=1)
    gain_grads = mm_tn(device_pick, gain_grads.astype(bf16))
    gain_grads = jnp.pad(
        gain_grads[:, None, :], ((0, 0), (model_rows, block_rows - model_rows - 1), (0, 2 * HEAD - gain_total))
    )
    last, grad_query = together(scatter_step((grad_kv + gain_grads).astype(bf16), *core_mask), grad_query)
    rest = [*reversed(more_masks), first_mask]
    last, grad_query, column_parts = together(
        scatter_step(last, *x_mask), scatter_step(grad_query, *rest[0]), column_exchange(both_grads)
    )
    column_parts = swap_members(column_parts)
    for masks, ahead in zip(rest[:-1], rest[1:]):
        last, grad_query, column_parts = together(
            scatter_step(last, *masks), scatter_step(grad_query, *ahead), column_parts
        )
    grad_gate, grad_up = unpack(column_parts, z_bit, tops, members, ff_rows)
    last = scatter_step(last, *first_mask)[0]
    grad_query, grad_out = grad_query[0, :model_rows, :wide_q], grad_query[0, :out_rows, wide_q:]
    gain_out, at = [], 0
    for size in gain_sizes:
        gain_out.append(last[model_rows, at : at + size])
        at += size
    return (
        output,
        input_grad,
        grad_query,
        last[:model_rows, :HEAD],
        last[:model_rows, HEAD:],
        grad_out,
        grad_gate,
        grad_up,
        grad_down,
        *gain_out,
    )


def solution(mesh):
    split = P(None, ALL, None)
    weight, gain = P(ALL, None), P(ALL)
    return jax.shard_map(
        per_device,
        mesh=mesh,
        in_specs=(split, split, P(), P(), *[weight] * 7, *[gain] * 6),
        out_specs=(split, split, *[weight] * 7, *[gain] * 6),
        check_vma=False,
    )
```

```python
import functools
import math

import jax
import jax.numpy as jnp
from jax import lax
from jax.experimental import pallas as pl
from jax.experimental.layout import Layout, with_layout_constraint
from jax.experimental.pallas import tpu as pltpu
from jax.sharding import PartitionSpec as P

HEADS = 4
HEAD = 256
MB = 2
STRETCH = 256

eps = 1e-06
rope_base = 1000000.0
masked_score = -1e30
bf16 = jnp.bfloat16
f32 = jnp.float32
ALL = ("dp", "seq")


def norm_scale(values):
    return lax.rsqrt(jnp.mean(values * values, axis=-1, keepdims=True) + eps)


def norm_back(values, scale, weighted):
    return scale * weighted - values * (scale * scale * scale) * jnp.mean(
        weighted * values, axis=-1, keepdims=True
    )


def rotate(values, cosine, sine):
    first, second = jnp.split(values, 2, axis=-1)
    return jnp.concatenate([first * cosine - second * sine, second * cosine + first * sine], axis=-1)


def layout_start(ends, row_ids):
    after = row_ids[:, None] >= ends[None, :]
    return jnp.max(jnp.where(after, ends[None, :], 0), axis=1)


def dot(left, right, dims):
    return lax.dot_general(left, right, (dims, ((), ())), preferred_element_type=f32)


def mm(left, right):
    return dot(left, right, ((1,), (0,)))


def mm_tn(left, right):
    return dot(left, right, ((0,), (0,)))


def mm_nt(left, right):
    return dot(left, right, ((1,), (1,)))


def xor(value, axis, mask):
    return lax.ppermute(value, axis, [(i, i ^ mask) for i in range(lax.axis_size(axis))])


def xor_both(value, dp_mask, seq_mask):
    members = lax.axis_size("seq")
    mask = dp_mask * members + seq_mask
    return lax.ppermute(value, ALL, [(i, i ^ mask) for i in range(lax.axis_size("dp") * members)])


def flips(value, bits):
    for axis, bit in enumerate(bits):
        halves = [lax.slice_in_dim(value, i, i + 1, axis=axis) for i in (1, 0)]
        value = jnp.where(bit == 1, lax.concatenate(halves, axis), value)
    return value


def add16(left, right):
    return (left.astype(f32) + right.astype(f32)).astype(bf16)


def together(*values):
    return lax.optimization_barrier(values)


def all_masks():
    rows = [(1 << bit, 0) for bit in range(1, 16) if 1 << bit < lax.axis_size("dp")]
    return rows + [(1, 0), (0, 2), (0, 1)]


def gather_step(value, dp_mask, seq_mask):
    return jnp.concatenate([value, xor_both(value, dp_mask, seq_mask)])


def all_labels():
    labels = [(0, 0)]
    for dp_mask, seq_mask in all_masks():
        labels = labels + [(d ^ dp_mask, s ^ seq_mask) for d, s in labels]
    return labels


def scatter_step(total, dp_mask, seq_mask):
    half = total.shape[0] // 2
    got = xor_both(total[half:], dp_mask, seq_mask)
    total = total[:half].astype(f32) + got.astype(f32)
    return total if half == 1 else total.astype(bf16)


def scatter_rest(total):
    for masks in list(reversed(all_masks()))[1:]:
        total = scatter_step(total, *masks)
    return total[0]


def gather_group(rows):
    half = rows.shape[0] // 2
    across, along = xor(rows, "seq", 2), xor(rows, "dp", 2)
    corner = [xor(across[:half], "dp", 2), xor(along[half:], "seq", 2)]
    near = [rows, across, along, *corner]
    far = [rows, jnp.concatenate([across, along]), jnp.concatenate(corner)]
    return jnp.concatenate(near + [xor(part, "seq", 1) for part in far], axis=0)


def scatter_group(total):
    parts = total.reshape(2, -1, total.shape[1])
    near = add16(parts[0], xor(parts[1], "seq", 1))
    mine, across, along, corner = jnp.split(near, 4)
    half = mine.shape[0] // 2
    low, high = xor(corner[:half], "dp", 2), xor(corner[half:], "seq", 2)
    across = jnp.concatenate([add16(across[:half], low), across[half:]])
    along = jnp.concatenate([along[:half], add16(along[half:], high)])
    return mine.astype(f32) + xor(across, "seq", 2).astype(f32) + xor(along, "dp", 2).astype(f32)


def place_kernel(sizes, target_ref, *refs):
    pieces, out = refs[: len(sizes)], refs[len(sizes)]
    buffer, arrived, left = refs[len(sizes) + 1 :]
    ins, outs, block = [], [], 0
    for piece, size in zip(pieces, sizes):
        for index in range(size):
            ins.append(pltpu.make_async_copy(piece.at[index], buffer.at[block], arrived.at[block]))
            outs.append(pltpu.make_async_copy(buffer.at[block], out.at[target_ref[block]], left.at[block]))
            ins[-1].start()
            block += 1
    for copy_in, copy_out in zip(ins, outs):
        copy_in.wait()
        copy_out.start()
    for copy_out in outs:
        copy_out.wait()


def place(pieces, targets):
    sizes = [piece.shape[0] for piece in pieces]
    shape = (sum(sizes), *pieces[0].shape[1:])
    anywhere = pl.BlockSpec(memory_space=pl.ANY)
    return pl.pallas_call(
        functools.partial(place_kernel, sizes),
        grid_spec=pltpu.PrefetchScalarGridSpec(
            num_scalar_prefetch=1,
            grid=(1,),
            in_specs=[anywhere] * len(pieces),
            out_specs=anywhere,
            scratch_shapes=[
                pltpu.VMEM(shape, pieces[0].dtype),
                pltpu.SemaphoreType.DMA((shape[0],)),
                pltpu.SemaphoreType.DMA((shape[0],)),
            ],
        ),
        out_shape=jax.ShapeDtypeStruct(shape, pieces[0].dtype),
        name="place",
        cost_estimate=pl.CostEstimate(flops=0, bytes_accessed=4 * math.prod(shape), transcendentals=0),
    )(targets, *pieces)


def project_kernel(scale, picked_ref, weight_ref, gain_ref, cos_ref, sin_ref, raw_ref, out_ref):
    raw = mm(picked_ref[...], weight_ref[...])
    raw_ref[0] = raw
    turned = rotate(raw * norm_scale(raw) * gain_ref[...], cos_ref[...], sin_ref[...]).astype(bf16)
    out_ref[...] = (turned * scale).astype(bf16).reshape(out_ref.shape)


def project(picked, weight, gain, cosine, sine):
    count, deep = picked.shape
    rows = count // 2
    same = lambda h: (0, 0)
    return pl.pallas_call(
        functools.partial(project_kernel, HEAD**-0.5),
        grid=(HEADS,),
        in_specs=[
            pl.BlockSpec((count, deep), same),
            pl.BlockSpec((deep, HEAD), lambda h: (0, h)),
            pl.BlockSpec((1, HEAD), same),
            pl.BlockSpec((count, HEAD // 2), same),
            pl.BlockSpec((count, HEAD // 2), same),
        ],
        out_specs=[
            pl.BlockSpec((1, count, HEAD), lambda h: (h, 0, 0)),
            pl.BlockSpec((2, 1, rows, HEAD), lambda h: (0, h, 0, 0)),
        ],
        out_shape=[
            jax.ShapeDtypeStruct((HEADS, count, HEAD), f32),
            jax.ShapeDtypeStruct((2, HEADS, rows, HEAD), bf16),
        ],
        name="project",
        cost_estimate=pl.CostEstimate(
            flops=2 * count * deep * HEADS * HEAD, bytes_accessed=2 * deep * HEADS * HEAD, transcendentals=0
        ),
    )(picked, weight, gain, cosine, sine)


def project_keys_kernel(picked_ref, weight_ref, gain_ref, cos_ref, sin_ref, raw_ref, out_ref):
    both = mm(picked_ref[...], weight_ref[...])
    raw = both[:, :HEAD]
    raw_ref[...] = raw
    turned = rotate(raw * norm_scale(raw) * gain_ref[...], cos_ref[...], sin_ref[...])
    both = jnp.concatenate([turned, both[:, HEAD:]], axis=1).astype(bf16)
    out_ref[...] = both.reshape(out_ref.shape)


def project_keys(picked, weight, gain, cosine, sine):
    count, deep = picked.shape
    return pl.pallas_call(
        project_keys_kernel,
        grid=(1,),
        in_specs=[
            whole_of(picked),
            whole_of(weight),
            whole_of(gain),
            whole_of(cosine),
            whole_of(sine),
        ],
        out_specs=[
            pl.BlockSpec((count, HEAD), lambda i: (0, 0)),
            pl.BlockSpec((2, count // 2, 2 * HEAD), lambda i: (0, 0, 0)),
        ],
        out_shape=[
            jax.ShapeDtypeStruct((count, HEAD), f32),
            jax.ShapeDtypeStruct((2, count // 2, 2 * HEAD), bf16),
        ],
        name="project_keys",
        cost_estimate=pl.CostEstimate(
            flops=4 * count * deep * HEAD, bytes_accessed=4 * deep * HEAD, transcendentals=0
        ),
    )(picked, weight, gain, cosine, sine)


def mask_of(meta_ref, ends_ref, unit, rows, key_stretch):
    lanes = lax.broadcasted_iota(jnp.int32, (1, HEADS * rows), 1)
    ids = meta_ref[3 * unit] + lanes % rows
    start = jnp.zeros_like(ids)
    for index in range(ends_ref.shape[0]):
        end = ends_ref[index]
        start = jnp.where(ids >= end, end, start)
    place_in = lax.broadcasted_iota(jnp.int32, (STRETCH, 1), 0)
    near = meta_ref[6] * rows
    place_in = jnp.where(place_in < rows, place_in + near, place_in - near)
    key = key_stretch * STRETCH + place_in
    return (key <= ids) & (key >= start)


def attend_kernel(
    rows, meta_ref, ends_ref, slots_ref, q_ref, near_ref, far_ref, c_ref, turned_ref, lse_ref, top, total, acc
):
    step = pl.program_id(0)

    @pl.when(step == 0)
    def _():
        top[...] = jnp.full_like(top, masked_score)
        total[...] = jnp.zeros_like(total)
        acc[...] = jnp.zeros_like(acc)

    key_stretch = slots_ref[step]
    for unit in range(2):

        @pl.when((key_stretch <= meta_ref[3 * unit + 1]) & (key_stretch >= meta_ref[3 * unit + 2]))
        def _():
            mask = mask_of(meta_ref, ends_ref, unit, rows, key_stretch)
            block = jnp.concatenate([near_ref[...], far_ref[...]], axis=0)
            query = q_ref[unit].reshape(HEADS * rows, HEAD)
            scores = jnp.where(mask, mm_nt(block[:, :HEAD], query), masked_score)
            old = top[unit]
            new = jnp.maximum(old, jnp.max(scores, axis=0, keepdims=True))
            keep = jnp.exp(old - new)
            terms = jnp.exp(scores - new)
            top[unit] = new
            total[unit] = total[unit] * keep + jnp.sum(terms, axis=0, keepdims=True)
            acc[unit] = acc[unit] * keep + mm_tn(block[:, HEAD:], terms.astype(bf16))

    @pl.when(step == pl.num_programs(0) - 1)
    def _():
        for unit in range(2):
            out = acc[unit] * (1.0 / total[unit])
            turned_ref[unit] = out
            lse_ref[unit] = top[unit] + jnp.log(total[unit])
            out = out.T.astype(bf16)
            for head in range(HEADS):
                c_ref[unit * rows : (unit + 1) * rows, head * HEAD : (head + 1) * HEAD] = out[
                    head * rows : (head + 1) * rows
                ]


def attend_back_kernel(
    rows,
    meta_ref,
    ends_ref,
    slots_ref,
    q_ref,
    dc_ref,
    lse_ref,
    turned_ref,
    raw_ref,
    gain_ref,
    cos_ref,
    sin_ref,
    near_ref,
    far_ref,
    dq_ref,
    dgain_ref,
    dnear_ref,
    dfar_ref,
    grads,
    delta,
    acc,
    both,
):
    step = pl.program_id(0)

    @pl.when(step == 0)
    def _():
        acc[...] = jnp.zeros_like(acc)
        for unit in range(2):
            for head in range(HEADS):
                grads[unit, head * rows : (head + 1) * rows] = dc_ref[
                    unit * rows : (unit + 1) * rows, head * HEAD : (head + 1) * HEAD
                ]
            across = grads[unit].astype(f32).T
            delta[unit] = jnp.sum(across * turned_ref[unit], axis=0, keepdims=True)

    key_stretch = slots_ref[step]
    both[...] = jnp.zeros_like(both)
    for unit in range(2):

        @pl.when((key_stretch <= meta_ref[3 * unit + 1]) & (key_stretch >= meta_ref[3 * unit + 2]))
        def _():
            mask = mask_of(meta_ref, ends_ref, unit, rows, key_stretch)
            block = jnp.concatenate([near_ref[...], far_ref[...]], axis=0)
            key, value = block[:, :HEAD], block[:, HEAD:]
            query = q_ref[unit].reshape(HEADS * rows, HEAD)
            grad = grads[unit]
            probs = jnp.where(mask, jnp.exp(mm_nt(key, query) - lse_ref[unit]), 0.0)
            score_grad = (probs * (mm_nt(value, grad) - delta[unit])).astype(bf16)
            acc[unit] += mm_tn(key, score_grad)
            both[:, :HEAD] += mm(score_grad, query)
            both[:, HEAD:] += mm(probs.astype(bf16), grad)

    dnear_ref[...] = both[:rows].astype(bf16)
    dfar_ref[...] = both[rows:].astype(bf16)

    @pl.when(step == pl.num_programs(0) - 1)
    def _():
        gain = gain_ref[...]
        total = jnp.zeros_like(gain)
        for unit in range(2):
            mine = slice(unit * rows, (unit + 1) * rows)
            grad = acc[unit].T * HEAD**-0.5
            for head in range(HEADS):
                back = rotate(grad[head * rows : (head + 1) * rows], cos_ref[mine], -sin_ref[mine])
                raw = raw_ref[head, mine]
                scale = norm_scale(raw)
                total = total + jnp.sum(back * raw * scale, axis=0, keepdims=True)
                back = norm_back(raw, scale, gain * back)
                dq_ref[mine, head * HEAD : (head + 1) * HEAD] = back.astype(bf16)
        dgain_ref[...] = total


def whole_of(array):
    return pl.BlockSpec(array.shape, lambda *_: (0,) * len(array.shape))


def attend(meta, ends, slots, query, near, far):
    rows = query.shape[2]
    wide = HEADS * rows
    keys = pl.BlockSpec((None, None, rows, 2 * HEAD), lambda j, *_: (j // 2, j % 2, 0, 0))
    outs = [
        jax.ShapeDtypeStruct((2 * rows, HEADS * HEAD), bf16),
        jax.ShapeDtypeStruct((2, HEAD, wide), f32),
        jax.ShapeDtypeStruct((2, 1, wide), f32),
    ]
    return pl.pallas_call(
        functools.partial(attend_kernel, rows),
        grid_spec=pltpu.PrefetchScalarGridSpec(
            num_scalar_prefetch=3,
            grid=(slots.shape[0],),
            in_specs=[whole_of(query), keys, keys],
            out_specs=[whole_of(out) for out in outs],
            scratch_shapes=[
                pltpu.VMEM((2, 1, wide), f32),
                pltpu.VMEM((2, 1, wide), f32),
                pltpu.VMEM((2, HEAD, wide), f32),
            ],
        ),
        out_shape=outs,
        name="attend",
        cost_estimate=pl.CostEstimate(
            flops=4 * 2 * 9 * STRETCH * wide * HEAD,
            bytes_accessed=4 * near.size,
            transcendentals=2 * 9 * STRETCH * wide,
        ),
    )(meta, ends, slots, query, near, far)


def attend_back(meta, ends, slots, query, grad, lse, turned, raw, gain, cosine, sine, near, far):
    rows = query.shape[2]
    wide = HEADS * rows
    keys = pl.BlockSpec((None, None, rows, 2 * HEAD), lambda j, *_: (j // 2, j % 2, 0, 0))
    fixed = [query, grad, lse, turned, raw, gain, cosine, sine]
    outs = [jax.ShapeDtypeStruct(grad.shape, bf16), jax.ShapeDtypeStruct(gain.shape, f32)]
    return pl.pallas_call(
        functools.partial(attend_back_kernel, rows),
        grid_spec=pltpu.PrefetchScalarGridSpec(
            num_scalar_prefetch=3,
            grid=(slots.shape[0],),
            in_specs=[*[whole_of(array) for array in fixed], keys, keys],
            out_specs=[*[whole_of(out) for out in outs], keys, keys],
            scratch_shapes=[
                pltpu.VMEM((2, wide, HEAD), bf16),
                pltpu.VMEM((2, 1, wide), f32),
                pltpu.VMEM((2, HEAD, wide), f32),
                pltpu.VMEM((STRETCH, 2 * HEAD), f32),
            ],
        ),
        out_shape=[*outs, jax.ShapeDtypeStruct(near.shape, bf16), jax.ShapeDtypeStruct(near.shape, bf16)],
        name="attend_back",
        cost_estimate=pl.CostEstimate(
            flops=10 * 2 * 9 * STRETCH * wide * HEAD,
            bytes_accessed=8 * near.size,
            transcendentals=2 * 9 * STRETCH * wide,
        ),
    )(meta, ends, slots, *fixed, near, far)


def blocks_of(tops, low, member, members, ff):
    return [(((hi * 2 + low) * 2 + y) * members + member) * ff for hi in range(tops) for y in range(2)]

def pack_kernel(tops, members, ff, gate_ref, up_ref, out_ref):
    for which, ref in enumerate((gate_ref, up_ref)):
        value = ref[...]
        for low in range(2):
            for member in range(members):
                cuts = [value[:, at : at + ff] for at in blocks_of(tops, low, member, members, ff)]
                out_ref[low, member, which] = jnp.concatenate(cuts, axis=1)

def pack(gate, up, tops, members, ff):
    rows = gate.shape[0]
    return pl.pallas_call(functools.partial(pack_kernel, tops, members, ff),
        out_shape=jax.ShapeDtypeStruct((2, members, 2, rows, 2 * tops * ff), bf16), name="pack")(gate, up)

def unpack_kernel(tops, members, ff, low_ref, in_ref, gate_ref, up_ref):
    for which, ref in enumerate((gate_ref, up_ref)):
        pieces = [None] * (2 * tops * 2 * members)
        for low in range(2):
            for member in range(members):
                value = in_ref[member, low_ref[0] ^ low, which].astype(f32)
                for i, at in enumerate(blocks_of(tops, low, member, members, ff)):
                    pieces[at // ff] = value[:, i * ff : (i + 1) * ff]
        ref[...] = jnp.concatenate(pieces, axis=1)

def unpack(moved, low_bit, tops, members, ff):
    rows = moved.shape[3]
    shape = jax.ShapeDtypeStruct((rows, 4 * tops * members * ff), f32)
    return pl.pallas_call(functools.partial(unpack_kernel, tops, members, ff),
        in_specs=[pl.BlockSpec(memory_space=pltpu.SMEM), pl.BlockSpec(memory_space=pltpu.VMEM)],
        out_shape=[shape, shape], name="unpack")(low_bit[None], moved)

def merge_kernel(in_ref, gate_ref, up_ref):
    for which, ref in enumerate((gate_ref, up_ref)):
        for low in range(2):
            ref[low] = jnp.concatenate([in_ref[m, low, which] for m in range(in_ref.shape[0])], axis=0)

def merge(moved):
    members, _, _, rows, wide = moved.shape
    shape = jax.ShapeDtypeStruct((2, members * rows, wide), bf16)
    return pl.pallas_call(merge_kernel, out_shape=[shape, shape], name="merge")(moved)

def split_kernel(gate_ref, up_ref, out_ref):
    members, rows = out_ref.shape[1], out_ref.shape[3]
    for which, ref in enumerate((gate_ref, up_ref)):
        for low in range(2):
            value = ref[low]
            for m in range(members):
                out_ref[low, m, which] = value[m * rows : (m + 1) * rows]

def split(gate, up, members):
    _, tall, wide = gate.shape
    return pl.pallas_call(split_kernel,
        out_shape=jax.ShapeDtypeStruct((2, members, 2, tall // members, wide), bf16), name="split")(gate, up)


def per_device(
    inputs,
    cotangent,
    lengths,
    deal,
    w_query,
    w_key,
    w_value,
    w_out,
    w_gate,
    w_up,
    w_down,
    gain_attn_pre,
    gain_attn_post,
    gain_ffw_pre,
    gain_ffw_post,
    gain_query,
    gain_key,
):
    rows, width = inputs.shape[1], inputs.shape[2]
    groups, members = lax.axis_size("dp"), lax.axis_size("seq")
    devices = groups * members
    total_rows = rows * devices
    dp_id, seq_id = lax.axis_index("dp"), lax.axis_index("seq")
    half_bit, x_bit, y_bit, z_bit = seq_id % 2, seq_id // 2, dp_id % 2, dp_id // 2 % 2
    tops = groups // 4
    count = 2 * rows
    model_rows, out_rows, ff_rows = w_query.shape[0], w_out.shape[0], w_down.shape[0]
    ff_local = 2 * tops * ff_rows
    wide_q = HEADS * HEAD
    gain_sizes = [gain_attn_pre.shape[0]] * 4 + [gain_query.shape[0]] * 2
    gain_total = sum(gain_sizes)
    block_rows = (model_rows + 8) // 8 * 8

    def regroup(array):
        kept = lax.dynamic_index_in_dim(array, y_bit, 0, keepdims=False)
        sent = lax.dynamic_index_in_dim(array, 1 - y_bit, 0, keepdims=False)
        return jnp.concatenate([kept, xor(sent, "dp", 1)], axis=0)

    def ungroup(array):
        kept, sent = array[:rows], array[rows:]
        return flips(jnp.stack([kept, xor(sent, "dp", 1)]), [y_bit])


    def column_exchange(packed):
        kept = lax.dynamic_index_in_dim(packed, z_bit, 0, keepdims=False)
        sent = lax.dynamic_index_in_dim(packed, 1 - z_bit, 0, keepdims=False)
        return jnp.stack([kept, xor(sent, "dp", 2)], axis=1)

    def swap_members(parts):
        return lax.all_to_all(parts, "seq", split_axis=0, concat_axis=0, tiled=True)

    top_id = dp_id // 4

    def from_tops(piece):
        return [piece] + [xor(piece, "dp", 4 * k) for k in range(1, tops)]

    def both_sides(tall):
        return tall + [xor(part, "dp", 1) for part in tall]

    gain_line, at = jnp.zeros((1, 2 * HEAD), f32), 0
    for gain in (gain_attn_pre, gain_attn_post, gain_ffw_pre, gain_ffw_post, gain_query, gain_key):
        gain_line += jnp.pad(gain.astype(f32)[None, :], ((0, 0), (at, gain_line.shape[1] - at - gain.shape[0])))
        at += gain.shape[0]
    shard = jnp.concatenate([jnp.concatenate([w_key, w_value], axis=1), gain_line.astype(bf16)], axis=0)
    blocks = jnp.pad(shard, ((0, block_rows - model_rows - 1), (0, 0)))[None]
    q_blocks = jnp.pad(w_query, ((0, block_rows - model_rows), (0, 0)))[None]
    packed = pack(w_gate, w_up, tops, members, ff_rows)
    first_mask, *more_masks, x_mask, core_mask = all_masks()
    blocks = gather_step(blocks, *first_mask)
    last_mask = first_mask
    for masks in [*more_masks, x_mask]:
        blocks, q_blocks = together(gather_step(blocks, *masks), gather_step(q_blocks, *last_mask))
        last_mask = masks
    blocks, packed, down_tall, rows_low = together(blocks, packed, from_tops(w_down[None]), regroup(inputs))
    rows_in = rows_low.astype(f32)
    q_blocks = gather_step(q_blocks, *x_mask)
    blocks = gather_step(blocks, *core_mask)
    kv_weight = blocks.reshape(devices * block_rows, 2 * HEAD)
    labels = all_labels()
    natural = jnp.stack([(dp_id ^ d) * members + (seq_id ^ s) for d, s in labels]).astype(jnp.int32)

    def selection(order, size, block, padded):
        within = jnp.arange(padded, dtype=jnp.int32)
        source = jnp.where(within < block, order[:, None] * block + within, -1).reshape(-1)
        return (jnp.arange(size, dtype=jnp.int32)[:, None] == source[None, :]).astype(bf16)

    model_pick = selection(natural, width, model_rows, block_rows)
    device_pick = selection(natural, devices, 1, 1)
    gain_blocks = blocks[:, model_rows, :gain_total]
    gain_all = mm(device_pick, gain_blocks)
    full_gain, at = [], 0
    for size in gain_sizes:
        full_gain.append(gain_all[:, at : at + size].reshape(devices * size))
        at += size
    pre_attention, post_attention, pre_feed, post_feed, query_gain, key_gain = full_gain


    owners = [(top_id ^ k) * 2 + (y_bit ^ u) for u in range(2) for k in range(tops)]
    owners = jnp.stack(owners).astype(jnp.int32)
    sources = [((top_id ^ k) * 2 + (z_bit ^ v)) * 2 + (y_bit ^ u) for u in range(2) for k in range(tops) for v in range(2)]
    sources = jnp.stack(sources).astype(jnp.int32)

    seq_ends = jnp.cumsum(lax.dynamic_index_in_dim(lengths, y_bit, 0, keepdims=False))
    dealt = lax.dynamic_index_in_dim(deal, y_bit, 0, keepdims=False)
    unit_ids = jnp.stack([(dp_id ^ u) * members + seq_id for u in range(2)])
    stretches = dealt[unit_ids * rows // STRETCH]
    first_rows = stretches * STRETCH + unit_ids * rows % STRETCH
    my_rows = (first_rows[:, None] + jnp.arange(rows, dtype=jnp.int32)).reshape(count)
    starts = layout_start(seq_ends, my_rows)
    lows = starts.reshape(2, rows)[:, 0] // STRETCH
    meta = jnp.concatenate([jnp.stack([first_rows, stretches, lows], axis=1).reshape(-1), half_bit[None]])
    layers = groups // 2
    slot_ids = jnp.stack(
        [
            ((dp_id // 2 ^ z) * 2 + (y_bit ^ u)) * (members // 2) + (x_bit ^ x)
            for x in range(2)
            for z in range(layers)
            for u in range(2)
        ]
    )
    slots = dealt[slot_ids]
    positions = my_rows - starts
    valid = (my_rows < total_rows - STRETCH)[:, None]
    freqs = rope_base ** (-2.0 * jnp.arange(HEAD // 2, dtype=f32) / HEAD)
    angle = positions.astype(f32)[:, None] * freqs
    cosine, sine = jnp.cos(angle), jnp.sin(angle)

    scale_one = norm_scale(rows_in)
    normed_one = (rows_in * scale_one * pre_attention).astype(bf16)
    picked_one = mm(normed_one, model_pick).astype(bf16)
    key_raw, keys_mine = project_keys(picked_one, kv_weight, key_gain[None], cosine, sine)
    column = [keys_mine] + [xor(keys_mine, "dp", 2 * k) for k in range(1, layers)]
    key_raw, packed = together(key_raw, packed)
    column_parts = column_exchange(packed)
    others, down_pieces, column_parts, late_out, q_blocks = together(
        column[1:], both_sides(down_tall), column_parts, w_out, q_blocks
    )
    column = [column[0], *others]
    out_weight = lax.all_gather(late_out, ALL, axis=0, tiled=True)
    halves = merge(swap_members(column_parts))
    q_weight = gather_step(q_blocks, *core_mask).reshape(devices * block_rows, wide_q)
    gate_tall, up_tall = from_tops(halves[0]), from_tops(halves[1])
    across = [xor(part, "seq", 2) for part in column]
    column, across = jnp.stack(column), jnp.stack(across)
    near_keys = jnp.concatenate([column, across])
    far_keys = jnp.concatenate([xor(column, "seq", 1), xor(across, "seq", 1)])
    query_raw, query_heads = project(picked_one, q_weight, query_gain[None], cosine, sine)
    context_rows, turned, lse = attend(meta, seq_ends, slots, query_heads, near_keys, far_keys)
    context_rows, gate_tall, up_tall = together(context_rows, gate_tall, up_tall)
    gate_pieces, up_pieces = both_sides(gate_tall), both_sides(up_tall)
    down_weight = place(down_pieces, owners).reshape(ff_local, width)
    attended = mm(context_rows, out_weight)
    scale_two = norm_scale(attended)
    hidden_res = rows_in + attended * scale_two * post_attention
    scale_three = norm_scale(hidden_res)
    normed_two = (hidden_res * scale_three * pre_feed).astype(bf16)

    normed_group, up_pieces = together(gather_group(normed_two), up_pieces)
    gate_weight, up_weight = [place(pieces, sources).reshape(width, ff_local) for pieces in (gate_pieces, up_pieces)]
    gate_raw = mm(normed_group, gate_weight)
    up_raw = mm(normed_group, up_weight)
    hidden_low = (jax.nn.gelu(gate_raw, approximate=True) * up_raw).astype(bf16)
    mixed = scatter_group(mm(hidden_low, down_weight).astype(bf16))
    q_natural, kv_natural = mm(model_pick, q_weight).astype(bf16), mm(model_pick, kv_weight).astype(bf16)
    q_natural, kv_natural, mixed = together(q_natural, kv_natural, mixed)
    scale_four = norm_scale(mixed)
    result = hidden_res + mixed * scale_four * post_feed
    output = ungroup(jnp.where(valid, result, 0.0).astype(bf16))

    upstream = jnp.where(valid, regroup(cotangent).astype(f32), 0.0)
    grad_post_feed = jnp.sum(upstream * mixed * scale_four, axis=0)
    mixed_grad = norm_back(mixed, scale_four, post_feed * upstream).astype(bf16)
    mixed_group = gather_group(mixed_grad)
    hidden_grad = mm_nt(mixed_group, down_weight)
    _, gelu_pull = jax.vjp(lambda g, u: jax.nn.gelu(g, approximate=True) * u, gate_raw, up_raw)
    gate_grad, up_grad = gelu_pull(hidden_grad)
    gate_grad, up_grad = gate_grad.astype(bf16), up_grad.astype(bf16)
    partial_grad = (mm_nt(gate_grad, gate_weight) + mm_nt(up_grad, up_weight)).astype(bf16)
    hidden_low, mixed_group, normed_group, gate_grad, up_grad, partial_grad = together(
        hidden_low, mixed_group, normed_group, gate_grad, up_grad, partial_grad
    )
    normed_two_grad = scatter_group(partial_grad)
    grad_pre_feed = jnp.sum(normed_two_grad * hidden_res * scale_three, axis=0)
    hidden_res_grad = upstream + norm_back(hidden_res, scale_three, pre_feed * normed_two_grad)

    def halve(total):
        kept = lax.dynamic_index_in_dim(total, y_bit, 2, keepdims=False)
        return kept, xor(lax.dynamic_index_in_dim(total, 1 - y_bit, 2, keepdims=False), "dp", 1)

    def by_top(kept, got):
        kept = add16(kept, got)
        return [lax.dynamic_index_in_dim(kept, top_id ^ k, 0, keepdims=False) for k in range(tops)]

    def send_tops(parts):
        return [part if k == 0 else xor(part, "dp", 4 * k) for k, part in enumerate(parts)]

    def total_of(parts):
        return functools.reduce(jnp.add, [part.astype(f32) for part in parts])

    def column_blocks(total):
        total = with_layout_constraint(total.astype(bf16), Layout((0, 1)))
        return total.reshape(tops, 2, 2, members * model_rows, ff_local)

    down_halves = halve(mm_tn(hidden_low, mixed_group).astype(bf16).reshape(tops, 1, 2, ff_rows, width))
    down_kept, gate_grad = together(down_halves[0], gate_grad)
    gate_halves = halve(column_blocks(mm_tn(normed_group, gate_grad)))
    gate_kept, down_got, up_grad = together(gate_halves[0], down_halves[1], up_grad)
    up_halves = halve(column_blocks(mm_tn(normed_group, up_grad)))
    down_halves, gate_halves = (down_kept, down_got), (gate_kept, gate_halves[1])

    grad_post_attention = jnp.sum(hidden_res_grad * attended * scale_two, axis=0)
    attended_grad = norm_back(attended, scale_two, post_attention * hidden_res_grad).astype(bf16)
    out_total = mm_tn(context_rows, attended_grad).astype(bf16)
    attended_grad, out_total, gate_kept, up_kept = lax.optimization_barrier(
        (attended_grad, out_total, gate_halves[0], up_halves[0])
    )
    gate_halves, up_halves = (gate_kept, gate_halves[1]), (up_kept, up_halves[1])
    down_parts = send_tops(by_top(*down_halves))
    grad_out = lax.psum_scatter(out_total, ALL, scatter_dimension=0, tiled=True)
    context_grad = mm_nt(attended_grad, out_weight).astype(bf16)
    query_grad, grad_query_gain, near_part, far_part = attend_back(
        meta, seq_ends, slots, query_heads, context_grad, lse, turned, query_raw, query_gain[None], cosine, sine, near_keys, far_keys
    )
    far_part, near_part, gate_halves, up_halves, down_parts = lax.optimization_barrier(
        (far_part, near_part, gate_halves, up_halves, down_parts)
    )
    gate_parts, up_parts = [send_tops(by_top(*half)) for half in (gate_halves, up_halves)]
    far_part = xor(far_part, "seq", 1)
    query_low, far_part = together(query_grad, far_part)
    near_part = add16(near_part, far_part).reshape(2, layers, count, 2 * HEAD)
    near_part = add16(near_part[0], xor(near_part[1], "seq", 2))
    grad_query = mm_tn(picked_one, query_low).astype(bf16).reshape(devices, block_rows, wide_q)
    grad_query, near_part, gate_parts = together(scatter_step(grad_query, *core_mask), near_part, gate_parts)
    grad_query = scatter_rest(grad_query)
    key_parts = [near_part[k] if k == 0 else xor(near_part[k], "dp", 2 * k) for k in range(layers)]
    key_parts, up_parts = together(key_parts, up_parts)
    key_grads = functools.reduce(jnp.add, [part.astype(f32) for part in key_parts])
    value_grad = key_grads[:, HEAD:].astype(bf16)
    key_turned = rotate(key_grads[:, :HEAD], cosine, -sine)
    key_scale = norm_scale(key_raw)
    grad_key_gain = jnp.sum(key_turned * key_raw * key_scale, axis=0)
    key_grad = norm_back(key_raw, key_scale, key_gain * key_turned).astype(bf16)
    kv_grad = jnp.concatenate([key_grad, value_grad], axis=1)
    normed_one_grad = mm_nt(query_grad, q_natural) + mm_nt(kv_grad, kv_natural)
    grad_pre_attention = jnp.sum(normed_one_grad * rows_in * scale_one, axis=0)
    rows_grad = hidden_res_grad + norm_back(rows_in, scale_one, pre_attention * normed_one_grad)
    rows_low, down_parts, gate_parts, up_parts = together(rows_grad.astype(bf16), down_parts, gate_parts, up_parts)
    grad_down = total_of(down_parts)[0]
    both_grads = split(total_of(gate_parts).astype(bf16), total_of(up_parts).astype(bf16), members)
    grad_gate, grad_up = unpack(swap_members(column_exchange(both_grads)), z_bit, tops, members, ff_rows)
    input_grad = ungroup(rows_low)
    grad_kv = mm_tn(picked_one, kv_grad).reshape(devices, block_rows, 2 * HEAD)
    gain_grads = [
        grad_pre_attention,
        grad_post_attention,
        grad_pre_feed,
        grad_post_feed,
        grad_query_gain,
        grad_key_gain,
    ]
    gain_grads = jnp.concatenate([g.reshape(devices, -1) for g in gain_grads], axis=1)
    gain_grads = mm_tn(device_pick, gain_grads.astype(bf16))
    gain_grads = jnp.pad(
        gain_grads[:, None, :], ((0, 0), (model_rows, block_rows - model_rows - 1), (0, 2 * HEAD - gain_total))
    )
    last = scatter_rest(scatter_step((grad_kv + gain_grads).astype(bf16), *core_mask))
    last, grad_out = together(last, grad_out)
    grad_out = grad_out.astype(f32)
    gain_out, at = [], 0
    for size in gain_sizes:
        gain_out.append(last[model_rows, at : at + size])
        at += size
    return (
        output,
        input_grad,
        grad_query[:model_rows],
        last[:model_rows, :HEAD],
        last[:model_rows, HEAD:],
        grad_out,
        grad_gate,
        grad_up,
        grad_down,
        *gain_out,
    )


def solution(mesh):
    split = P(None, ALL, None)
    weight, gain = P(ALL, None), P(ALL)
    return jax.shard_map(
        per_device,
        mesh=mesh,
        in_specs=(split, split, P(), P(), *[weight] * 7, *[gain] * 6),
        out_specs=(split, split, *[weight] * 7, *[gain] * 6),
        check_vma=False,
    )
```

```python
import functools
import math

import jax
import jax.numpy as jnp
from jax import lax
from jax.experimental import pallas as pl
from jax.experimental.layout import Layout, with_layout_constraint
from jax.experimental.pallas import tpu as pltpu
from jax.sharding import PartitionSpec as P

HEADS = 4
HEAD = 256
MB = 2
STRETCH = 256

eps = 1e-06
rope_base = 1000000.0
masked_score = -1e30
bf16 = jnp.bfloat16
f32 = jnp.float32
ALL = ("dp", "seq")


def norm_scale(values):
    return lax.rsqrt(jnp.mean(values * values, axis=-1, keepdims=True) + eps)


def norm_back(values, scale, weighted):
    return scale * weighted - values * (scale * scale * scale) * jnp.mean(
        weighted * values, axis=-1, keepdims=True
    )


def rotate(values, cosine, sine):
    first, second = jnp.split(values, 2, axis=-1)
    return jnp.concatenate([first * cosine - second * sine, second * cosine + first * sine], axis=-1)


def layout_start(ends, row_ids):
    after = row_ids[:, None] >= ends[None, :]
    return jnp.max(jnp.where(after, ends[None, :], 0), axis=1)


def dot(left, right, dims):
    return lax.dot_general(left, right, (dims, ((), ())), preferred_element_type=f32)


def mm(left, right):
    return dot(left, right, ((1,), (0,)))


def mm_tn(left, right):
    return dot(left, right, ((0,), (0,)))


def mm_nt(left, right):
    return dot(left, right, ((1,), (1,)))


def xor(value, axis, mask):
    return lax.ppermute(value, axis, [(i, i ^ mask) for i in range(lax.axis_size(axis))])


def xor_both(value, dp_mask, seq_mask):
    members = lax.axis_size("seq")
    mask = dp_mask * members + seq_mask
    return lax.ppermute(value, ALL, [(i, i ^ mask) for i in range(lax.axis_size("dp") * members)])


def flips(value, bits):
    for axis, bit in enumerate(bits):
        halves = [lax.slice_in_dim(value, i, i + 1, axis=axis) for i in (1, 0)]
        value = jnp.where(bit == 1, lax.concatenate(halves, axis), value)
    return value


def add16(left, right):
    return (left.astype(f32) + right.astype(f32)).astype(bf16)


def together(*values):
    return lax.optimization_barrier(values)


def all_masks():
    rows = [(1 << bit, 0) for bit in range(1, 16) if 1 << bit < lax.axis_size("dp")]
    return rows + [(1, 0), (0, 2), (0, 1)]


def gather_step(value, dp_mask, seq_mask):
    return jnp.concatenate([value, xor_both(value, dp_mask, seq_mask)])


def all_labels():
    labels = [(0, 0)]
    for dp_mask, seq_mask in all_masks():
        labels = labels + [(d ^ dp_mask, s ^ seq_mask) for d, s in labels]
    return labels


def scatter_step(total, dp_mask, seq_mask):
    half = total.shape[0] // 2
    got = xor_both(total[half:], dp_mask, seq_mask)
    total = total[:half].astype(f32) + got.astype(f32)
    return total if half == 1 else total.astype(bf16)


def scatter_rest(total):
    for masks in list(reversed(all_masks()))[1:]:
        total = scatter_step(total, *masks)
    return total[0]


def gather_group(rows):
    half = rows.shape[0] // 2
    across, along = xor(rows, "seq", 2), xor(rows, "dp", 2)
    corner = [xor(across[:half], "dp", 2), xor(along[half:], "seq", 2)]
    near = [rows, across, along, *corner]
    far = [rows, jnp.concatenate([across, along]), jnp.concatenate(corner)]
    return jnp.concatenate(near + [xor(part, "seq", 1) for part in far], axis=0)


def scatter_group(total):
    parts = total.reshape(2, -1, total.shape[1])
    near = add16(parts[0], xor(parts[1], "seq", 1))
    mine, across, along, corner = jnp.split(near, 4)
    half = mine.shape[0] // 2
    low, high = xor(corner[:half], "dp", 2), xor(corner[half:], "seq", 2)
    across = jnp.concatenate([add16(across[:half], low), across[half:]])
    along = jnp.concatenate([along[:half], add16(along[half:], high)])
    return mine.astype(f32) + xor(across, "seq", 2).astype(f32) + xor(along, "dp", 2).astype(f32)


def place_kernel(sizes, target_ref, *refs):
    pieces, out = refs[: len(sizes)], refs[len(sizes)]
    buffer, arrived, left = refs[len(sizes) + 1 :]
    ins, outs, block = [], [], 0
    for piece, size in zip(pieces, sizes):
        for index in range(size):
            ins.append(pltpu.make_async_copy(piece.at[index], buffer.at[block], arrived.at[block]))
            outs.append(pltpu.make_async_copy(buffer.at[block], out.at[target_ref[block]], left.at[block]))
            ins[-1].start()
            block += 1
    for copy_in, copy_out in zip(ins, outs):
        copy_in.wait()
        copy_out.start()
    for copy_out in outs:
        copy_out.wait()


def place(pieces, targets):
    sizes = [piece.shape[0] for piece in pieces]
    shape = (sum(sizes), *pieces[0].shape[1:])
    anywhere = pl.BlockSpec(memory_space=pl.ANY)
    return pl.pallas_call(
        functools.partial(place_kernel, sizes),
        grid_spec=pltpu.PrefetchScalarGridSpec(
            num_scalar_prefetch=1,
            grid=(1,),
            in_specs=[anywhere] * len(pieces),
            out_specs=anywhere,
            scratch_shapes=[
                pltpu.VMEM(shape, pieces[0].dtype),
                pltpu.SemaphoreType.DMA((shape[0],)),
                pltpu.SemaphoreType.DMA((shape[0],)),
            ],
        ),
        out_shape=jax.ShapeDtypeStruct(shape, pieces[0].dtype),
        name="place",
        cost_estimate=pl.CostEstimate(flops=0, bytes_accessed=4 * math.prod(shape), transcendentals=0),
    )(targets, *pieces)


def project_kernel(scale, picked_ref, weight_ref, gain_ref, cos_ref, sin_ref, raw_ref, out_ref):
    raw = mm(picked_ref[...], weight_ref[...])
    raw_ref[0] = raw
    turned = rotate(raw * norm_scale(raw) * gain_ref[...], cos_ref[...], sin_ref[...]).astype(bf16)
    out_ref[...] = (turned * scale).astype(bf16).reshape(out_ref.shape)


def project(picked, weight, gain, cosine, sine):
    count, deep = picked.shape
    rows = count // 2
    same = lambda h: (0, 0)
    return pl.pallas_call(
        functools.partial(project_kernel, HEAD**-0.5),
        grid=(HEADS,),
        in_specs=[
            pl.BlockSpec((count, deep), same),
            pl.BlockSpec((deep, HEAD), lambda h: (0, h)),
            pl.BlockSpec((1, HEAD), same),
            pl.BlockSpec((count, HEAD // 2), same),
            pl.BlockSpec((count, HEAD // 2), same),
        ],
        out_specs=[
            pl.BlockSpec((1, count, HEAD), lambda h: (h, 0, 0)),
            pl.BlockSpec((2, 1, rows, HEAD), lambda h: (0, h, 0, 0)),
        ],
        out_shape=[
            jax.ShapeDtypeStruct((HEADS, count, HEAD), f32),
            jax.ShapeDtypeStruct((2, HEADS, rows, HEAD), bf16),
        ],
        name="project",
        cost_estimate=pl.CostEstimate(
            flops=2 * count * deep * HEADS * HEAD, bytes_accessed=2 * deep * HEADS * HEAD, transcendentals=0
        ),
    )(picked, weight, gain, cosine, sine)


def project_keys_kernel(picked_ref, weight_ref, gain_ref, cos_ref, sin_ref, raw_ref, out_ref):
    both = mm(picked_ref[...], weight_ref[...])
    raw = both[:, :HEAD]
    raw_ref[...] = raw
    turned = rotate(raw * norm_scale(raw) * gain_ref[...], cos_ref[...], sin_ref[...])
    both = jnp.concatenate([turned, both[:, HEAD:]], axis=1).astype(bf16)
    out_ref[...] = both.reshape(out_ref.shape)


def project_keys(picked, weight, gain, cosine, sine):
    count, deep = picked.shape
    return pl.pallas_call(
        project_keys_kernel,
        grid=(1,),
        in_specs=[
            whole_of(picked),
            pl.BlockSpec((deep, 2 * HEAD), lambda i: (0, HEADS // 2)),
            whole_of(gain),
            whole_of(cosine),
            whole_of(sine),
        ],
        out_specs=[
            pl.BlockSpec((count, HEAD), lambda i: (0, 0)),
            pl.BlockSpec((2, count // 2, 2 * HEAD), lambda i: (0, 0, 0)),
        ],
        out_shape=[
            jax.ShapeDtypeStruct((count, HEAD), f32),
            jax.ShapeDtypeStruct((2, count // 2, 2 * HEAD), bf16),
        ],
        name="project_keys",
        cost_estimate=pl.CostEstimate(
            flops=4 * count * deep * HEAD, bytes_accessed=4 * deep * HEAD, transcendentals=0
        ),
    )(picked, weight, gain, cosine, sine)


def mask_of(meta_ref, ends_ref, unit, rows, key_stretch):
    lanes = lax.broadcasted_iota(jnp.int32, (1, HEADS * rows), 1)
    ids = meta_ref[3 * unit] + lanes % rows
    start = jnp.zeros_like(ids)
    for index in range(ends_ref.shape[0]):
        end = ends_ref[index]
        start = jnp.where(ids >= end, end, start)
    place_in = lax.broadcasted_iota(jnp.int32, (STRETCH, 1), 0)
    near = meta_ref[6] * rows
    place_in = jnp.where(place_in < rows, place_in + near, place_in - near)
    key = key_stretch * STRETCH + place_in
    return (key <= ids) & (key >= start)


def attend_kernel(
    rows, meta_ref, ends_ref, slots_ref, q_ref, near_ref, far_ref, c_ref, turned_ref, lse_ref, top, total, acc
):
    step = pl.program_id(0)

    @pl.when(step == 0)
    def _():
        top[...] = jnp.full_like(top, masked_score)
        total[...] = jnp.zeros_like(total)
        acc[...] = jnp.zeros_like(acc)

    key_stretch = slots_ref[step]
    for unit in range(2):

        @pl.when((key_stretch <= meta_ref[3 * unit + 1]) & (key_stretch >= meta_ref[3 * unit + 2]))
        def _():
            mask = mask_of(meta_ref, ends_ref, unit, rows, key_stretch)
            block = jnp.concatenate([near_ref[...], far_ref[...]], axis=0)
            query = q_ref[unit].reshape(HEADS * rows, HEAD)
            scores = jnp.where(mask, mm_nt(block[:, :HEAD], query), masked_score)
            old = top[unit]
            new = jnp.maximum(old, jnp.max(scores, axis=0, keepdims=True))
            keep = jnp.exp(old - new)
            terms = jnp.exp(scores - new)
            top[unit] = new
            total[unit] = total[unit] * keep + jnp.sum(terms, axis=0, keepdims=True)
            acc[unit] = acc[unit] * keep + mm_tn(block[:, HEAD:], terms.astype(bf16))

    @pl.when(step == pl.num_programs(0) - 1)
    def _():
        for unit in range(2):
            out = acc[unit] * (1.0 / total[unit])
            turned_ref[unit] = out
            lse_ref[unit] = top[unit] + jnp.log(total[unit])
            out = out.T.astype(bf16)
            for head in range(HEADS):
                c_ref[unit * rows : (unit + 1) * rows, head * HEAD : (head + 1) * HEAD] = out[
                    head * rows : (head + 1) * rows
                ]


def attend_back_kernel(
    rows,
    meta_ref,
    ends_ref,
    slots_ref,
    q_ref,
    dc_ref,
    lse_ref,
    turned_ref,
    raw_ref,
    gain_ref,
    cos_ref,
    sin_ref,
    near_ref,
    far_ref,
    dq_ref,
    dgain_ref,
    dnear_ref,
    dfar_ref,
    grads,
    delta,
    acc,
    both,
):
    step = pl.program_id(0)

    @pl.when(step == 0)
    def _():
        acc[...] = jnp.zeros_like(acc)
        for unit in range(2):
            for head in range(HEADS):
                grads[unit, head * rows : (head + 1) * rows] = dc_ref[
                    unit * rows : (unit + 1) * rows, head * HEAD : (head + 1) * HEAD
                ]
            across = grads[unit].astype(f32).T
            delta[unit] = jnp.sum(across * turned_ref[unit], axis=0, keepdims=True)

    key_stretch = slots_ref[step]
    both[...] = jnp.zeros_like(both)
    for unit in range(2):

        @pl.when((key_stretch <= meta_ref[3 * unit + 1]) & (key_stretch >= meta_ref[3 * unit + 2]))
        def _():
            mask = mask_of(meta_ref, ends_ref, unit, rows, key_stretch)
            block = jnp.concatenate([near_ref[...], far_ref[...]], axis=0)
            key, value = block[:, :HEAD], block[:, HEAD:]
            query = q_ref[unit].reshape(HEADS * rows, HEAD)
            grad = grads[unit]
            probs = jnp.where(mask, jnp.exp(mm_nt(key, query) - lse_ref[unit]), 0.0)
            score_grad = (probs * (mm_nt(value, grad) - delta[unit])).astype(bf16)
            acc[unit] += mm_tn(key, score_grad)
            both[:, :HEAD] += mm(score_grad, query)
            both[:, HEAD:] += mm(probs.astype(bf16), grad)

    dnear_ref[...] = both[:rows].astype(bf16)
    dfar_ref[...] = both[rows:].astype(bf16)

    @pl.when(step == pl.num_programs(0) - 1)
    def _():
        gain = gain_ref[...]
        total = jnp.zeros_like(gain)
        for unit in range(2):
            mine = slice(unit * rows, (unit + 1) * rows)
            grad = acc[unit].T * HEAD**-0.5
            for head in range(HEADS):
                back = rotate(grad[head * rows : (head + 1) * rows], cos_ref[mine], -sin_ref[mine])
                raw = raw_ref[head, mine]
                scale = norm_scale(raw)
                total = total + jnp.sum(back * raw * scale, axis=0, keepdims=True)
                back = norm_back(raw, scale, gain * back)
                dq_ref[mine, head * HEAD : (head + 1) * HEAD] = back.astype(bf16)
        dgain_ref[...] = total


def whole_of(array):
    return pl.BlockSpec(array.shape, lambda *_: (0,) * len(array.shape))


def attend(meta, ends, slots, query, near, far):
    rows = query.shape[2]
    wide = HEADS * rows
    keys = pl.BlockSpec((None, None, rows, 2 * HEAD), lambda j, *_: (j // 2, j % 2, 0, 0))
    outs = [
        jax.ShapeDtypeStruct((2 * rows, HEADS * HEAD), bf16),
        jax.ShapeDtypeStruct((2, HEAD, wide), f32),
        jax.ShapeDtypeStruct((2, 1, wide), f32),
    ]
    return pl.pallas_call(
        functools.partial(attend_kernel, rows),
        grid_spec=pltpu.PrefetchScalarGridSpec(
            num_scalar_prefetch=3,
            grid=(slots.shape[0],),
            in_specs=[whole_of(query), keys, keys],
            out_specs=[whole_of(out) for out in outs],
            scratch_shapes=[
                pltpu.VMEM((2, 1, wide), f32),
                pltpu.VMEM((2, 1, wide), f32),
                pltpu.VMEM((2, HEAD, wide), f32),
            ],
        ),
        out_shape=outs,
        name="attend",
        cost_estimate=pl.CostEstimate(
            flops=4 * 2 * 9 * STRETCH * wide * HEAD,
            bytes_accessed=4 * near.size,
            transcendentals=2 * 9 * STRETCH * wide,
        ),
    )(meta, ends, slots, query, near, far)


def attend_back(meta, ends, slots, query, grad, lse, turned, raw, gain, cosine, sine, near, far):
    rows = query.shape[2]
    wide = HEADS * rows
    keys = pl.BlockSpec((None, None, rows, 2 * HEAD), lambda j, *_: (j // 2, j % 2, 0, 0))
    fixed = [query, grad, lse, turned, raw, gain, cosine, sine]
    outs = [jax.ShapeDtypeStruct(grad.shape, bf16), jax.ShapeDtypeStruct(gain.shape, f32)]
    return pl.pallas_call(
        functools.partial(attend_back_kernel, rows),
        grid_spec=pltpu.PrefetchScalarGridSpec(
            num_scalar_prefetch=3,
            grid=(slots.shape[0],),
            in_specs=[*[whole_of(array) for array in fixed], keys, keys],
            out_specs=[*[whole_of(out) for out in outs], keys, keys],
            scratch_shapes=[
                pltpu.VMEM((2, wide, HEAD), bf16),
                pltpu.VMEM((2, 1, wide), f32),
                pltpu.VMEM((2, HEAD, wide), f32),
                pltpu.VMEM((STRETCH, 2 * HEAD), f32),
            ],
        ),
        out_shape=[*outs, jax.ShapeDtypeStruct(near.shape, bf16), jax.ShapeDtypeStruct(near.shape, bf16)],
        name="attend_back",
        cost_estimate=pl.CostEstimate(
            flops=10 * 2 * 9 * STRETCH * wide * HEAD,
            bytes_accessed=8 * near.size,
            transcendentals=2 * 9 * STRETCH * wide,
        ),
    )(meta, ends, slots, *fixed, near, far)


def blocks_of(tops, low, member, members, ff):
    return [(((hi * 2 + low) * 2 + y) * members + member) * ff for hi in range(tops) for y in range(2)]

def pack_kernel(tops, members, ff, gate_ref, up_ref, out_ref):
    for which, ref in enumerate((gate_ref, up_ref)):
        value = ref[...]
        for low in range(2):
            for member in range(members):
                cuts = [value[:, at : at + ff] for at in blocks_of(tops, low, member, members, ff)]
                out_ref[low, member, which] = jnp.concatenate(cuts, axis=1)

def pack(gate, up, tops, members, ff):
    rows = gate.shape[0]
    return pl.pallas_call(functools.partial(pack_kernel, tops, members, ff),
        out_shape=jax.ShapeDtypeStruct((2, members, 2, rows, 2 * tops * ff), bf16), name="pack")(gate, up)

def unpack_kernel(tops, members, ff, low_ref, in_ref, gate_ref, up_ref):
    for which, ref in enumerate((gate_ref, up_ref)):
        pieces = [None] * (2 * tops * 2 * members)
        for low in range(2):
            for member in range(members):
                value = in_ref[member, low_ref[0] ^ low, which].astype(f32)
                for i, at in enumerate(blocks_of(tops, low, member, members, ff)):
                    pieces[at // ff] = value[:, i * ff : (i + 1) * ff]
        ref[...] = jnp.concatenate(pieces, axis=1)

def unpack(moved, low_bit, tops, members, ff):
    rows = moved.shape[3]
    shape = jax.ShapeDtypeStruct((rows, 4 * tops * members * ff), f32)
    return pl.pallas_call(functools.partial(unpack_kernel, tops, members, ff),
        in_specs=[pl.BlockSpec(memory_space=pltpu.SMEM), pl.BlockSpec(memory_space=pltpu.VMEM)],
        out_shape=[shape, shape], name="unpack")(low_bit[None], moved)

def merge_kernel(in_ref, gate_ref, up_ref):
    for which, ref in enumerate((gate_ref, up_ref)):
        for low in range(2):
            ref[low] = jnp.concatenate([in_ref[m, low, which] for m in range(in_ref.shape[0])], axis=0)

def merge(moved):
    members, _, _, rows, wide = moved.shape
    shape = jax.ShapeDtypeStruct((2, members * rows, wide), bf16)
    return pl.pallas_call(merge_kernel, out_shape=[shape, shape], name="merge")(moved)

def split_kernel(gate_ref, up_ref, out_ref):
    members, rows = out_ref.shape[1], out_ref.shape[3]
    for which, ref in enumerate((gate_ref, up_ref)):
        for low in range(2):
            value = ref[low]
            for m in range(members):
                out_ref[low, m, which] = value[m * rows : (m + 1) * rows]

def split(gate, up, members):
    _, tall, wide = gate.shape
    return pl.pallas_call(split_kernel,
        out_shape=jax.ShapeDtypeStruct((2, members, 2, tall // members, wide), bf16), name="split")(gate, up)


def per_device(
    inputs,
    cotangent,
    lengths,
    deal,
    w_query,
    w_key,
    w_value,
    w_out,
    w_gate,
    w_up,
    w_down,
    gain_attn_pre,
    gain_attn_post,
    gain_ffw_pre,
    gain_ffw_post,
    gain_query,
    gain_key,
):
    rows, width = inputs.shape[1], inputs.shape[2]
    groups, members = lax.axis_size("dp"), lax.axis_size("seq")
    devices = groups * members
    total_rows = rows * devices
    dp_id, seq_id = lax.axis_index("dp"), lax.axis_index("seq")
    half_bit, x_bit, y_bit, z_bit = seq_id % 2, seq_id // 2, dp_id % 2, dp_id // 2 % 2
    tops = groups // 4
    count = 2 * rows
    model_rows, out_rows, ff_rows = w_query.shape[0], w_out.shape[0], w_down.shape[0]
    ff_local = 2 * tops * ff_rows
    wide_q = HEADS * HEAD
    gain_sizes = [gain_attn_pre.shape[0]] * 4 + [gain_query.shape[0]] * 2
    gain_total = sum(gain_sizes)
    block_rows = (model_rows + 8) // 8 * 8

    def regroup(array):
        kept = lax.dynamic_index_in_dim(array, y_bit, 0, keepdims=False)
        sent = lax.dynamic_index_in_dim(array, 1 - y_bit, 0, keepdims=False)
        return jnp.concatenate([kept, xor(sent, "dp", 1)], axis=0)

    def ungroup(array):
        kept, sent = array[:rows], array[rows:]
        return flips(jnp.stack([kept, xor(sent, "dp", 1)]), [y_bit])


    def column_exchange(packed):
        kept = lax.dynamic_index_in_dim(packed, z_bit, 0, keepdims=False)
        sent = lax.dynamic_index_in_dim(packed, 1 - z_bit, 0, keepdims=False)
        return jnp.stack([kept, xor(sent, "dp", 2)], axis=1)

    def swap_members(parts):
        return lax.all_to_all(parts, "seq", split_axis=0, concat_axis=0, tiled=True)

    gain_line, at = jnp.zeros((1, wide_q + 2 * HEAD), f32), 0
    for gain in (gain_attn_pre, gain_attn_post, gain_ffw_pre, gain_ffw_post, gain_query, gain_key):
        gain_line += jnp.pad(gain.astype(f32)[None, :], ((0, 0), (at, gain_line.shape[1] - at - gain.shape[0])))
        at += gain.shape[0]
    shard = jnp.concatenate([w_query, w_key, w_value], axis=1)
    shard = jnp.concatenate([shard, gain_line.astype(bf16)], axis=0)
    blocks = jnp.pad(shard, ((0, block_rows - model_rows - 1), (0, 0)))[None]
    packed = pack(w_gate, w_up, tops, members, ff_rows)
    *row_masks, y_mask, x_mask, core_mask = all_masks()
    for masks in row_masks:
        blocks = gather_step(blocks, *masks)
    blocks, rows_low = together(blocks, regroup(inputs))
    rows_in = rows_low.astype(f32)
    blocks = gather_step(gather_step(blocks, *y_mask), *x_mask)
    blocks = gather_step(blocks, *core_mask)
    blocks, late_out = together(blocks, w_out)
    qkv_weight = blocks.reshape(devices * block_rows, wide_q + 2 * HEAD)
    out_weight = lax.all_gather(late_out, ALL, axis=0, tiled=True)
    labels = all_labels()
    natural = jnp.stack([(dp_id ^ d) * members + (seq_id ^ s) for d, s in labels]).astype(jnp.int32)

    def selection(order, size, block, padded):
        within = jnp.arange(padded, dtype=jnp.int32)
        source = jnp.where(within < block, order[:, None] * block + within, -1).reshape(-1)
        return (jnp.arange(size, dtype=jnp.int32)[:, None] == source[None, :]).astype(bf16)

    model_pick = selection(natural, width, model_rows, block_rows)
    device_pick = selection(natural, devices, 1, 1)
    gain_blocks = blocks[:, model_rows, :gain_total]
    gain_all = mm(device_pick, gain_blocks)
    full_gain, at = [], 0
    for size in gain_sizes:
        full_gain.append(gain_all[:, at : at + size].reshape(devices * size))
        at += size
    pre_attention, post_attention, pre_feed, post_feed, query_gain, key_gain = full_gain

    top_id = dp_id // 4

    def from_tops(piece):
        return [piece] + [xor(piece, "dp", 4 * k) for k in range(1, tops)]

    def both_sides(tall):
        return tall + [xor(part, "dp", 1) for part in tall]

    owners = [(top_id ^ k) * 2 + (y_bit ^ u) for u in range(2) for k in range(tops)]
    owners = jnp.stack(owners).astype(jnp.int32)
    sources = [((top_id ^ k) * 2 + (z_bit ^ v)) * 2 + (y_bit ^ u) for u in range(2) for k in range(tops) for v in range(2)]
    sources = jnp.stack(sources).astype(jnp.int32)

    seq_ends = jnp.cumsum(lax.dynamic_index_in_dim(lengths, y_bit, 0, keepdims=False))
    dealt = lax.dynamic_index_in_dim(deal, y_bit, 0, keepdims=False)
    unit_ids = jnp.stack([(dp_id ^ u) * members + seq_id for u in range(2)])
    stretches = dealt[unit_ids * rows // STRETCH]
    first_rows = stretches * STRETCH + unit_ids * rows % STRETCH
    my_rows = (first_rows[:, None] + jnp.arange(rows, dtype=jnp.int32)).reshape(count)
    starts = layout_start(seq_ends, my_rows)
    lows = starts.reshape(2, rows)[:, 0] // STRETCH
    meta = jnp.concatenate([jnp.stack([first_rows, stretches, lows], axis=1).reshape(-1), half_bit[None]])
    layers = groups // 2
    slot_ids = jnp.stack(
        [
            ((dp_id // 2 ^ z) * 2 + (y_bit ^ u)) * (members // 2) + (x_bit ^ x)
            for x in range(2)
            for z in range(layers)
            for u in range(2)
        ]
    )
    slots = dealt[slot_ids]
    positions = my_rows - starts
    valid = (my_rows < total_rows - STRETCH)[:, None]
    freqs = rope_base ** (-2.0 * jnp.arange(HEAD // 2, dtype=f32) / HEAD)
    angle = positions.astype(f32)[:, None] * freqs
    cosine, sine = jnp.cos(angle), jnp.sin(angle)

    scale_one = norm_scale(rows_in)
    normed_one = (rows_in * scale_one * pre_attention).astype(bf16)
    picked_one = mm(normed_one, model_pick).astype(bf16)
    key_raw, keys_mine = project_keys(picked_one, qkv_weight, key_gain[None], cosine, sine)
    key_raw, packed = together(key_raw, packed)
    column = [keys_mine] + [xor(keys_mine, "dp", 2 * k) for k in range(1, layers)]
    others, column_parts, down_piece = together(column[1:], column_exchange(packed), w_down[None])
    column = [column[0], *others]
    down_tall = from_tops(down_piece)
    halves = merge(swap_members(column_parts))
    gate_tall, up_tall = from_tops(halves[0]), from_tops(halves[1])
    across = [xor(part, "seq", 2) for part in column]
    down_pieces = both_sides(down_tall)
    column, across = jnp.stack(column), jnp.stack(across)
    near_keys = jnp.concatenate([column, across])
    far_keys = jnp.concatenate([xor(column, "seq", 1), xor(across, "seq", 1)])
    query_raw, query_heads = project(picked_one, qkv_weight, query_gain[None], cosine, sine)
    context_rows, turned, lse = attend(meta, seq_ends, slots, query_heads, near_keys, far_keys)
    context_rows, gate_tall = together(context_rows, gate_tall)
    gate_pieces = both_sides(gate_tall)
    down_weight = place(down_pieces, owners).reshape(ff_local, width)
    attended = mm(context_rows, out_weight)
    scale_two = norm_scale(attended)
    hidden_res = rows_in + attended * scale_two * post_attention
    scale_three = norm_scale(hidden_res)
    normed_two = (hidden_res * scale_three * pre_feed).astype(bf16)

    normed_two, up_tall = together(normed_two, up_tall)
    up_pieces = both_sides(up_tall)
    normed_group, gate_pieces, up_pieces = together(gather_group(normed_two), gate_pieces, up_pieces)
    gate_weight, up_weight = [place(pieces, sources).reshape(width, ff_local) for pieces in (gate_pieces, up_pieces)]
    gate_raw = mm(normed_group, gate_weight)
    up_raw = mm(normed_group, up_weight)
    hidden_low = (jax.nn.gelu(gate_raw, approximate=True) * up_raw).astype(bf16)
    mixed = scatter_group(mm(hidden_low, down_weight).astype(bf16))
    natural_weight, mixed = together(mm(model_pick, qkv_weight).astype(bf16), mixed)
    scale_four = norm_scale(mixed)
    result = hidden_res + mixed * scale_four * post_feed
    output = ungroup(jnp.where(valid, result, 0.0).astype(bf16))

    upstream = jnp.where(valid, regroup(cotangent).astype(f32), 0.0)
    grad_post_feed = jnp.sum(upstream * mixed * scale_four, axis=0)
    mixed_grad = norm_back(mixed, scale_four, post_feed * upstream).astype(bf16)
    mixed_group = gather_group(mixed_grad)
    hidden_grad = mm_nt(mixed_group, down_weight)
    _, gelu_pull = jax.vjp(lambda g, u: jax.nn.gelu(g, approximate=True) * u, gate_raw, up_raw)
    gate_grad, up_grad = gelu_pull(hidden_grad)
    gate_grad, up_grad = gate_grad.astype(bf16), up_grad.astype(bf16)
    partial_grad = (mm_nt(gate_grad, gate_weight) + mm_nt(up_grad, up_weight)).astype(bf16)
    hidden_low, mixed_group, normed_group, gate_grad, up_grad, partial_grad = together(
        hidden_low, mixed_group, normed_group, gate_grad, up_grad, partial_grad
    )
    normed_two_grad = scatter_group(partial_grad)
    grad_pre_feed = jnp.sum(normed_two_grad * hidden_res * scale_three, axis=0)
    hidden_res_grad = upstream + norm_back(hidden_res, scale_three, pre_feed * normed_two_grad)

    def halve(total):
        kept = lax.dynamic_index_in_dim(total, y_bit, 2, keepdims=False)
        return kept, xor(lax.dynamic_index_in_dim(total, 1 - y_bit, 2, keepdims=False), "dp", 1)

    def by_top(kept, got):
        kept = add16(kept, got)
        return [lax.dynamic_index_in_dim(kept, top_id ^ k, 0, keepdims=False) for k in range(tops)]

    def send_tops(parts):
        return [part if k == 0 else xor(part, "dp", 4 * k) for k, part in enumerate(parts)]

    def total_of(parts):
        return functools.reduce(jnp.add, [part.astype(f32) for part in parts])

    def column_blocks(total):
        total = with_layout_constraint(total.astype(bf16), Layout((0, 1)))
        return total.reshape(tops, 2, 2, members * model_rows, ff_local)

    down_halves = halve(mm_tn(hidden_low, mixed_group).astype(bf16).reshape(tops, 1, 2, ff_rows, width))
    down_kept, gate_grad = together(down_halves[0], gate_grad)
    gate_halves = halve(column_blocks(mm_tn(normed_group, gate_grad)))
    gate_kept, down_got, up_grad = together(gate_halves[0], down_halves[1], up_grad)
    up_halves = halve(column_blocks(mm_tn(normed_group, up_grad)))
    down_halves, gate_halves = (down_kept, down_got), (gate_kept, gate_halves[1])

    grad_post_attention = jnp.sum(hidden_res_grad * attended * scale_two, axis=0)
    attended_grad = norm_back(attended, scale_two, post_attention * hidden_res_grad).astype(bf16)
    out_total = mm_tn(context_rows, attended_grad).astype(bf16)
    attended_grad, out_total, gate_kept, up_kept = lax.optimization_barrier(
        (attended_grad, out_total, gate_halves[0], up_halves[0])
    )
    gate_halves, up_halves = (gate_kept, gate_halves[1]), (up_kept, up_halves[1])
    down_parts = send_tops(by_top(*down_halves))
    grad_out = lax.psum_scatter(out_total, ALL, scatter_dimension=0, tiled=True)
    context_grad = mm_nt(attended_grad, out_weight).astype(bf16)
    query_grad, grad_query_gain, near_part, far_part = attend_back(
        meta, seq_ends, slots, query_heads, context_grad, lse, turned, query_raw, query_gain[None], cosine, sine, near_keys, far_keys
    )
    far_part, near_part, gate_halves, up_halves, down_parts = lax.optimization_barrier(
        (far_part, near_part, gate_halves, up_halves, down_parts)
    )
    gate_parts, up_parts = [send_tops(by_top(*half)) for half in (gate_halves, up_halves)]
    far_part = xor(far_part, "seq", 1)
    query_low, far_part = together(query_grad, far_part)
    near_part = add16(near_part, far_part).reshape(2, layers, count, 2 * HEAD)
    near_part = add16(near_part[0], xor(near_part[1], "seq", 2))
    grad_query = mm_tn(picked_one, query_low).astype(bf16).reshape(devices, block_rows, wide_q)
    grad_query, near_part, gate_parts = together(scatter_step(grad_query, *core_mask), near_part, gate_parts)
    grad_query = scatter_rest(grad_query)
    key_parts = [near_part[k] if k == 0 else xor(near_part[k], "dp", 2 * k) for k in range(layers)]
    key_parts, up_parts = together(key_parts, up_parts)
    key_grads = functools.reduce(jnp.add, [part.astype(f32) for part in key_parts])
    value_grad = key_grads[:, HEAD:].astype(bf16)
    key_turned = rotate(key_grads[:, :HEAD], cosine, -sine)
    key_scale = norm_scale(key_raw)
    grad_key_gain = jnp.sum(key_turned * key_raw * key_scale, axis=0)
    key_grad = norm_back(key_raw, key_scale, key_gain * key_turned).astype(bf16)
    kv_grad = jnp.concatenate([key_grad, value_grad], axis=1)
    normed_one_grad = mm_nt(query_grad, natural_weight[:, :wide_q]) + mm_nt(kv_grad, natural_weight[:, wide_q:])
    grad_pre_attention = jnp.sum(normed_one_grad * rows_in * scale_one, axis=0)
    rows_grad = hidden_res_grad + norm_back(rows_in, scale_one, pre_attention * normed_one_grad)
    rows_low, down_parts, gate_parts, up_parts = together(rows_grad.astype(bf16), down_parts, gate_parts, up_parts)
    grad_down = total_of(down_parts)[0]
    both_grads = split(total_of(gate_parts).astype(bf16), total_of(up_parts).astype(bf16), members)
    grad_gate, grad_up = unpack(swap_members(column_exchange(both_grads)), z_bit, tops, members, ff_rows)
    input_grad = ungroup(rows_low)
    grad_kv = mm_tn(picked_one, kv_grad).reshape(devices, block_rows, 2 * HEAD)
    gain_grads = [
        grad_pre_attention,
        grad_post_attention,
        grad_pre_feed,
        grad_post_feed,
        grad_query_gain,
        grad_key_gain,
    ]
    gain_grads = jnp.concatenate([g.reshape(devices, -1) for g in gain_grads], axis=1)
    gain_grads = mm_tn(device_pick, gain_grads.astype(bf16))
    gain_grads = jnp.pad(
        gain_grads[:, None, :], ((0, 0), (model_rows, block_rows - model_rows - 1), (0, 2 * HEAD - gain_total))
    )
    last = scatter_rest(scatter_step((grad_kv + gain_grads).astype(bf16), *core_mask))
    last, grad_out = together(last, grad_out)
    grad_out = grad_out.astype(f32)
    gain_out, at = [], 0
    for size in gain_sizes:
        gain_out.append(last[model_rows, at : at + size])
        at += size
    return (
        output,
        input_grad,
        grad_query[:model_rows],
        last[:model_rows, :HEAD],
        last[:model_rows, HEAD:],
        grad_out,
        grad_gate,
        grad_up,
        grad_down,
        *gain_out,
    )


def solution(mesh):
    split = P(None, ALL, None)
    weight, gain = P(ALL, None), P(ALL)
    return jax.shard_map(
        per_device,
        mesh=mesh,
        in_specs=(split, split, P(), P(), *[weight] * 7, *[gain] * 6),
        out_specs=(split, split, *[weight] * 7, *[gain] * 6),
        check_vma=False,
    )
```
